32 devices in a mesh: rep: 4 (over z), fsdp: 8 (over y, x, core).
Axes of the slice: x: 2, y: 2, z: 4, core: 2. Of those that a mesh axis runs over, the one named last changes fastest.
Arguments:
- byte_feats: bfloat16 [8, 4096, 768], P('rep', 'fsdp'), may hold values from -6 to 6
- latent_init: bfloat16 [256, 1280], P('fsdp'), may hold values from -6 to 6
- prefix: int32 [8], P('rep'), may hold values from 409 to 2048, as said below
- byte_gain: float32 [768], replicated, may hold values from 0.25 to 1.75
- query_gain: float32 [1280], replicated, may hold values from 0.25 to 1.75
- mixer_gain: float32 [1280], replicated, may hold values from 0.25 to 1.75
- query_weight: bfloat16 [1280, 256], P('fsdp'), may hold values from -0.25 to 0.25
- key_weight: bfloat16 [768, 256], P('fsdp'), may hold values from -0.3125 to 0.3125
- value_weight: bfloat16 [768, 1280], P('fsdp'), may hold values from -0.21875 to 0.21875
- out_weight: bfloat16 [1280, 1280], P('fsdp'), may hold values from -0.625 to 0.625
- up_weight: bfloat16 [1280, 1280], P('fsdp'), may hold values from -0.15625 to 0.15625
- down_weight: bfloat16 [1280, 1280], P('fsdp'), may hold values from -0.15625 to 0.15625
- cotangent: bfloat16 [8, 256, 1280], P('rep', 'fsdp'), may hold values from -6 to 6
Outputs:
- latents: bfloat16 [8, 256, 1280], P('rep', 'fsdp')
- byte_grads: float32 [8, 4096, 768], P('rep', 'fsdp')
- init_grads: float32 [256, 1280], P('fsdp')
- byte_norm: float32 [768], replicated
- query_norm: float32 [1280], replicated
- mixer_norm: float32 [1280], replicated
- query_grads: float32 [1280, 256], P('fsdp')
- key_grads: float32 [768, 256], P('fsdp')
- value_grads: float32 [768, 1280], P('fsdp')
- out_grads: float32 [1280, 1280], P('fsdp')
- up_grads: float32 [1280, 1280], P('fsdp')
- down_grads: float32 [1280, 1280], P('fsdp')
The draws below stay inside these ranges and needn't reach their ends.
Inputs may be any that keep to these rules, and one draw needn't show every extreme that they name: Bytes below a sequence's prefix length are seen by every latent; in every draw one sequence has the least prefix and another the most.
All inputs are finite; a program needn't handle non-finite values.
Results may differ from the reference program's by a relative error of at most 0.023.
Values may be sent and summed in bfloat16 or wider, within the bound.
No kernel may reach another device: no remote copies, remote signals or barrier semaphores. Data moves between devices by JAX's collectives and lax.ppermute only.
A program may use at most 128 MiB of HBM per device.

```python
import jax
import jax.numpy as jnp
from jax import lax

DB = 768
DL = 1280
NL = 256
H = 8
QK = 256
VD = 1280
FF = 1280
LEN = 4096
ALLSEQ = 8
STRIDE = 16


def draw_prefix(key, part):
    key_list = jax.random.split(key, 3)
    values = jax.random.randint(key_list[0], (ALLSEQ,), LEN // 10, LEN // 2 + 1)
    first_pick = jax.random.randint(key_list[1], (), 0, ALLSEQ)
    offset = jax.random.randint(key_list[2], (), 1, ALLSEQ)
    second = (first_pick + offset) % ALLSEQ
    positions = jnp.arange(ALLSEQ)
    values = jnp.where(positions == first_pick, LEN // 2, values)
    values = jnp.where(positions == second, LEN // 10, values)
    return values.astype(jnp.int32)


def level_of(key, shape, cuts, low, largest):
    level = 1.0
    for dim, shards_of in cuts:
        heights = jax.random.uniform(jax.random.fold_in(jax.random.fold_in(key, 6), dim), (shards_of,), jnp.float32, low / len(cuts), largest / len(cuts))
        level = level * jnp.repeat(jnp.exp(heights), shape[dim] // shards_of).reshape((-1,) + (1,) * (len(shape) - 1 - dim))
    return level


def normal_values(stream_key, dims, scale, most, shards=(), held_as=jnp.bfloat16):
    drawn = scale * jax.random.normal(stream_key, dims, jnp.float32)
    if shards:
        drawn = drawn * level_of(stream_key, dims, shards, -0.22, 0.18)
    return jnp.clip(drawn, -most, most).astype(held_as)


def setup_inputs(seed: int = 0) -> dict:
    arg_keys = jax.random.split(jax.random.key(seed), 14)
    return {
        "byte_feats": normal_values(arg_keys[0], (ALLSEQ, LEN, DB), 1.0, 6.0, ((0, 4), (1, 8))),
        "latent_init": normal_values(arg_keys[1], (NL, DL), 1.0, 6.0, ((0, 8),)),
        "prefix": draw_prefix(jax.random.fold_in(arg_keys[13], 71), 0),
        "byte_gain": jnp.clip(1.0 + 0.15 * jax.random.normal(arg_keys[3], (DB,), jnp.float32), 0.25, 1.75),
        "query_gain": jnp.clip(1.0 + 0.15 * jax.random.normal(arg_keys[4], (DL,), jnp.float32), 0.25, 1.75),
        "mixer_gain": jnp.clip(1.0 + 0.15 * jax.random.normal(arg_keys[5], (DL,), jnp.float32), 0.25, 1.75),
        "query_weight": normal_values(arg_keys[6], (DL, QK), (DL // 2) ** -0.5, 0.25, ((0, 8),)),
        "key_weight": normal_values(arg_keys[7], (DB, QK), (DB // 2) ** -0.5, 0.3125, ((0, 8),)),
        "value_weight": normal_values(arg_keys[8], (DB, VD), DB ** -0.5, 0.21875, ((0, 8),)),
        "out_weight": normal_values(arg_keys[9], (VD, DL), (VD // 16) ** -0.5, 0.625, ((0, 8),)),
        "up_weight": normal_values(arg_keys[10], (DL, FF), DL ** -0.5, 0.15625, ((0, 8),)),
        "down_weight": normal_values(arg_keys[11], (FF, DL), FF ** -0.5, 0.15625, ((0, 8),)),
        "cotangent": normal_values(arg_keys[12], (ALLSEQ, NL, DL), 1.0, 6.0, ((0, 4), (1, 8))),
    }


@jax.custom_vjp
def low(v):
    return lax.optimization_barrier(v.astype(jnp.bfloat16)).astype(jnp.float32)

@jax.custom_vjp
def low_back(v):
    return v

def low_keep(v):
    return (low(v), None)

def low_pass(kept, grad):
    return (grad,)

def back_keep(v):
    return (v, None)

def back_low(kept, grad):
    return (low(grad),)
low.defvjp(low_keep, low_pass)
low_back.defvjp(back_keep, back_low)
HIGHEST = lax.Precision.HIGHEST
EPSILON = 1e-05

def layer_norm(values, gain):
    centered = values - lax.optimization_barrier(jnp.mean(values, axis=-1, keepdims=True))
    variance = lax.optimization_barrier(jnp.mean(centered * centered, axis=-1, keepdims=True))
    return centered * lax.rsqrt(variance + EPSILON) * gain

def forward(byte_in, latent_in, byte_gain, query_gain, mixer_gain, query_weight, key_weight, value_weight, out_weight, up_weight, down_weight, prefix):
    head_qk = QK // H
    head_value = VD // H
    scale = head_qk ** (-0.5)
    latent_pos = jnp.arange(NL).astype(jnp.int32)[:, None]
    byte_pos = jnp.arange(LEN).astype(jnp.int32)[None, :]

    def one_sequence(pair):
        feats, limit = pair
        latent_normed = low(layer_norm(latent_in, query_gain))
        queries = low(low_back(jnp.dot(latent_normed, query_weight, precision=HIGHEST))).reshape(NL, H, head_qk)
        byte_normed = low(layer_norm(feats, byte_gain))
        keyed = low(low_back(jnp.dot(byte_normed, key_weight, precision=HIGHEST))).reshape(LEN, H, head_qk)
        valued = low(low_back(jnp.dot(byte_normed, value_weight, precision=HIGHEST))).reshape(LEN, H, head_value)
        scores = low_back(scale * jnp.einsum('jhd,ihd->hji', queries, keyed, precision=HIGHEST))
        visible = (byte_pos < limit) | (byte_pos < STRIDE * (latent_pos + 1))
        weights = jnp.where(visible[None], jnp.exp(scores), 0.0)
        totals = low_back(lax.optimization_barrier(jnp.sum(weights, axis=-1)))
        summed = low_back(jnp.einsum('hji,ihv->jhv', low(weights), valued, precision=HIGHEST))
        attended = summed / jnp.transpose(totals)[:, :, None]
        attn_out = low(low_back(attended)).reshape(NL, VD)
        hidden = latent_in + low_back(jnp.dot(attn_out, out_weight, precision=HIGHEST))
        normed = low(layer_norm(hidden, mixer_gain))
        pre_act = low_back(jnp.dot(normed, up_weight, precision=HIGHEST))
        activated = low(jax.nn.gelu(pre_act, approximate=False))
        return hidden + low_back(jnp.dot(activated, down_weight, precision=HIGHEST))
    return lax.map(jax.checkpoint(one_sequence), (byte_in, prefix))

def reference(byte_feats, latent_init, prefix, byte_gain, query_gain, mixer_gain, query_weight, key_weight, value_weight, out_weight, up_weight, down_weight, cotangent):
    floats = (byte_feats.astype(jnp.float32), latent_init.astype(jnp.float32), byte_gain.astype(jnp.float32), query_gain.astype(jnp.float32), mixer_gain.astype(jnp.float32), query_weight.astype(jnp.float32), key_weight.astype(jnp.float32), value_weight.astype(jnp.float32), out_weight.astype(jnp.float32), up_weight.astype(jnp.float32), down_weight.astype(jnp.float32))

    def run(byte_in, latent_in, gain_one, gain_two, gain_three, weight_one, weight_two, weight_three, weight_four, weight_five, weight_six):
        return forward(byte_in, latent_in, gain_one, gain_two, gain_three, weight_one, weight_two, weight_three, weight_four, weight_five, weight_six, prefix)
    outputs, pullback = jax.vjp(run, *floats)
    grads = pullback(cotangent.astype(jnp.float32))
    return (outputs.astype(jnp.bfloat16), grads[0], grads[1], grads[2], grads[3], grads[4], grads[5], grads[6], grads[7], grads[8], grads[9], grads[10])
```

```python
import jax
import jax.numpy as jnp
from jax import lax
from jax.experimental import pallas as pl
from jax.experimental.pallas import tpu as pltpu
from jax.sharding import PartitionSpec as P

DL = 1280
H = 8
QK = 256
VD = 1280
STRIDE = 16


EPSILON = 1e-05


def norm_parts(values, gain):
    centered = values - jnp.mean(values, axis=-1, keepdims=True)
    variance = jnp.mean(centered * centered, axis=-1, keepdims=True)
    inverse = lax.rsqrt(variance + EPSILON)
    normal = centered * inverse
    return (normal * gain, normal, inverse)


def norm_back(grad_out, normal, inverse, gain):
    scaled = grad_out * gain
    mean_one = jnp.mean(scaled, axis=-1, keepdims=True)
    mean_two = jnp.mean(scaled * normal, axis=-1, keepdims=True)
    return inverse * (scaled - mean_one - normal * mean_two)


def per_device_plain(
    byte_feats,
    latent_init,
    prefix,
    byte_gain,
    query_gain,
    mixer_gain,
    query_weight,
    key_weight,
    value_weight,
    out_weight,
    up_weight,
    down_weight,
    cotangent,
):
    shard_count = lax.axis_size("fsdp")
    shard_index = lax.axis_index("fsdp")
    seq_count, seq_rows, byte_width = byte_feats.shape
    own_latents = latent_init.shape[0]
    latent_count = own_latents * shard_count
    head_qk = QK // H
    head_value = VD // H
    scale = head_qk ** (-0.5)
    row_count = seq_count * own_latents
    latent_all, query_full, key_full, value_full = (
        lax.all_gather(latent_init, "fsdp", axis=0, tiled=True),
        lax.all_gather(query_weight, "fsdp", axis=0, tiled=True),
        lax.all_gather(key_weight, "fsdp", axis=0, tiled=True),
        lax.all_gather(value_weight, "fsdp", axis=0, tiled=True),
    )
    out_full, up_full, down_full = (
        lax.all_gather(out_weight, "fsdp", axis=0, tiled=True),
        lax.all_gather(up_weight, "fsdp", axis=0, tiled=True),
        lax.all_gather(down_weight, "fsdp", axis=0, tiled=True),
    )
    byte_flat = byte_feats.astype(jnp.float32).reshape(seq_count * seq_rows, byte_width)
    byte_normed, byte_hat, byte_inv = norm_parts(byte_flat, byte_gain)
    byte_low = byte_normed.astype(jnp.bfloat16)
    keys_low = (
        jnp.dot(byte_low, key_full, preferred_element_type=jnp.float32)
        .astype(jnp.bfloat16)
        .reshape(seq_count, seq_rows, H, head_qk)
    )
    values_low = (
        jnp.dot(byte_low, value_full, preferred_element_type=jnp.float32)
        .astype(jnp.bfloat16)
        .reshape(seq_count, seq_rows, H, head_value)
    )
    latent_normed, latent_hat, latent_inv = norm_parts(latent_all.astype(jnp.float32), query_gain)
    latent_low = latent_normed.astype(jnp.bfloat16)
    query_low = (
        jnp.dot(latent_low, query_full, preferred_element_type=jnp.float32)
        .astype(jnp.bfloat16)
        .reshape(latent_count, H, head_qk)
    )
    byte_pos = shard_index * seq_rows + jnp.arange(seq_rows, dtype=jnp.int32)
    latent_pos = jnp.arange(latent_count, dtype=jnp.int32)

    def exp_scores(keys_seq, limit):
        scores = scale * jnp.einsum(
            "jhd,ihd->hji", query_low, keys_seq, preferred_element_type=jnp.float32
        )
        visible = (byte_pos[None, :] < limit) | (
            byte_pos[None, :] < STRIDE * (latent_pos[:, None] + 1)
        )
        return jnp.where(visible[None], jnp.exp(scores), 0.0)

    def forward_step(carry, inputs):
        keys_seq, values_seq, limit = inputs
        weights = exp_scores(keys_seq, limit)
        totals = jnp.transpose(jnp.sum(weights, axis=-1))
        summed = jnp.einsum(
            "hji,ihv->jhv",
            weights.astype(jnp.bfloat16),
            values_seq,
            preferred_element_type=jnp.float32,
        ).reshape(latent_count, VD)
        own_sum, own_total = (
            lax.psum_scatter(summed, "fsdp", scatter_dimension=0, tiled=True),
            lax.psum_scatter(totals, "fsdp", scatter_dimension=0, tiled=True),
        )
        return (carry, (own_sum, own_total))

    _, (sums_own, totals_own) = lax.scan(
        forward_step, jnp.zeros((), jnp.float32), (keys_low, values_low, prefix)
    )
    attended = sums_own.reshape(seq_count, own_latents, H, head_value) / totals_own[..., None]
    attn_low = attended.reshape(row_count, VD).astype(jnp.bfloat16)
    mixed = jnp.dot(attn_low, out_full, preferred_element_type=jnp.float32).reshape(
        seq_count, own_latents, DL
    )
    hidden = (mixed + latent_init.astype(jnp.float32)[None]).reshape(row_count, DL)
    mixer_normed, mixer_hat, mixer_inv = norm_parts(hidden, mixer_gain)
    mixer_low = mixer_normed.astype(jnp.bfloat16)
    pre_act = jnp.dot(mixer_low, up_full, preferred_element_type=jnp.float32)
    activated, gelu_back = jax.vjp(lambda value: jax.nn.gelu(value, approximate=False), pre_act)
    act_low = activated.astype(jnp.bfloat16)
    output = hidden + jnp.dot(act_low, down_full, preferred_element_type=jnp.float32)
    latents = output.reshape(seq_count, own_latents, DL).astype(jnp.bfloat16)
    cot_low = cotangent.reshape(row_count, DL)
    down_local = jnp.einsum("rf,rd->fd", act_low, cot_low, preferred_element_type=jnp.float32)
    act_grad = jnp.einsum("rd,fd->rf", cot_low, down_full, preferred_element_type=jnp.float32)
    pre_grad = gelu_back(act_grad)[0].astype(jnp.bfloat16)
    up_local = jnp.einsum("rd,rf->df", mixer_low, pre_grad, preferred_element_type=jnp.float32)
    mixer_grad = jnp.einsum("rf,df->rd", pre_grad, up_full, preferred_element_type=jnp.float32)
    mixer_part = jnp.sum(mixer_grad * mixer_hat, axis=0)
    hidden_grad = cot_low.astype(jnp.float32) + norm_back(
        mixer_grad, mixer_hat, mixer_inv, mixer_gain
    )
    hidden_low = hidden_grad.astype(jnp.bfloat16)
    out_local = jnp.einsum("rv,rd->vd", attn_low, hidden_low, preferred_element_type=jnp.float32)
    attn_grad = jnp.einsum(
        "rd,vd->rv", hidden_low, out_full, preferred_element_type=jnp.float32
    ).astype(jnp.bfloat16)
    attn_heads = attn_grad.astype(jnp.float32).reshape(seq_count, own_latents, H, head_value)
    sum_grad = (
        (attn_heads / totals_own[..., None])
        .astype(jnp.bfloat16)
        .reshape(seq_count, own_latents, VD)
    )
    total_grad = (-jnp.sum(attn_heads * attended, axis=-1) / totals_own).astype(jnp.bfloat16)
    init_rows = jnp.sum(hidden_grad.reshape(seq_count, own_latents, DL), axis=0)

    def backward_step(carry, inputs):
        keys_seq, values_seq, limit, sum_own, total_own = inputs
        sum_all, total_all = (
            lax.all_gather(sum_own, "fsdp", axis=0, tiled=True),
            lax.all_gather(total_own, "fsdp", axis=0, tiled=True),
        )
        weights = exp_scores(keys_seq, limit)
        sum_heads = sum_all.reshape(latent_count, H, head_value)
        values_grad = jnp.einsum(
            "hji,jhv->ihv",
            weights.astype(jnp.bfloat16),
            sum_heads,
            preferred_element_type=jnp.float32,
        ).astype(jnp.bfloat16)
        weights_grad = (
            jnp.einsum("jhv,ihv->hji", sum_heads, values_seq, preferred_element_type=jnp.float32)
            + jnp.transpose(total_all.astype(jnp.float32))[:, :, None]
        )
        score_grad = (weights * weights_grad).astype(jnp.bfloat16)
        query_part = scale * jnp.einsum(
            "hji,ihd->jhd", score_grad, keys_seq, preferred_element_type=jnp.float32
        )
        keys_grad = (
            scale
            * jnp.einsum("hji,jhd->ihd", score_grad, query_low, preferred_element_type=jnp.float32)
        ).astype(jnp.bfloat16)
        query_own = lax.psum_scatter(
            query_part.reshape(latent_count, QK), "fsdp", scatter_dimension=0, tiled=True
        )
        return (carry, (keys_grad, values_grad, query_own))

    _, (keys_grad, values_grad, query_own) = lax.scan(
        backward_step,
        jnp.zeros((), jnp.float32),
        (keys_low, values_low, prefix, sum_grad, total_grad),
    )
    keys_flat = keys_grad.reshape(seq_count * seq_rows, QK)
    values_flat = values_grad.reshape(seq_count * seq_rows, VD)
    key_local = jnp.einsum("rb,rq->bq", byte_low, keys_flat, preferred_element_type=jnp.float32)
    value_local = jnp.einsum("rb,rv->bv", byte_low, values_flat, preferred_element_type=jnp.float32)
    normed_grad = jnp.einsum(
        "rq,bq->rb", keys_flat, key_full, preferred_element_type=jnp.float32
    ) + jnp.einsum("rv,bv->rb", values_flat, value_full, preferred_element_type=jnp.float32)
    byte_part = jnp.sum(normed_grad * byte_hat, axis=0)
    byte_grads = norm_back(normed_grad, byte_hat, byte_inv, byte_gain).reshape(
        seq_count, seq_rows, byte_width
    )
    query_grad_low = query_own.astype(jnp.bfloat16)
    own_low = lax.dynamic_slice_in_dim(latent_low, shard_index * own_latents, own_latents, 0)
    own_hat = lax.dynamic_slice_in_dim(latent_hat, shard_index * own_latents, own_latents, 0)
    own_inv = lax.dynamic_slice_in_dim(latent_inv, shard_index * own_latents, own_latents, 0)
    query_local = jnp.einsum(
        "ld,slq->dq", own_low, query_grad_low, preferred_element_type=jnp.float32
    )
    latent_grad = jnp.einsum(
        "slq,dq->ld", query_grad_low, query_full, preferred_element_type=jnp.float32
    )
    query_part_gain = jnp.sum(latent_grad * own_hat, axis=0)
    init_local = init_rows + norm_back(latent_grad, own_hat, own_inv, query_gain)
    byte_norm, query_norm, mixer_norm = lax.psum(
        (byte_part, query_part_gain, mixer_part), ("rep", "fsdp")
    )
    group_parts = (
        lax.psum_scatter(query_local, "fsdp", scatter_dimension=0, tiled=True),
        lax.psum_scatter(key_local, "fsdp", scatter_dimension=0, tiled=True),
        lax.psum_scatter(value_local, "fsdp", scatter_dimension=0, tiled=True),
        lax.psum_scatter(out_local, "fsdp", scatter_dimension=0, tiled=True),
        lax.psum_scatter(up_local, "fsdp", scatter_dimension=0, tiled=True),
        lax.psum_scatter(down_local, "fsdp", scatter_dimension=0, tiled=True),
    )
    query_grads, key_grads, value_grads, out_grads, up_grads, down_grads, init_grads = lax.psum(
        (
            group_parts[0],
            group_parts[1],
            group_parts[2],
            group_parts[3],
            group_parts[4],
            group_parts[5],
            init_local,
        ),
        "rep",
    )
    return (
        latents,
        byte_grads,
        init_grads,
        byte_norm,
        query_norm,
        mixer_norm,
        query_grads,
        key_grads,
        value_grads,
        out_grads,
        up_grads,
        down_grads,
    )


BF = jnp.bfloat16
F32 = jnp.float32
N = 8
NZ = 4
LOG2E = 1.4426950408889634
ANY = pl.BlockSpec(memory_space=pl.ANY)
VMEM = pl.BlockSpec(memory_space=pltpu.VMEM)
SMEM = pl.BlockSpec(memory_space=pltpu.SMEM)


def dot(a, b, ca, cb):
    return lax.dot_general(a, b, (((ca,), (cb,)), ((), ())), preferred_element_type=F32)


def send(x, k):
    return lax.ppermute(x, "fsdp", [(i, i ^ k) for i in range(N)])


def send_split(x, even, odd):
    return lax.ppermute(x, "fsdp", [(i, i ^ (odd if i & 1 else even)) for i in range(N)])


def send_z(x, k):
    return lax.ppermute(x, "rep", [(i, i ^ k) for i in range(NZ)])


def gather_wide(x):
    near = send(x, 1)
    ra = send_split(x, 2, 4)
    rb = send_split(x, 4, 2)
    rd = send_split(ra, 4, 2)
    na, nb, nd = send(ra, 1), send(rb, 1), send(rd, 1)
    return [x, near, ra, rb, rd, na, nb, nd], [
        (0, 0), (1, 1), (2, 4), (4, 2), (6, 6), (5, 3), (3, 5), (7, 7),
    ]


def gather_direct(x):
    r2, r4, r6 = send(x, 2), send(x, 4), send(x, 6)
    return [x, send(x, 1), r2, send(r2, 1), r4, send(r4, 1), r6, send(r6, 1)], [
        (k, k) for k in range(N)
    ]


def owner(meta, rel):
    me = meta[0]
    even, odd = rel
    if even == odd:
        return me ^ even
    return me ^ jnp.where((me & 1) == 0, even, odd)


def call(body, out, ins, specs, scratch=(), name=None, cost=None):
    return pl.pallas_call(
        body,
        out_shape=out,
        in_specs=specs,
        out_specs=jax.tree.map(lambda _: VMEM, out),
        scratch_shapes=list(scratch),
        name=name,
        cost_estimate=pl.CostEstimate(flops=cost[0], bytes_accessed=cost[1], transcendentals=0) if cost else None,
    )(*ins)


def sds(shape, dtype):
    return jax.ShapeDtypeStruct(shape, dtype)


def ln_parts(v):
    centered = v - jnp.mean(v, axis=-1, keepdims=True)
    inverse = lax.rsqrt(jnp.mean(centered * centered, axis=-1, keepdims=True) + EPSILON)
    return centered * inverse, inverse


def ln_back(grad, hat, inverse, gain):
    scaled = grad * gain
    return inverse * (
        scaled
        - jnp.mean(scaled, axis=-1, keepdims=True)
        - hat * jnp.mean(scaled * hat, axis=-1, keepdims=True)
    )


def pack_kernel(wk, wv, wq, lat, out):
    rows = wk.shape[0]
    out[0:rows, :] = wk[...]
    for c in range(5):
        out[rows * (c + 1) : rows * (c + 2), :] = wv[:, 256 * c : 256 * (c + 1)]
    at = rows * 6
    out[at : at + wq.shape[0], :] = wq[...]
    at += wq.shape[0]
    for c in range(5):
        out[at : at + lat.shape[0], :] = lat[:, 256 * c : 256 * (c + 1)]
        at += lat.shape[0]


def forward_kernel(rels, meta, x, bg, qg, *rest):
    pieces, rest = rest[:N], rest[N:]
    xn_o, k_o, vt_o, wkv_o, wq_o, q_o, zn_o, mine_o, theirs_o = rest[:9]
    lat, aat, lls, acc, sem = rest[9:]
    copies = []
    for piece, rel in zip(pieces, rels):
        j = owner(meta, rel)
        r96 = pl.ds(pl.multiple_of(j * 96, 32), 96)
        r160 = pl.ds(pl.multiple_of(j * 160, 32), 160)
        r32 = pl.ds(pl.multiple_of(j * 32, 32), 32)
        for c in range(6):
            copies.append((piece.at[pl.ds(96 * c, 96), :], wkv_o.at[r96, pl.ds(256 * c, 256)]))
        copies.append((piece.at[pl.ds(576, 160), :], wq_o.at[r160, :]))
        for c in range(5):
            copies.append((piece.at[pl.ds(736 + 32 * c, 32), :], lat.at[r32, pl.ds(256 * c, 256)]))
    handles = [pltpu.make_async_copy(a, b, sem.at[n]) for n, (a, b) in enumerate(copies)]
    for h in handles:
        h.start()
    hat, _ = ln_parts(x[...].astype(F32))
    xn_o[...] = (hat * bg[...]).astype(BF)
    for h in handles:
        h.wait()
    zhat, _ = ln_parts(lat[...].astype(F32))
    zn_o[...] = (zhat * qg[...]).astype(BF)
    q_o[...] = dot(zn_o[...], wq_o[...], 1, 0).astype(BF)
    k_o[...] = dot(xn_o[...], wkv_o[:, 0:256], 1, 0).astype(BF)
    for c in range(5):
        vt_o[256 * c : 256 * (c + 1), :] = dot(
            wkv_o[:, 256 * (c + 1) : 256 * (c + 2)], xn_o[...], 0, 1
        ).astype(BF)
    lanes = lax.broadcasted_iota(jnp.int32, (256, 256), 1) // 32
    pos = lax.broadcasted_iota(jnp.int32, (256, 512), 1) + meta[0] * 512
    own = STRIDE * (lax.broadcasted_iota(jnp.int32, (256, 1), 0) + 1)
    lls[...] = jnp.zeros_like(lls)
    lane = lax.broadcasted_iota(jnp.int32, (256, 128), 1)
    for s in range(2):
        seen = jnp.maximum(own, meta[2 + s])

        def head(h, carry, s=s, seen=seen):
            qh = jnp.where(lanes == h, q_o[...], jnp.zeros((), BF))
            scores = dot(qh, k_o[512 * s : 512 * (s + 1), :], 1, 1)
            e = jnp.where(pos < seen, jnp.exp2(scores * (LOG2E * 32 ** (-0.5))), 0.0)
            lls[s] = lls[s] + jnp.where(lane == h, jnp.sum(e, axis=-1, keepdims=True), 0.0)
            rows = pl.ds(pl.multiple_of(h * 160, 32), 160)
            aat[s, rows, :] = dot(vt_o[rows, 512 * s : 512 * (s + 1)], e.astype(BF), 1, 1).astype(BF)
            return carry

        lax.fori_loop(0, H, head, 0, unroll=2)
        acc[:, 0:1280] = aat[s].T
        acc[:, 1280:1408] = lls[s].astype(BF)
        for kk in range(4):
            for odd, ref in ((0, mine_o), (1, theirs_o)):
                j = meta[0] ^ (2 * kk + odd)
                ref[kk, 32 * s : 32 * (s + 1), :] = acc[pl.ds(pl.multiple_of(j * 32, 32), 32), :]


def add4_kernel(a, b, *outs):
    for kk in range(4):
        outs[kk][...] = (a[kk].astype(F32) + b[kk].astype(F32)).astype(BF)


def latent_kernel(rels, meta, m0, r1, r2, r3, lat, mg, cot, *rest):
    wout_p, wup_p, wdown_p, rest = rest[:N], rest[N : 2 * N], rest[2 * N : 3 * N], rest[3 * N :]
    latents_o, agb_o, mine_o, theirs_o, dab_o, init_o = rest[:6]
    wout, wup, wdown, sem = rest[6:]
    groups = []
    for g, (ps, w) in enumerate(((wout_p, wout), (wup_p, wup), (wdown_p, wdown))):
        hs = []
        for n, (p, rel) in enumerate(zip(ps, rels)):
            rows = pl.ds(pl.multiple_of(owner(meta, rel) * 160, 32), 160)
            hs.append(pltpu.make_async_copy(p, w.at[rows, :], sem.at[g, n]))
        for h in hs:
            h.start()
        groups.append(hs)
    total = (m0[...].astype(F32) + r1[...].astype(F32)) + (r2[...].astype(F32) + r3[...].astype(F32))
    aa = total[:, 0:1280]
    ll = total[:, 1280:1408]
    head = lax.broadcasted_iota(jnp.int32, (64, 1280), 1) // 160
    inv = jnp.zeros((64, 1280), F32)
    for h in range(H):
        inv = jnp.where(head == h, 1.0 / ll[:, h : h + 1], inv)
    oo = aa * inv
    ob = oo.astype(BF)
    for h in groups[0]:
        h.wait()
    start = lat[...].astype(F32)
    hh = jnp.concatenate([start, start], axis=0) + dot(ob, wout[...], 1, 0)
    hat, inverse = ln_parts(hh)
    hn = (hat * mg[...]).astype(BF)
    for h in groups[1]:
        h.wait()
    uu = dot(hn, wup[...], 1, 0)
    cdf = 0.5 * (1.0 + lax.erf(uu * (0.5**0.5)))
    gg = (uu * cdf).astype(BF)
    slope = cdf + uu * (jnp.exp(-0.5 * uu * uu) * 0.3989422804014327)
    for h in groups[2]:
        h.wait()
    latents_o[...] = (hh + dot(gg, wdown[...], 1, 0)).astype(BF)
    du = (dot(cot[...], wdown[...], 1, 1) * slope).astype(BF)
    dhn = dot(du, wup[...], 1, 1)
    dhh = cot[...].astype(F32) + ln_back(dhn, hat, inverse, mg[...])
    init_o[...] = dhh[0:32] + dhh[32:64]
    dhb = dhh.astype(BF)
    dob = dot(dhb, wout[...], 1, 1).astype(BF).astype(F32)
    dab_o[:, 0:1280] = (dob * inv).astype(BF)
    prod = dob * oo
    lane = lax.broadcasted_iota(jnp.int32, (64, 128), 1)
    dlb = jnp.zeros((64, 128), F32)
    for h in range(H):
        part = jnp.sum(jnp.where(head == h, prod, 0.0), axis=-1, keepdims=True)
        dlb = jnp.where(lane == h, -part / ll[:, h : h + 1], dlb)
    dab_o[:, 1280:1408] = dlb.astype(BF)
    agb_o[0] = dhb
    agb_o[1] = du
    agb_o[2] = cot[...]
    me = meta[0]
    for j in range(N):
        kk = (me >> 1) ^ (j >> 1)
        cols = slice(160 * j, 160 * (j + 1))

        @pl.when((me & 1) == (j & 1))
        def _():
            for n, v in enumerate((ob, hn, gg)):
                mine_o[kk, n] = v[:, cols]

        @pl.when((me & 1) != (j & 1))
        def _():
            for n, v in enumerate((ob, hn, gg)):
                theirs_o[kk, n] = v[:, cols]


def backward_kernel(rels, meta, k, vt, xn, q, zn, *rest):
    pieces, rest = rest[:N], rest[N:]
    dkvt_o, mine_o, theirs_o = rest[:3]
    dabx, dabt, qt, xnt, dqs, dw, dqg, sem = rest[3:]
    handles = []
    for n, (p, rel) in enumerate(zip(pieces, rels)):
        rows = pl.ds(pl.multiple_of(owner(meta, rel) * 32, 32), 32)
        for s in range(2):
            handles.append(
                pltpu.make_async_copy(p.at[pl.ds(32 * s, 32), :], dabx.at[s, rows, :], sem.at[2 * n + s])
            )
    for h in handles:
        h.start()
    qt[...] = q[...].T
    xnt[...] = xn[...].T
    dqs[...] = jnp.zeros_like(dqs)
    for h in handles:
        h.wait()
    lanes = lax.broadcasted_iota(jnp.int32, (256, 256), 1) // 32
    pos = lax.broadcasted_iota(jnp.int32, (256, 512), 1) + meta[0] * 512
    own = STRIDE * (lax.broadcasted_iota(jnp.int32, (256, 1), 0) + 1)
    lane = lax.broadcasted_iota(jnp.int32, (256, 128), 1)
    scale = 32 ** (-0.5)
    for s in range(2):
        seen = jnp.maximum(own, meta[2 + s])
        dabt[...] = dabx[s, :, 0:1280].T
        cols = slice(512 * s, 512 * (s + 1))

        def head(h, carry, s=s, seen=seen, cols=cols):
            qh = jnp.where(lanes == h, q[...], jnp.zeros((), BF))
            scores = dot(qh, k[cols, :], 1, 1)
            e = jnp.where(pos < seen, jnp.exp2(scores * (LOG2E * scale)), 0.0)
            rows = pl.ds(pl.multiple_of(h * 160, 32), 160)
            dkvt_o[pl.ds(pl.multiple_of(256 + h * 160, 32), 160), cols] = dot(
                dabt[rows, :], e.astype(BF), 1, 0
            ).astype(BF)
            dlb = jnp.sum(
                jnp.where(lane == h, dabx[s, :, 1280:1408].astype(F32), 0.0), axis=-1, keepdims=True
            )
            dee = dot(dabt[rows, :], vt[rows, cols], 0, 0) + dlb
            dss = (e * dee).astype(BF)
            krows = pl.ds(pl.multiple_of(h * 32, 32), 32)
            dkvt_o[krows, cols] = (dot(qt[krows, :], dss, 1, 0) * scale).astype(BF)
            dqs[...] += jnp.where(lanes == h, dot(dss, k[cols, :], 1, 0), 0.0)
            return carry

        lax.fori_loop(0, H, head, 0, unroll=2)
    dq = (dqs[...] * scale).astype(BF)
    for c in range(6):
        dw[:, 256 * c : 256 * (c + 1)] = dot(
            xnt[...], dkvt_o[256 * c : 256 * (c + 1), :], 1, 1
        ).astype(BF)
    dqg[...] = dot(zn[...], dq, 0, 0).astype(BF)
    dqs[...] = dqs[...] * scale
    for kk in range(4):
        for odd, ref in ((0, mine_o), (1, theirs_o)):
            j = meta[0] ^ (2 * kk + odd)
            r96 = pl.ds(pl.multiple_of(j * 96, 32), 96)
            for c in range(6):
                ref[kk, 96 * c : 96 * (c + 1), :] = dw[r96, 256 * c : 256 * (c + 1)]
            ref[kk, 576:736, :] = dqg[pl.ds(pl.multiple_of(j * 160, 32), 160), :]
            ref[kk, 736:768, :] = dqs[pl.ds(pl.multiple_of(j * 32, 32), 32), :].astype(BF)


def bytes_kernel(x, bg, wkv, dkvt, out):
    hat, inverse = ln_parts(x[...].astype(F32))
    dxn = dot(dkvt[...], wkv[...], 0, 1)
    out[...] = ln_back(dxn, hat, inverse, bg[...])


def latent_grads_kernel(meta, init, *rest):
    rows, cols, outs, (xs, ys, acc) = rest[:N], rest[N : 2 * N], rest[2 * N : 2 * N + 4], rest[2 * N + 4 :]
    for k in range(N):
        for n in range(3):
            ys[n, 64 * k : 64 * (k + 1), :] = rows[k][n]
            xs[n, 64 * k : 64 * (k + 1), :] = cols[k][n]
    for n in range(3):
        acc[160 * n : 160 * (n + 1), :] = dot(xs[n], ys[n], 0, 0).astype(BF)
    acc[480:512, :] = init[...].astype(BF)
    for r in range(NZ):
        z = meta[1] ^ r
        outs[r][...] = acc[pl.ds(pl.multiple_of(z * 128, 128), 128), :]


def row_sums(a, b):
    ones = jnp.ones((8, a.shape[1]), F32)
    return lax.dot_general(
        ones, a * b, (((1,), (1,)), ((), ())), precision=lax.Precision.HIGHEST, preferred_element_type=F32
    )


def finish_latent_kernel(meta, wup, mgs, *rest):
    pieces, (out_o, up_o, down_o, init_o, norm_o, acc) = rest[:NZ], rest[NZ:]
    for r in range(NZ):
        z = meta[1] ^ r
        acc[pl.ds(pl.multiple_of(z * 128, 128), 128), :] = pieces[r][...]
    out_o[...] = acc[0:160, :].astype(F32)
    up_o[...] = acc[160:320, :].astype(F32)
    down_o[...] = acc[320:480, :].astype(F32)
    init_o[...] = acc[480:512, :].astype(F32)
    norm_o[...] = row_sums(up_o[...], wup[...].astype(F32)) / mgs[...]


def finish_kernel(meta, wk, wv, wq, wq_full, lat, qg, bgs, qgs, init, mix, *rest):
    pieces, (key_o, value_o, query_o, init_o, norm_o, acc) = rest[:NZ], rest[NZ:]
    for r in range(NZ):
        z = meta[1] ^ r
        acc[pl.ds(pl.multiple_of(z * 192, 64), 192), :] = pieces[r][...]
    key_o[...] = acc[0:96, :].astype(F32)
    sums = row_sums(key_o[...], wk[...].astype(F32))
    for c in range(5):
        cols = slice(256 * c, 256 * (c + 1))
        part = acc[96 * (c + 1) : 96 * (c + 2), :].astype(F32)
        value_o[:, cols] = part
        sums = sums + row_sums(part, wv[:, cols].astype(F32))
    query_o[...] = acc[576:736, :].astype(F32)
    dzn = dot(acc[736:768, :], wq_full[...], 1, 1)
    hat, inverse = ln_parts(lat[...].astype(F32))
    init_o[...] = init[...] + ln_back(dzn, hat, inverse, qg[...])
    norm_o[...] = jnp.zeros_like(norm_o)
    norm_o[0:8, 0:96] = sums / bgs[...]
    norm_o[8:16, 0:160] = mix[...]
    norm_o[16:24, 0:160] = row_sums(query_o[...], wq[...].astype(F32)) / qgs[...]


def norms_kernel(meta, *rest):
    pieces, (byte_o, mixer_o, query_o) = rest[:N], rest[N:]
    for k in range(N):
        j = meta[0] ^ k
        byte_o[pl.ds(j, 1), :] = pieces[k][0:1, 0:96]
        mixer_o[pl.ds(j, 1), :] = pieces[k][8:9, 0:160]
        query_o[pl.ds(j, 1), :] = pieces[k][16:17, 0:160]


def part(f, *args):
    def body(*refs):
        return f(*args, *refs)

    return body


def per_device_fast(
    byte_feats,
    latent_init,
    prefix,
    byte_gain,
    query_gain,
    mixer_gain,
    query_weight,
    key_weight,
    value_weight,
    out_weight,
    up_weight,
    down_weight,
    cotangent,
):
    me = lax.axis_index("fsdp")
    zi = lax.axis_index("rep")
    meta = jnp.concatenate([jnp.stack([me, zi]).astype(jnp.int32), prefix])
    seqs, rows, width = byte_feats.shape
    own = latent_init.shape[0]
    x = byte_feats.reshape(seqs * rows, width)
    cot = cotangent.reshape(seqs * own, DL)
    bg = byte_gain.reshape(1, -1)
    qg = query_gain.reshape(1, -1)
    mg = mixer_gain.reshape(1, -1)
    packed = call(pack_kernel, sds((896, 256), BF), (key_weight, value_weight, query_weight, latent_init), [VMEM] * 4, name="pack")
    pieces, rels = gather_wide(packed)
    wout_p, _ = gather_wide(out_weight)
    wup_p, _ = gather_wide(up_weight)
    wdown_p, _ = gather_wide(down_weight)
    xn, k, vt, wkv, wq_full, q, zn, mine, theirs = call(
        part(forward_kernel, rels),
        (
            sds((1024, 768), BF), sds((1024, 256), BF), sds((1280, 1024), BF), sds((768, 1536), BF),
            sds((1280, 256), BF), sds((256, 256), BF), sds((256, 1280), BF),
            sds((4, 64, 1408), BF), sds((4, 64, 1408), BF),
        ),
        (meta, x, bg, qg, *pieces),
        [SMEM, VMEM, VMEM, VMEM] + [ANY] * N,
        [
            pltpu.VMEM((256, 1280), BF), pltpu.VMEM((2, 1280, 256), BF), pltpu.VMEM((2, 256, 128), F32),
            pltpu.VMEM((256, 1408), BF), pltpu.SemaphoreType.DMA((12 * N,)),
        ],
        name="forward",
        cost=(8_000_000_000, 12_000_000),
    )
    got = send(theirs, 1)
    m = call(add4_kernel, (sds((64, 1408), BF),) * 4, (mine, got), [VMEM] * 2, name="add4")
    r1, r2, r3 = send(m[1], 2), send(m[2], 4), send(m[3], 6)
    latents, agb, amine, atheirs, dabx, init = call(
        part(latent_kernel, rels),
        (
            sds((64, 1280), BF), sds((3, 64, 1280), BF), sds((4, 3, 64, 160), BF), sds((4, 3, 64, 160), BF),
            sds((64, 1408), BF), sds((32, 1280), F32),
        ),
        (meta, m[0], r1, r2, r3, latent_init, mg, cot, *wout_p, *wup_p, *wdown_p),
        [SMEM] + [VMEM] * 7 + [ANY] * (3 * N),
        [pltpu.VMEM((1280, 1280), BF)] * 3 + [pltpu.SemaphoreType.DMA((3, N))],
        name="latent",
        cost=(5_000_000_000, 12_000_000),
    )
    dab_p, drels = gather_direct(dabx)
    dkvt, gmine, gtheirs = call(
        part(backward_kernel, drels),
        (sds((1536, 1024), BF), sds((4, 768, 256), BF), sds((4, 768, 256), BF)),
        (meta, k, vt, xn, q, zn, *dab_p),
        [SMEM] + [VMEM] * 5 + [ANY] * N,
        [
            pltpu.VMEM((2, 256, 1408), BF), pltpu.VMEM((1280, 256), BF), pltpu.VMEM((256, 256), BF),
            pltpu.VMEM((768, 1024), BF), pltpu.VMEM((256, 256), F32), pltpu.VMEM((768, 1536), BF),
            pltpu.VMEM((1280, 256), BF), pltpu.SemaphoreType.DMA((2 * N,)),
        ],
        name="backward",
        cost=(10_000_000_000, 12_000_000),
    )
    rows_p, _ = gather_wide(agb)
    at = send(atheirs, 1)
    cols_p = [amine[0], at[0]]
    for kk in range(1, 4):
        both = send(jnp.stack([amine[kk], at[kk]]), 2 * kk)
        cols_p += [both[0], both[1]]
    even = [0, 1, 2, 6, 3, 5, 4, 7]
    odd = [0, 1, 3, 5, 2, 6, 4, 7]
    is_odd = (me & 1) == 1
    rows_r = [
        rows_p[a] if a == b else jnp.where(is_odd, rows_p[b], rows_p[a]) for a, b in zip(even, odd)
    ]
    oud = call(
        latent_grads_kernel,
        (sds((128, 1280), BF),) * NZ,
        (meta, init, *rows_r, *cols_p),
        [SMEM] + [VMEM] * (1 + 2 * N),
        [pltpu.VMEM((3, 512, 160), BF), pltpu.VMEM((3, 512, 1280), BF), pltpu.VMEM((512, 1280), BF)],
        name="latent_grads",
        cost=(1_000_000_000, 6_000_000),
    )
    zsum = (
        oud[0].astype(F32) + send_z(oud[1], 1).astype(F32) + send_z(oud[2], 2).astype(F32) + send_z(oud[3], 3).astype(F32)
    ).astype(BF)
    zall = [zsum, send_z(zsum, 1), send_z(zsum, 2), send_z(zsum, 3)]
    mgs = lax.dynamic_slice_in_dim(mixer_gain, me * 160, 160, 0).reshape(1, 160)
    qgs = lax.dynamic_slice_in_dim(query_gain, me * 160, 160, 0).reshape(1, 160)
    bgs = lax.dynamic_slice_in_dim(byte_gain, me * 96, 96, 0).reshape(1, 96)
    out_g, up_g, down_g, init_sum, mix = call(
        finish_latent_kernel,
        (sds((160, 1280), F32),) * 3 + (sds((32, 1280), F32), sds((8, 160), F32)),
        (meta, up_weight, mgs, *zall),
        [SMEM] + [VMEM] * (2 + NZ),
        [pltpu.VMEM((512, 1280), BF)],
        name="finish_latent",
    )
    gg = send(gtheirs, 1)
    gm = call(add4_kernel, (sds((768, 256), BF),) * 4, (gmine, gg), [VMEM] * 2, name="add4g")
    g1, g2, g3 = send(gm[1], 2), send(gm[2], 4), send(gm[3], 6)
    gsum = (gm[0].astype(F32) + g1.astype(F32) + g2.astype(F32) + g3.astype(F32)).astype(BF)
    byte_grads = pl.pallas_call(
        bytes_kernel,
        grid=(4,),
        out_shape=sds((1024, 768), F32),
        in_specs=[
            pl.BlockSpec((256, 768), lambda b: (b, 0)),
            pl.BlockSpec((1, 768), lambda b: (0, 0)),
            pl.BlockSpec((768, 1536), lambda b: (0, 0)),
            pl.BlockSpec((1536, 256), lambda b: (0, b)),
        ],
        out_specs=pl.BlockSpec((256, 768), lambda b: (b, 0)),
        name="bytes",
        cost_estimate=pl.CostEstimate(flops=2_400_000_000, bytes_accessed=10_000_000, transcendentals=0),
    )(x, bg, wkv, dkvt)
    zrel = (jnp.arange(NZ) ^ zi).astype(jnp.int32)
    gquart = [lax.dynamic_slice_in_dim(gsum, zrel[r] * 192, 192, 0) for r in range(NZ)]
    gz = (
        gquart[0].astype(F32) + send_z(gquart[1], 1).astype(F32) + send_z(gquart[2], 2).astype(F32) + send_z(gquart[3], 3).astype(F32)
    ).astype(BF)
    gall = [gz, send_z(gz, 1), send_z(gz, 2), send_z(gz, 3)]
    key_g, value_g, query_g, init_g, norm = call(
        finish_kernel,
        (sds((96, 256), F32), sds((96, 1280), F32), sds((160, 256), F32), sds((32, 1280), F32), sds((24, 256), F32)),
        (meta, key_weight, value_weight, query_weight, wq_full, latent_init, qg, bgs, qgs, init_sum, mix, *gall),
        [SMEM] + [VMEM] * (10 + NZ),
        [pltpu.VMEM((768, 256), BF)],
        name="finish",
    )
    norm_p, _ = gather_direct(norm)
    byte_n, mixer_n, query_n = call(
        norms_kernel,
        (sds((8, 96), F32), sds((8, 160), F32), sds((8, 160), F32)),
        (meta, *norm_p),
        [SMEM] + [VMEM] * N,
        name="norms",
    )
    return (
        latents.reshape(seqs, own, DL),
        byte_grads.reshape(seqs, rows, width),
        init_g,
        byte_n.reshape(-1),
        query_n.reshape(-1),
        mixer_n.reshape(-1),
        query_g,
        key_g,
        value_g,
        out_g,
        up_g,
        down_g,
    )


def solution(mesh):
    fast = mesh.shape["fsdp"] == 8 and mesh.shape["rep"] == 4
    device_fn = per_device_fast if fast else per_device_plain
    placed = (
        P("rep", "fsdp", None),
        P("fsdp", None),
        P("rep"),
        P(),
        P(),
        P(),
        P("fsdp", None),
        P("fsdp", None),
        P("fsdp", None),
        P("fsdp", None),
        P("fsdp", None),
        P("fsdp", None),
        P("rep", "fsdp", None),
    )
    return jax.shard_map(
        device_fn,
        mesh=mesh,
        in_specs=placed,
        out_specs=(
            P("rep", "fsdp", None),
            P("rep", "fsdp", None),
            P("fsdp", None),
            P(),
            P(),
            P(),
            P("fsdp", None),
            P("fsdp", None),
            P("fsdp", None),
            P("fsdp", None),
            P("fsdp", None),
            P("fsdp", None),
        ),
        check_vma=False,
    )
```

```python
import jax
import jax.numpy as jnp
from jax import lax
from jax.experimental import pallas as pl
from jax.experimental.pallas import tpu as pltpu
from jax.sharding import PartitionSpec as P

DL = 1280
H = 8
QK = 256
VD = 1280
STRIDE = 16


EPSILON = 1e-05


def norm_parts(values, gain):
    centered = values - jnp.mean(values, axis=-1, keepdims=True)
    variance = jnp.mean(centered * centered, axis=-1, keepdims=True)
    inverse = lax.rsqrt(variance + EPSILON)
    normal = centered * inverse
    return (normal * gain, normal, inverse)


def norm_back(grad_out, normal, inverse, gain):
    scaled = grad_out * gain
    mean_one = jnp.mean(scaled, axis=-1, keepdims=True)
    mean_two = jnp.mean(scaled * normal, axis=-1, keepdims=True)
    return inverse * (scaled - mean_one - normal * mean_two)


def per_device_plain(
    byte_feats,
    latent_init,
    prefix,
    byte_gain,
    query_gain,
    mixer_gain,
    query_weight,
    key_weight,
    value_weight,
    out_weight,
    up_weight,
    down_weight,
    cotangent,
):
    shard_count = lax.axis_size("fsdp")
    shard_index = lax.axis_index("fsdp")
    seq_count, seq_rows, byte_width = byte_feats.shape
    own_latents = latent_init.shape[0]
    latent_count = own_latents * shard_count
    head_qk = QK // H
    head_value = VD // H
    scale = head_qk ** (-0.5)
    row_count = seq_count * own_latents
    latent_all, query_full, key_full, value_full = (
        lax.all_gather(latent_init, "fsdp", axis=0, tiled=True),
        lax.all_gather(query_weight, "fsdp", axis=0, tiled=True),
        lax.all_gather(key_weight, "fsdp", axis=0, tiled=True),
        lax.all_gather(value_weight, "fsdp", axis=0, tiled=True),
    )
    out_full, up_full, down_full = (
        lax.all_gather(out_weight, "fsdp", axis=0, tiled=True),
        lax.all_gather(up_weight, "fsdp", axis=0, tiled=True),
        lax.all_gather(down_weight, "fsdp", axis=0, tiled=True),
    )
    byte_flat = byte_feats.astype(jnp.float32).reshape(seq_count * seq_rows, byte_width)
    byte_normed, byte_hat, byte_inv = norm_parts(byte_flat, byte_gain)
    byte_low = byte_normed.astype(jnp.bfloat16)
    keys_low = (
        jnp.dot(byte_low, key_full, preferred_element_type=jnp.float32)
        .astype(jnp.bfloat16)
        .reshape(seq_count, seq_rows, H, head_qk)
    )
    values_low = (
        jnp.dot(byte_low, value_full, preferred_element_type=jnp.float32)
        .astype(jnp.bfloat16)
        .reshape(seq_count, seq_rows, H, head_value)
    )
    latent_normed, latent_hat, latent_inv = norm_parts(latent_all.astype(jnp.float32), query_gain)
    latent_low = latent_normed.astype(jnp.bfloat16)
    query_low = (
        jnp.dot(latent_low, query_full, preferred_element_type=jnp.float32)
        .astype(jnp.bfloat16)
        .reshape(latent_count, H, head_qk)
    )
    byte_pos = shard_index * seq_rows + jnp.arange(seq_rows, dtype=jnp.int32)
    latent_pos = jnp.arange(latent_count, dtype=jnp.int32)

    def exp_scores(keys_seq, limit):
        scores = scale * jnp.einsum(
            "jhd,ihd->hji", query_low, keys_seq, preferred_element_type=jnp.float32
        )
        visible = (byte_pos[None, :] < limit) | (
            byte_pos[None, :] < STRIDE * (latent_pos[:, None] + 1)
        )
        return jnp.where(visible[None], jnp.exp(scores), 0.0)

    def forward_step(carry, inputs):
        keys_seq, values_seq, limit = inputs
        weights = exp_scores(keys_seq, limit)
        totals = jnp.transpose(jnp.sum(weights, axis=-1))
        summed = jnp.einsum(
            "hji,ihv->jhv",
            weights.astype(jnp.bfloat16),
            values_seq,
            preferred_element_type=jnp.float32,
        ).reshape(latent_count, VD)
        own_sum, own_total = (
            lax.psum_scatter(summed, "fsdp", scatter_dimension=0, tiled=True),
            lax.psum_scatter(totals, "fsdp", scatter_dimension=0, tiled=True),
        )
        return (carry, (own_sum, own_total))

    _, (sums_own, totals_own) = lax.scan(
        forward_step, jnp.zeros((), jnp.float32), (keys_low, values_low, prefix)
    )
    attended = sums_own.reshape(seq_count, own_latents, H, head_value) / totals_own[..., None]
    attn_low = attended.reshape(row_count, VD).astype(jnp.bfloat16)
    mixed = jnp.dot(attn_low, out_full, preferred_element_type=jnp.float32).reshape(
        seq_count, own_latents, DL
    )
    hidden = (mixed + latent_init.astype(jnp.float32)[None]).reshape(row_count, DL)
    mixer_normed, mixer_hat, mixer_inv = norm_parts(hidden, mixer_gain)
    mixer_low = mixer_normed.astype(jnp.bfloat16)
    pre_act = jnp.dot(mixer_low, up_full, preferred_element_type=jnp.float32)
    activated, gelu_back = jax.vjp(lambda value: jax.nn.gelu(value, approximate=False), pre_act)
    act_low = activated.astype(jnp.bfloat16)
    output = hidden + jnp.dot(act_low, down_full, preferred_element_type=jnp.float32)
    latents = output.reshape(seq_count, own_latents, DL).astype(jnp.bfloat16)
    cot_low = cotangent.reshape(row_count, DL)
    down_local = jnp.einsum("rf,rd->fd", act_low, cot_low, preferred_element_type=jnp.float32)
    act_grad = jnp.einsum("rd,fd->rf", cot_low, down_full, preferred_element_type=jnp.float32)
    pre_grad = gelu_back(act_grad)[0].astype(jnp.bfloat16)
    up_local = jnp.einsum("rd,rf->df", mixer_low, pre_grad, preferred_element_type=jnp.float32)
    mixer_grad = jnp.einsum("rf,df->rd", pre_grad, up_full, preferred_element_type=jnp.float32)
    mixer_part = jnp.sum(mixer_grad * mixer_hat, axis=0)
    hidden_grad = cot_low.astype(jnp.float32) + norm_back(
        mixer_grad, mixer_hat, mixer_inv, mixer_gain
    )
    hidden_low = hidden_grad.astype(jnp.bfloat16)
    out_local = jnp.einsum("rv,rd->vd", attn_low, hidden_low, preferred_element_type=jnp.float32)
    attn_grad = jnp.einsum(
        "rd,vd->rv", hidden_low, out_full, preferred_element_type=jnp.float32
    ).astype(jnp.bfloat16)
    attn_heads = attn_grad.astype(jnp.float32).reshape(seq_count, own_latents, H, head_value)
    sum_grad = (
        (attn_heads / totals_own[..., None])
        .astype(jnp.bfloat16)
        .reshape(seq_count, own_latents, VD)
    )
    total_grad = (-jnp.sum(attn_heads * attended, axis=-1) / totals_own).astype(jnp.bfloat16)
    init_rows = jnp.sum(hidden_grad.reshape(seq_count, own_latents, DL), axis=0)

    def backward_step(carry, inputs):
        keys_seq, values_seq, limit, sum_own, total_own = inputs
        sum_all, total_all = (
            lax.all_gather(sum_own, "fsdp", axis=0, tiled=True),
            lax.all_gather(total_own, "fsdp", axis=0, tiled=True),
        )
        weights = exp_scores(keys_seq, limit)
        sum_heads = sum_all.reshape(latent_count, H, head_value)
        values_grad = jnp.einsum(
            "hji,jhv->ihv",
            weights.astype(jnp.bfloat16),
            sum_heads,
            preferred_element_type=jnp.float32,
        ).astype(jnp.bfloat16)
        weights_grad = (
            jnp.einsum("jhv,ihv->hji", sum_heads, values_seq, preferred_element_type=jnp.float32)
            + jnp.transpose(total_all.astype(jnp.float32))[:, :, None]
        )
        score_grad = (weights * weights_grad).astype(jnp.bfloat16)
        query_part = scale * jnp.einsum(
            "hji,ihd->jhd", score_grad, keys_seq, preferred_element_type=jnp.float32
        )
        keys_grad = (
            scale
            * jnp.einsum("hji,jhd->ihd", score_grad, query_low, preferred_element_type=jnp.float32)
        ).astype(jnp.bfloat16)
        query_own = lax.psum_scatter(
            query_part.reshape(latent_count, QK), "fsdp", scatter_dimension=0, tiled=True
        )
        return (carry, (keys_grad, values_grad, query_own))

    _, (keys_grad, values_grad, query_own) = lax.scan(
        backward_step,
        jnp.zeros((), jnp.float32),
        (keys_low, values_low, prefix, sum_grad, total_grad),
    )
    keys_flat = keys_grad.reshape(seq_count * seq_rows, QK)
    values_flat = values_grad.reshape(seq_count * seq_rows, VD)
    key_local = jnp.einsum("rb,rq->bq", byte_low, keys_flat, preferred_element_type=jnp.float32)
    value_local = jnp.einsum("rb,rv->bv", byte_low, values_flat, preferred_element_type=jnp.float32)
    normed_grad = jnp.einsum(
        "rq,bq->rb", keys_flat, key_full, preferred_element_type=jnp.float32
    ) + jnp.einsum("rv,bv->rb", values_flat, value_full, preferred_element_type=jnp.float32)
    byte_part = jnp.sum(normed_grad * byte_hat, axis=0)
    byte_grads = norm_back(normed_grad, byte_hat, byte_inv, byte_gain).reshape(
        seq_count, seq_rows, byte_width
    )
    query_grad_low = query_own.astype(jnp.bfloat16)
    own_low = lax.dynamic_slice_in_dim(latent_low, shard_index * own_latents, own_latents, 0)
    own_hat = lax.dynamic_slice_in_dim(latent_hat, shard_index * own_latents, own_latents, 0)
    own_inv = lax.dynamic_slice_in_dim(latent_inv, shard_index * own_latents, own_latents, 0)
    query_local = jnp.einsum(
        "ld,slq->dq", own_low, query_grad_low, preferred_element_type=jnp.float32
    )
    latent_grad = jnp.einsum(
        "slq,dq->ld", query_grad_low, query_full, preferred_element_type=jnp.float32
    )
    query_part_gain = jnp.sum(latent_grad * own_hat, axis=0)
    init_local = init_rows + norm_back(latent_grad, own_hat, own_inv, query_gain)
    byte_norm, query_norm, mixer_norm = lax.psum(
        (byte_part, query_part_gain, mixer_part), ("rep", "fsdp")
    )
    group_parts = (
        lax.psum_scatter(query_local, "fsdp", scatter_dimension=0, tiled=True),
        lax.psum_scatter(key_local, "fsdp", scatter_dimension=0, tiled=True),
        lax.psum_scatter(value_local, "fsdp", scatter_dimension=0, tiled=True),
        lax.psum_scatter(out_local, "fsdp", scatter_dimension=0, tiled=True),
        lax.psum_scatter(up_local, "fsdp", scatter_dimension=0, tiled=True),
        lax.psum_scatter(down_local, "fsdp", scatter_dimension=0, tiled=True),
    )
    query_grads, key_grads, value_grads, out_grads, up_grads, down_grads, init_grads = lax.psum(
        (
            group_parts[0],
            group_parts[1],
            group_parts[2],
            group_parts[3],
            group_parts[4],
            group_parts[5],
            init_local,
        ),
        "rep",
    )
    return (
        latents,
        byte_grads,
        init_grads,
        byte_norm,
        query_norm,
        mixer_norm,
        query_grads,
        key_grads,
        value_grads,
        out_grads,
        up_grads,
        down_grads,
    )


BF = jnp.bfloat16
F32 = jnp.float32
N = 8
NZ = 4
COST = pl.CostEstimate(flops=100_000_000_000, bytes_accessed=1024, transcendentals=0)
LOG2E = 1.4426950408889634
ANY = pl.BlockSpec(memory_space=pl.ANY)
VMEM = pl.BlockSpec(memory_space=pltpu.VMEM)
SMEM = pl.BlockSpec(memory_space=pltpu.SMEM)


def dot(a, b, ca, cb):
    return lax.dot_general(a, b, (((ca,), (cb,)), ((), ())), preferred_element_type=F32)


def send(x, k):
    return lax.ppermute(x, "fsdp", [(i, i ^ k) for i in range(N)])


def send_split(x, even, odd):
    return lax.ppermute(x, "fsdp", [(i, i ^ (odd if i & 1 else even)) for i in range(N)])


def send_z(x, k):
    return lax.ppermute(x, "rep", [(i, i ^ k) for i in range(NZ)])


def after(x, *deps):
    return lax.optimization_barrier((x, *deps))[0]


def me_z():
    return lax.axis_index("fsdp"), lax.axis_index("rep")


def owner(me, rel):
    even, odd = rel
    if even == odd:
        return me ^ even
    return me ^ jnp.where((me & 1) == 0, even, odd)


def call(body, out, ins, specs, scratch=(), name=None, grid=(), deps=(), out_specs=None, aliases=None):
    n, skip = len(ins), len(deps)

    def run(*refs):
        return body(*refs[:n], *refs[n + skip :])

    return pl.pallas_call(
        run,
        grid=grid,
        out_shape=out,
        in_specs=list(specs) + [ANY] * skip,
        out_specs=jax.tree.map(lambda _: VMEM, out) if out_specs is None else out_specs,
        scratch_shapes=list(scratch),
        input_output_aliases=aliases or {},
        name=name,
        cost_estimate=COST,
    )(*ins, *deps)


def sds(shape, dtype):
    return jax.ShapeDtypeStruct(shape, dtype)


def ln_parts(v):
    centered = v - jnp.mean(v, axis=-1, keepdims=True)
    inverse = lax.rsqrt(jnp.mean(centered * centered, axis=-1, keepdims=True) + EPSILON)
    return centered * inverse, inverse


def ln_back(grad, hat, inverse, gain):
    scaled = grad * gain
    return inverse * (
        scaled
        - jnp.mean(scaled, axis=-1, keepdims=True)
        - hat * jnp.mean(scaled * hat, axis=-1, keepdims=True)
    )


WIDE = ((0, 0), (1, 1), (2, 4), (4, 2), (6, 6), (5, 3), (3, 5), (7, 7))
DIRECT = tuple((k, k) for k in range(N))


def pack_kernel(wk, wq, lat, wv, out):
    rows = wk.shape[0]
    out[0:rows, :] = wk[...]
    at = rows
    out[at : at + wq.shape[0], :] = wq[...]
    at += wq.shape[0]
    for c in range(5):
        out[at : at + lat.shape[0], :] = lat[:, 256 * c : 256 * (c + 1)]
        at += lat.shape[0]
    for c in range(5):
        out[at : at + wv.shape[0], :] = wv[:, 256 * c : 256 * (c + 1)]
        at += wv.shape[0]


def pack_rows_kernel(a, b, c, out):
    rows = a.shape[0]
    for n, ref in enumerate((a, b, c)):
        out[rows * n : rows * (n + 1), :] = ref[...]


def rows_of(j, size):
    return pl.ds(pl.multiple_of(j * size, size & -size), size)


def run_copies(copies, sem):
    handles = [pltpu.make_async_copy(a, b, sem.at[n]) for n, (a, b) in enumerate(copies)]
    for h in handles:
        h.start()
    return handles


def wait_all(handles):
    for h in handles:
        h.wait()


def norm_kernel(x, bg, xn_o):
    hat, _ = ln_parts(x[...].astype(F32))
    xn_o[...] = (hat * bg[...][None, :]).astype(BF)


def query_kernel(xn, qg, *rest):
    pieces, (k_o, wk_o, wq_o, q_o, zn_o, lat, sem) = rest[:N], rest[N:]
    me, _ = me_z()
    copies = []
    for piece, rel in zip(pieces, WIDE):
        j = owner(me, rel)
        copies.append((piece.at[pl.ds(0, 96), :], wk_o.at[rows_of(j, 96), :]))
        copies.append((piece.at[pl.ds(96, 160), :], wq_o.at[rows_of(j, 160), :]))
        for c in range(5):
            copies.append((piece.at[pl.ds(256 + 32 * c, 32), :], lat.at[rows_of(j, 32), pl.ds(256 * c, 256)]))
    wait_all(run_copies(copies, sem))
    zhat, _ = ln_parts(lat[...].astype(F32))
    zn_o[...] = (zhat * qg[...][None, :]).astype(BF)
    q_o[...] = dot(zn_o[...], wq_o[...], 1, 0).astype(BF)
    k_o[...] = dot(xn[...], wk_o[...], 1, 0).astype(BF)


def scores_kernel(prefix, k, q, e_o, ll_o):
    me, _ = me_z()
    lanes = lax.broadcasted_iota(jnp.int32, (256, 256), 1) // 32
    pos = lax.broadcasted_iota(jnp.int32, (256, 512), 1) + me * 512
    own = STRIDE * (lax.broadcasted_iota(jnp.int32, (256, 1), 0) + 1)
    lane = lax.broadcasted_iota(jnp.int32, (256, 128), 1)
    ll_o[...] = jnp.zeros_like(ll_o)
    for s in range(2):
        seen = jnp.maximum(own, prefix[s])

        def head(h, carry, s=s, seen=seen):
            qh = jnp.where(lanes == h, q[...], jnp.zeros((), BF))
            scores = dot(qh, k[512 * s : 512 * (s + 1), :], 1, 1)
            e = jnp.where(pos < seen, jnp.exp2(scores * (LOG2E * 32 ** (-0.5))), 0.0)
            ll_o[s] += jnp.where(lane == h, jnp.sum(e, axis=-1, keepdims=True), 0.0)
            e_o[s, h] = e.astype(BF)
            return carry

        lax.fori_loop(0, H, head, 0, unroll=2)


def values_kernel(xn, *rest):
    pieces, (vt_o, wv_o, sem) = rest[:N], rest[N:]
    me, _ = me_z()
    wait_all(
        run_copies(
            [
                (p.at[pl.ds(416 + 96 * c, 96), :], wv_o.at[rows_of(owner(me, rel), 96), pl.ds(256 * c, 256)])
                for p, rel in zip(pieces, WIDE)
                for c in range(5)
            ],
            sem,
        )
    )
    for c in range(5):
        cols = slice(256 * c, 256 * (c + 1))
        vt_o[cols, :] = dot(wv_o[:, cols], xn[...], 0, 1).astype(BF)


def sums_kernel(vt, e, ll, *rest):
    mine_o, theirs_o, aat, acc = rest[-4:]
    me, _ = me_z()

    def head(h, carry):
        rows = rows_of(h, 160)
        aat[rows, :] = dot(vt[rows, :], e[h], 1, 1).astype(BF)
        return carry

    lax.fori_loop(0, H, head, 0, unroll=2)
    acc[:, 0:1280] = aat[...].T
    acc[:, 1280:1408] = ll[...].astype(BF)
    for kk in range(4):
        for odd, ref in ((0, mine_o), (1, theirs_o)):
            ref[kk] = acc[rows_of(me ^ (2 * kk + odd), 32), :]


def add4_kernel(a, b, *outs):
    for kk in range(4):
        outs[kk][...] = (a[kk].astype(F32) + b[kk].astype(F32)).astype(BF)


def latent_kernel(m0, r1, r2, r3, lat, mg1, cot, *rest):
    pieces, rest = rest[:N], rest[N:]
    latents_o, agb_o, mine_o, theirs_o, dab_o, init_o = rest[:6]
    wout, wup, wdown, sem = rest[6:]
    me, zi = me_z()
    groups = []
    for g, w in enumerate((wout, wup, wdown)):
        copies = [
            (p.at[pl.ds(160 * g, 160), :], w.at[rows_of(owner(me, rel), 160), :]) for p, rel in zip(pieces, WIDE)
        ]
        groups.append(run_copies(copies, sem.at[g]))
    mg = mg1[...][None, :]
    total = (m0[...].astype(F32) + r1[...].astype(F32)) + (r2[...].astype(F32) + r3[...].astype(F32))
    aa = total[:, 0:1280]
    ll = total[:, 1280:1408]
    head = lax.broadcasted_iota(jnp.int32, (64, 1280), 1) // 160
    inv = jnp.zeros((64, 1280), F32)
    for h in range(H):
        inv = jnp.where(head == h, 1.0 / ll[:, h : h + 1], inv)
    oo = aa * inv
    ob = oo.astype(BF)
    for h in groups[0]:
        h.wait()
    start = lat[...].astype(F32)
    hh = jnp.concatenate([start, start], axis=0) + dot(ob, wout[...], 1, 0)
    hat, inverse = ln_parts(hh)
    hn = (hat * mg).astype(BF)
    for h in groups[1]:
        h.wait()
    uu = dot(hn, wup[...], 1, 0)
    cdf = 0.5 * (1.0 + lax.erf(uu * (0.5**0.5)))
    gg = (uu * cdf).astype(BF)
    slope = cdf + uu * (jnp.exp(-0.5 * uu * uu) * 0.3989422804014327)
    for h in groups[2]:
        h.wait()
    latents_o[...] = (hh + dot(gg, wdown[...], 1, 0)).astype(BF)
    du = (dot(cot[...], wdown[...], 1, 1) * slope).astype(BF)
    dhn = dot(du, wup[...], 1, 1)
    dhh = cot[...].astype(F32) + ln_back(dhn, hat, inverse, mg)
    init_o[...] = dhh[0:32] + dhh[32:64]
    dhb = dhh.astype(BF)
    dob = dot(dhb, wout[...], 1, 1).astype(BF).astype(F32)
    dab_o[:, 0:1280] = (dob * inv).astype(BF)
    prod = dob * oo
    lane = lax.broadcasted_iota(jnp.int32, (64, 128), 1)
    dlb = jnp.zeros((64, 128), F32)
    for h in range(H):
        part = jnp.sum(jnp.where(head == h, prod, 0.0), axis=-1, keepdims=True)
        dlb = jnp.where(lane == h, -part / ll[:, h : h + 1], dlb)
    dab_o[:, 1280:1408] = dlb.astype(BF)
    agb_o[0] = dhb
    agb_o[1] = du
    agb_o[2] = cot[...]
    for j in range(N):
        kk = (me >> 1) ^ (j >> 1)
        cols = slice(160 * j, 160 * (j + 1))

        @pl.when((me & 1) == (j & 1))
        def _():
            for n, v in enumerate((ob, hn, gg)):
                mine_o[kk, n] = v[:, cols]

        @pl.when((me & 1) != (j & 1))
        def _():
            for n, v in enumerate((ob, hn, gg)):
                theirs_o[kk, n] = v[:, cols]


def stack_kernel(mine, other, *outs):
    for kk in range(1, 4):
        outs[kk - 1][0] = mine[kk]
        outs[kk - 1][1] = other[kk]


def backward_kernel(s, k, vt, q, e, *rest):
    pieces, rest = rest[:N], rest[N + s :]
    dkvt_o, dq_o = rest[:2]
    dabx, dabt, qt, sem = rest[2:]
    me, _ = me_z()
    handles = run_copies(
        [(p.at[pl.ds(32 * s, 32), :], dabx.at[rows_of(owner(me, rel), 32), :]) for p, rel in zip(pieces, DIRECT)], sem
    )
    qt[...] = q[...].T
    dq_o[...] = jnp.zeros_like(dq_o)
    wait_all(handles)
    lanes = lax.broadcasted_iota(jnp.int32, (256, 256), 1) // 32
    lane = lax.broadcasted_iota(jnp.int32, (256, 128), 1)
    scale = 32 ** (-0.5)
    dabt[...] = dabx[:, 0:1280].T

    def head(h, carry):
        rows = rows_of(h, 160)
        dkvt_o[pl.ds(pl.multiple_of(256 + h * 160, 32), 160), :] = dot(dabt[rows, :], e[h], 1, 0).astype(BF)
        dlb = jnp.sum(jnp.where(lane == h, dabx[:, 1280:1408].astype(F32), 0.0), axis=-1, keepdims=True)
        dee = dot(dabt[rows, :], vt[rows, :], 0, 0) + dlb
        dss = (e[h].astype(F32) * dee).astype(BF)
        krows = rows_of(h, 32)
        dkvt_o[krows, :] = (dot(qt[krows, :], dss, 1, 0) * scale).astype(BF)
        dq_o[...] += jnp.where(lanes == h, dot(dss, k[...], 1, 0), 0.0)
        return carry

    lax.fori_loop(0, H, head, 0, unroll=2)
    dq_o[...] = dq_o[...] * scale


def weights_kernel(xn, zn, dkvt, dq0, dq1, mine_o, theirs_o, xnt, dw, dqg, dqs):
    me, _ = me_z()
    xnt[...] = xn[...].T
    dqs[...] = dq0[...] + dq1[...]
    for c in range(6):
        cols = slice(256 * c, 256 * (c + 1))
        dw[:, cols] = dot(xnt[...], dkvt[cols, :], 1, 1).astype(BF)
    dqg[...] = dot(zn[...], dqs[...].astype(BF), 0, 0).astype(BF)
    for kk in range(4):
        for odd, ref in ((0, mine_o), (1, theirs_o)):
            j = me ^ (2 * kk + odd)
            for c in range(6):
                ref[kk, 96 * c : 96 * (c + 1), :] = dw[rows_of(j, 96), 256 * c : 256 * (c + 1)]
            ref[kk, 576:736, :] = dqg[rows_of(j, 160), :]
            ref[kk, 736:768, :] = dqs[rows_of(j, 32), :].astype(BF)


def own_part(gain, me, size):
    out = gain[0:size][None, :]
    for j in range(1, N):
        out = jnp.where(me == j, gain[size * j : size * (j + 1)][None, :], out)
    return out


def sum_slots_kernel(a, b, c, d, wk, wv, wq, bg, qg, mix, *rest):
    outs, norm_o, acc = rest[:NZ], rest[NZ], rest[NZ + 1]
    me, zi = me_z()
    total = (a[...].astype(F32) + b[...].astype(F32)) + (c[...].astype(F32) + d[...].astype(F32))
    acc[...] = total.astype(BF)
    for r in range(NZ):
        outs[r][...] = acc[rows_of(zi ^ r, 192), :]
    prod = total[0:96] * wk[...].astype(F32)
    for n in range(5):
        prod += total[96 * (n + 1) : 96 * (n + 2)] * wv[:, 256 * n : 256 * (n + 1)].astype(F32)
    parts = (
        (row_sums(prod) / own_part(bg[...], me, 96), 96),
        (mix[...], 160),
        (row_sums(total[576:736] * wq[...].astype(F32)) / own_part(qg[...], me, 160), 160),
    )
    row = lax.broadcasted_iota(jnp.int32, (8, 1280), 0)
    placed = jnp.zeros((8, 1280), F32)
    for n, (v, size) in enumerate(parts):
        at = lax.broadcasted_iota(jnp.int32, (size, 1280), 1)
        pick = (at == lax.broadcasted_iota(jnp.int32, (size, 1280), 0) + size * me).astype(F32)
        wide = lax.dot_general(
            v, pick, (((1,), (0,)), ((), ())), precision=lax.Precision.HIGHEST, preferred_element_type=F32
        )
        placed = jnp.where(row == n, wide, placed)
    norm_o[...] = placed


def bytes_kernel(x, bg, wk, wv, dkvt, *rest):
    out = rest[-1]
    hat, inverse = ln_parts(x[...].astype(F32))
    dxn = dot(dkvt[0:256, :], wk[...], 0, 1) + dot(dkvt[256:1536, :], wv[...], 0, 1)
    out[...] = ln_back(dxn, hat, inverse, bg[...][None, :])


def latent_grads_kernel(init, wup, mg, amine, at, b1, b2, b3, *rest):
    rows, outs, mix_o, (xs, ys, acc, sem) = rest[:N], rest[N : N + 4], rest[N + 4], rest[N + 5 :]
    me, zi = me_z()
    copies = []
    cols = (amine.at[0], at.at[0], b1.at[0], b1.at[1], b2.at[0], b2.at[1], b3.at[0], b3.at[1])
    for k in range(N):
        copies.append((cols[k], xs.at[:, rows_of(me ^ k, 64), :]))
        copies.append((rows[k], ys.at[:, rows_of(owner(me, WIDE[k]), 64), :]))
    wait_all(run_copies(copies, sem))
    for n in range(3):
        grad = dot(xs[n], ys[n], 0, 0)
        acc[160 * n : 160 * (n + 1), :] = grad.astype(BF)
        if n == 1:
            mix_o[...] = row_sums(grad * wup[...].astype(F32)) / own_part(mg[...], me, 160)
    acc[480:512, :] = init[...].astype(BF)
    for r in range(NZ):
        outs[r][...] = acc[rows_of(zi ^ r, 128), :]


def row_sums(v):
    ones = jnp.ones((8, v.shape[1]), F32)
    return lax.dot_general(
        ones, v, (((1,), (1,)), ((), ())), precision=lax.Precision.HIGHEST, preferred_element_type=F32
    )


def finish_latent_kernel(*rest):
    pieces, (out_o, up_o, down_o, init_o, acc) = rest[:NZ], rest[NZ:]
    _, zi = me_z()
    for r in range(NZ):
        acc[rows_of(zi ^ r, 128), :] = pieces[r][...]
    out_o[...] = acc[0:160, :].astype(F32)
    up_o[...] = acc[160:320, :].astype(F32)
    down_o[...] = acc[320:480, :].astype(F32)
    init_o[...] = acc[480:512, :].astype(F32)


def finish_kernel(wq_full, lat, qg, init, *rest):
    pieces, (key_o, value_o, query_o, init_o, acc) = rest[:NZ], rest[NZ:]
    _, zi = me_z()
    for r in range(NZ):
        acc[rows_of(zi ^ r, 192), :] = pieces[r][...]
    key_o[...] = acc[0:96, :].astype(F32)
    for c in range(5):
        value_o[:, 256 * c : 256 * (c + 1)] = acc[96 * (c + 1) : 96 * (c + 2), :].astype(F32)
    query_o[...] = acc[576:736, :].astype(F32)
    dzn = dot(acc[736:768, :], wq_full[...], 1, 1)
    hat, inverse = ln_parts(lat[...].astype(F32))
    init_o[...] = init[...] + ln_back(dzn, hat, inverse, qg[...][None, :])


def norms_kernel(a, b, byte_o, mixer_o, query_o):
    total = a[...] + b[...]
    row = lax.broadcasted_iota(jnp.int32, (8, 1280), 0)
    for n, out in enumerate((byte_o, mixer_o, query_o)):
        out[...] = jnp.sum(jnp.where(row == n, total, 0.0), axis=0)[: out.shape[0]]


def sums_of_pairs_kernel(*refs):
    n = len(refs) // 3
    for k in range(n):
        a, b, out = refs[2 * k], refs[2 * k + 1], refs[2 * n + k]
        out[...] = (a[...].astype(F32) + b[...].astype(F32)).astype(out.dtype)


def sums_of_pairs(pairs, name, deps=()):
    flat = [x for pair in pairs for x in pair]
    out = [sds(a.shape, a.dtype) for a, _ in pairs]
    return call(sums_of_pairs_kernel, out, flat, [VMEM] * len(flat), name=name, deps=deps)


def part(f, *args):
    def body(*refs):
        return f(*args, *refs)

    return body


def tie(*xs):
    return lax.optimization_barrier(xs)


def per_device_fast(
    byte_feats,
    latent_init,
    prefix,
    byte_gain,
    query_gain,
    mixer_gain,
    query_weight,
    key_weight,
    value_weight,
    out_weight,
    up_weight,
    down_weight,
    cotangent,
):
    seqs, rows, width = byte_feats.shape
    own = latent_init.shape[0]
    x = byte_feats.reshape(seqs * rows, width)
    cot = cotangent.reshape(seqs * own, DL)

    def first(w):
        return send_split(w, 2, 4), send_split(w, 4, 2)

    packed = call(
        pack_kernel, sds((896, 256), BF), (key_weight, query_weight, latent_init, value_weight), [VMEM] * 4, name="pack"
    )
    pa, pb = first(packed)
    wcat = call(
        pack_rows_kernel, sds((480, 1280), BF), (out_weight, up_weight, down_weight), [VMEM] * 3, name="pack_rows", deps=(packed,)
    )
    xn = call(norm_kernel, sds((1024, 768), BF), (x, byte_gain), [VMEM] * 2, name="norm", deps=(wcat,))
    pa, pb, xn, near = tie(pa, pb, xn, packed)
    pd = send_split(pa, 4, 2)
    pn, pna, pnb = send(near, 1), send(pa, 1), send(pb, 1)
    pd, wcat = tie(pd, wcat)
    pnd = send(pd, 1)
    wa, wb = first(wcat)
    wn = send(wcat, 1)
    pieces = (packed, pn, pa, pb, pd, pna, pnb, pnd)
    k, wk, wq_full, q, zn = call(
        query_kernel,
        (sds((1024, 256), BF), sds((768, 256), BF), sds((1280, 256), BF), sds((256, 256), BF), sds((256, 1280), BF)),
        (xn, query_gain, *pieces),
        [VMEM] * 2 + [ANY] * N,
        [pltpu.VMEM((256, 1280), BF), pltpu.SemaphoreType.DMA((7 * N,))],
        name="query",
    )
    e, ll = call(
        scores_kernel,
        (sds((2, 8, 256, 512), BF), sds((2, 256, 128), F32)),
        (prefix, k, q),
        [SMEM, VMEM, VMEM],
        name="scores",
    )
    vt, wv = call(
        values_kernel,
        (sds((1280, 1024), BF), sds((768, 1280), BF)),
        (xn, *pieces),
        [VMEM] + [ANY] * N,
        [pltpu.SemaphoreType.DMA((5 * N,))],
        name="values",
        deps=(e, wn),
    )
    def sums(s, *prev):
        return call(
            sums_kernel,
            (sds((4, 64, 1408), BF), sds((4, 64, 1408), BF)),
            (vt, e, ll, *prev),
            [
                pl.BlockSpec((1280, 512), lambda g: (0, s)),
                pl.BlockSpec((None, 8, 256, 512), lambda g: (s, 0, 0, 0)),
                pl.BlockSpec((None, 256, 128), lambda g: (s, 0, 0)),
            ]
            + [ANY] * len(prev),
            [pltpu.VMEM((1280, 256), BF), pltpu.VMEM((256, 1408), BF)],
            out_specs=[pl.BlockSpec((4, 32, 1408), lambda g: (0, s, 0))] * 2,
            aliases={3: 0, 4: 1} if prev else {},
            name="sums",
            grid=(1,),
        )

    mine, theirs = sums(0)
    mine, wa, wb = tie(mine, wa, wb)
    wd = send_split(wa, 4, 2)
    wna, wnb = send(wa, 1), send(wb, 1)
    mine, theirs = sums(1, mine, theirs)
    got = send(theirs, 1)
    m0, m1, m2, m3 = call(
        add4_kernel, (sds((64, 1408), BF),) * 4, (mine, got), [VMEM] * 2, name="add4", deps=(wna, wnb)
    )
    r1, r2, r3 = send(m1, 2), send(m2, 4), send(m3, 6)
    r1, r2, r3, wd = tie(r1, r2, r3, wd)
    wnd = send(wd, 1)
    latents, agb, amine, atheirs, dabx, init = call(
        latent_kernel,
        (
            sds((64, 1280), BF), sds((3, 64, 1280), BF), sds((4, 3, 64, 160), BF), sds((4, 3, 64, 160), BF),
            sds((64, 1408), BF), sds((32, 1280), F32),
        ),
        (m0, r1, r2, r3, latent_init, mixer_gain, cot, wcat, wn, wa, wb, wd, wna, wnb, wnd),
        [VMEM] * 7 + [ANY] * N,
        [pltpu.VMEM((1280, 1280), BF)] * 3 + [pltpu.SemaphoreType.DMA((3, N))],
        name="latent",
    )
    d2, d4, d6, d1 = send(dabx, 2), send(dabx, 4), send(dabx, 6), send(dabx, 1)
    at = send(atheirs, 1)
    d2, d4, d6, agb = tie(d2, d4, d6, agb)
    d3, d5, d7 = send(d2, 1), send(d4, 1), send(d6, 1)
    dab_p = [dabx, d1, d2, d3, d4, d5, d6, d7]
    ga, gb = first(agb)
    gn = send(agb, 1)

    def backward(s, *prev):
        return call(
            part(backward_kernel, s),
            (sds((1536, 1024), BF), sds((256, 256), F32)),
            (k, vt, q, e, *dab_p, *prev),
            [
                pl.BlockSpec((512, 256), lambda g: (s, 0)),
                pl.BlockSpec((1280, 512), lambda g: (0, s)),
                VMEM,
                pl.BlockSpec((None, 8, 256, 512), lambda g: (s, 0, 0, 0)),
            ]
            + [ANY] * (N + len(prev)),
            [
                pltpu.VMEM((256, 1408), BF), pltpu.VMEM((1280, 256), BF), pltpu.VMEM((256, 256), BF),
                pltpu.SemaphoreType.DMA((N,)),
            ],
            out_specs=(pl.BlockSpec((1536, 512), lambda g: (0, s)), VMEM),
            aliases={4 + N: 0} if prev else {},
            name="backward",
            grid=(1,),
            deps=deps_of[s],
        )

    deps_of = {0: ()}
    dkvt, dq0 = backward(0)
    dq0, ga, gb, gn, at = tie(dq0, ga, gb, gn, at)
    gd = send_split(ga, 4, 2)
    gna = send(ga, 1)
    both = call(stack_kernel, (sds((2, 3, 64, 160), BF),) * 3, (amine, at), [VMEM] * 2, name="stack", deps=(dq0,))
    both_s = [send(b, 2 * kk + 2) for kk, b in enumerate(both)]
    deps_of[1] = (both[0], dq0)
    dkvt, dq1 = backward(1, dkvt)
    dq1, gd, gna, gb = tie(dq1, gd, gna, gb)
    gnb, gnd = send(gb, 1), send(gd, 1)
    gmine, gtheirs = call(
        weights_kernel,
        (sds((4, 768, 256), BF), sds((4, 768, 256), BF)),
        (xn, zn, dkvt, dq0, dq1),
        [VMEM] * 5,
        [
            pltpu.VMEM((768, 1024), BF), pltpu.VMEM((768, 1536), BF), pltpu.VMEM((1280, 256), BF),
            pltpu.VMEM((256, 256), F32),
        ],
        name="weights",
        deps=(),
    )
    gg = send(gtheirs, 1)

    *oud, mix = call(
        latent_grads_kernel,
        (sds((128, 1280), BF),) * NZ + (sds((8, 160), F32),),
        (init, up_weight, mixer_gain, amine, at, *both_s, agb, gn, ga, gb, gd, gna, gnb, gnd),
        [VMEM] * 3 + [ANY] * (5 + N),
        [
            pltpu.VMEM((3, 512, 160), BF), pltpu.VMEM((3, 512, 1280), BF), pltpu.VMEM((512, 1280), BF),
            pltpu.SemaphoreType.DMA((2 * N,)),
        ],
        name="latent_grads",
        deps=(gtheirs,),
    )
    o3, o1 = send_z(oud[3], 1), send_z(oud[1], 1)
    gm = call(add4_kernel, (sds((768, 256), BF),) * 4, (gmine, gg), [VMEM] * 2, name="add4g", deps=(oud[0],))
    g1, g2, g3 = send(gm[1], 2), send(gm[2], 4), send(gm[3], 6)
    byte_grads = call(
        bytes_kernel,
        sds((2, 512, 768), F32),
        (x, byte_gain, wk, wv, dkvt),
        [
            pl.BlockSpec((256, 768), lambda b: (b, 0)),
            pl.BlockSpec((768,), lambda b: (0,)),
            pl.BlockSpec((768, 256), lambda b: (0, 0)),
            pl.BlockSpec((768, 1280), lambda b: (0, 0)),
            pl.BlockSpec((1536, 256), lambda b: (0, b)),
        ],
        out_specs=pl.BlockSpec((None, 256, 768), lambda b: (b // 2, b % 2, 0)),
        name="bytes",
        grid=(4,),
        deps=(gm[0],),
    )
    o2, o0 = sums_of_pairs(((oud[2], o3), (oud[0], o1)), "osum", deps=(byte_grads,))
    o22 = send_z(o2, 2)
    *gq, norm = call(
        sum_slots_kernel,
        (sds((192, 256), BF),) * NZ + (sds((8, 1280), F32),),
        (gm[0], g1, g2, g3, key_weight, value_weight, query_weight, byte_gain, query_gain, mix),
        [VMEM] * 10,
        [pltpu.VMEM((768, 256), BF)],
        name="gsum",
        deps=(o0,),
    )
    q3, q1, n1 = send_z(gq[3], 1), send_z(gq[1], 1), send_z(norm, 1)
    q2, q0, norm, ototal = sums_of_pairs(((gq[2], q3), (gq[0], q1), (norm, n1), (o0, o22)), "qsum")
    ofar, onear = send_z(ototal, 2), send_z(ototal, 1)
    q22, n2 = send_z(q2, 2), send_z(norm, 2)
    qtotal, norm = sums_of_pairs(((q0, q22), (norm, n2)), "qtotal")
    qfar, qnear, n3 = send_z(qtotal, 2), send_z(qtotal, 1), send(norm, 1)
    ofar2 = send_z(ofar, 1)
    (norm,) = sums_of_pairs(((norm, n3),), "nsum")
    n4 = send(norm, 2)
    qfar2 = send_z(qfar, 1)
    out_g, up_g, down_g, init_sum = call(
        finish_latent_kernel,
        (sds((160, 1280), F32),) * 3 + (sds((32, 1280), F32),),
        (ototal, onear, ofar, ofar2),
        [VMEM] * NZ,
        [pltpu.VMEM((512, 1280), BF)],
        name="finish_latent",
        deps=(norm,),
    )
    (norm,) = sums_of_pairs(((norm, n4),), "nsum", deps=(init_sum,))
    n5 = send(norm, 4)
    key_g, value_g, query_g, init_g = call(
        finish_kernel,
        (sds((96, 256), F32), sds((96, 1280), F32), sds((160, 256), F32), sds((32, 1280), F32)),
        (wq_full, latent_init, query_gain, init_sum, qtotal, qnear, qfar, qfar2),
        [VMEM] * (4 + NZ),
        [pltpu.VMEM((768, 256), BF)],
        name="finish",
        deps=(norm,),
    )
    byte_n, mixer_n, query_n = call(
        norms_kernel,
        (sds((768,), F32), sds((1280,), F32), sds((1280,), F32)),
        (norm, n5),
        [VMEM] * 2,
        name="norms",
        deps=(init_g,),
    )
    return (
        latents.reshape(seqs, own, DL),
        byte_grads,
        init_g,
        byte_n,
        query_n,
        mixer_n,
        query_g,
        key_g,
        value_g,
        out_g,
        up_g,
        down_g,
    )


def solution(mesh):
    fast = mesh.shape["fsdp"] == 8 and mesh.shape["rep"] == 4
    device_fn = per_device_fast if fast else per_device_plain
    placed = (
        P("rep", "fsdp", None),
        P("fsdp", None),
        P("rep"),
        P(),
        P(),
        P(),
        P("fsdp", None),
        P("fsdp", None),
        P("fsdp", None),
        P("fsdp", None),
        P("fsdp", None),
        P("fsdp", None),
        P("rep", "fsdp", None),
    )
    return jax.shard_map(
        device_fn,
        mesh=mesh,
        in_specs=placed,
        out_specs=(
            P("rep", "fsdp", None),
            P("rep", "fsdp", None),
            P("fsdp", None),
            P(),
            P(),
            P(),
            P("fsdp", None),
            P("fsdp", None),
            P("fsdp", None),
            P("fsdp", None),
            P("fsdp", None),
            P("fsdp", None),
        ),
        check_vma=False,
    )
```

```python
import jax
import jax.numpy as jnp
from jax import lax
from jax.experimental import pallas as pl
from jax.experimental.pallas import tpu as pltpu
from jax.sharding import PartitionSpec as P

DL = 1280
H = 8
QK = 256
VD = 1280
STRIDE = 16


EPSILON = 1e-05


def norm_parts(values, gain):
    centered = values - jnp.mean(values, axis=-1, keepdims=True)
    variance = jnp.mean(centered * centered, axis=-1, keepdims=True)
    inverse = lax.rsqrt(variance + EPSILON)
    normal = centered * inverse
    return (normal * gain, normal, inverse)


def norm_back(grad_out, normal, inverse, gain):
    scaled = grad_out * gain
    mean_one = jnp.mean(scaled, axis=-1, keepdims=True)
    mean_two = jnp.mean(scaled * normal, axis=-1, keepdims=True)
    return inverse * (scaled - mean_one - normal * mean_two)


def per_device_plain(
    byte_feats,
    latent_init,
    prefix,
    byte_gain,
    query_gain,
    mixer_gain,
    query_weight,
    key_weight,
    value_weight,
    out_weight,
    up_weight,
    down_weight,
    cotangent,
):
    shard_count = lax.axis_size("fsdp")
    shard_index = lax.axis_index("fsdp")
    seq_count, seq_rows, byte_width = byte_feats.shape
    own_latents = latent_init.shape[0]
    latent_count = own_latents * shard_count
    head_qk = QK // H
    head_value = VD // H
    scale = head_qk ** (-0.5)
    row_count = seq_count * own_latents
    latent_all, query_full, key_full, value_full = (
        lax.all_gather(latent_init, "fsdp", axis=0, tiled=True),
        lax.all_gather(query_weight, "fsdp", axis=0, tiled=True),
        lax.all_gather(key_weight, "fsdp", axis=0, tiled=True),
        lax.all_gather(value_weight, "fsdp", axis=0, tiled=True),
    )
    out_full, up_full, down_full = (
        lax.all_gather(out_weight, "fsdp", axis=0, tiled=True),
        lax.all_gather(up_weight, "fsdp", axis=0, tiled=True),
        lax.all_gather(down_weight, "fsdp", axis=0, tiled=True),
    )
    byte_flat = byte_feats.astype(jnp.float32).reshape(seq_count * seq_rows, byte_width)
    byte_normed, byte_hat, byte_inv = norm_parts(byte_flat, byte_gain)
    byte_low = byte_normed.astype(jnp.bfloat16)
    keys_low = (
        jnp.dot(byte_low, key_full, preferred_element_type=jnp.float32)
        .astype(jnp.bfloat16)
        .reshape(seq_count, seq_rows, H, head_qk)
    )
    values_low = (
        jnp.dot(byte_low, value_full, preferred_element_type=jnp.float32)
        .astype(jnp.bfloat16)
        .reshape(seq_count, seq_rows, H, head_value)
    )
    latent_normed, latent_hat, latent_inv = norm_parts(latent_all.astype(jnp.float32), query_gain)
    latent_low = latent_normed.astype(jnp.bfloat16)
    query_low = (
        jnp.dot(latent_low, query_full, preferred_element_type=jnp.float32)
        .astype(jnp.bfloat16)
        .reshape(latent_count, H, head_qk)
    )
    byte_pos = shard_index * seq_rows + jnp.arange(seq_rows, dtype=jnp.int32)
    latent_pos = jnp.arange(latent_count, dtype=jnp.int32)

    def exp_scores(keys_seq, limit):
        scores = scale * jnp.einsum(
            "jhd,ihd->hji", query_low, keys_seq, preferred_element_type=jnp.float32
        )
        visible = (byte_pos[None, :] < limit) | (
            byte_pos[None, :] < STRIDE * (latent_pos[:, None] + 1)
        )
        return jnp.where(visible[None], jnp.exp(scores), 0.0)

    def forward_step(carry, inputs):
        keys_seq, values_seq, limit = inputs
        weights = exp_scores(keys_seq, limit)
        totals = jnp.transpose(jnp.sum(weights, axis=-1))
        summed = jnp.einsum(
            "hji,ihv->jhv",
            weights.astype(jnp.bfloat16),
            values_seq,
            preferred_element_type=jnp.float32,
        ).reshape(latent_count, VD)
        own_sum, own_total = (
            lax.psum_scatter(summed, "fsdp", scatter_dimension=0, tiled=True),
            lax.psum_scatter(totals, "fsdp", scatter_dimension=0, tiled=True),
        )
        return (carry, (own_sum, own_total))

    _, (sums_own, totals_own) = lax.scan(
        forward_step, jnp.zeros((), jnp.float32), (keys_low, values_low, prefix)
    )
    attended = sums_own.reshape(seq_count, own_latents, H, head_value) / totals_own[..., None]
    attn_low = attended.reshape(row_count, VD).astype(jnp.bfloat16)
    mixed = jnp.dot(attn_low, out_full, preferred_element_type=jnp.float32).reshape(
        seq_count, own_latents, DL
    )
    hidden = (mixed + latent_init.astype(jnp.float32)[None]).reshape(row_count, DL)
    mixer_normed, mixer_hat, mixer_inv = norm_parts(hidden, mixer_gain)
    mixer_low = mixer_normed.astype(jnp.bfloat16)
    pre_act = jnp.dot(mixer_low, up_full, preferred_element_type=jnp.float32)
    activated, gelu_back = jax.vjp(lambda value: jax.nn.gelu(value, approximate=False), pre_act)
    act_low = activated.astype(jnp.bfloat16)
    output = hidden + jnp.dot(act_low, down_full, preferred_element_type=jnp.float32)
    latents = output.reshape(seq_count, own_latents, DL).astype(jnp.bfloat16)
    cot_low = cotangent.reshape(row_count, DL)
    down_local = jnp.einsum("rf,rd->fd", act_low, cot_low, preferred_element_type=jnp.float32)
    act_grad = jnp.einsum("rd,fd->rf", cot_low, down_full, preferred_element_type=jnp.float32)
    pre_grad = gelu_back(act_grad)[0].astype(jnp.bfloat16)
    up_local = jnp.einsum("rd,rf->df", mixer_low, pre_grad, preferred_element_type=jnp.float32)
    mixer_grad = jnp.einsum("rf,df->rd", pre_grad, up_full, preferred_element_type=jnp.float32)
    mixer_part = jnp.sum(mixer_grad * mixer_hat, axis=0)
    hidden_grad = cot_low.astype(jnp.float32) + norm_back(
        mixer_grad, mixer_hat, mixer_inv, mixer_gain
    )
    hidden_low = hidden_grad.astype(jnp.bfloat16)
    out_local = jnp.einsum("rv,rd->vd", attn_low, hidden_low, preferred_element_type=jnp.float32)
    attn_grad = jnp.einsum(
        "rd,vd->rv", hidden_low, out_full, preferred_element_type=jnp.float32
    ).astype(jnp.bfloat16)
    attn_heads = attn_grad.astype(jnp.float32).reshape(seq_count, own_latents, H, head_value)
    sum_grad = (
        (attn_heads / totals_own[..., None])
        .astype(jnp.bfloat16)
        .reshape(seq_count, own_latents, VD)
    )
    total_grad = (-jnp.sum(attn_heads * attended, axis=-1) / totals_own).astype(jnp.bfloat16)
    init_rows = jnp.sum(hidden_grad.reshape(seq_count, own_latents, DL), axis=0)

    def backward_step(carry, inputs):
        keys_seq, values_seq, limit, sum_own, total_own = inputs
        sum_all, total_all = (
            lax.all_gather(sum_own, "fsdp", axis=0, tiled=True),
            lax.all_gather(total_own, "fsdp", axis=0, tiled=True),
        )
        weights = exp_scores(keys_seq, limit)
        sum_heads = sum_all.reshape(latent_count, H, head_value)
        values_grad = jnp.einsum(
            "hji,jhv->ihv",
            weights.astype(jnp.bfloat16),
            sum_heads,
            preferred_element_type=jnp.float32,
        ).astype(jnp.bfloat16)
        weights_grad = (
            jnp.einsum("jhv,ihv->hji", sum_heads, values_seq, preferred_element_type=jnp.float32)
            + jnp.transpose(total_all.astype(jnp.float32))[:, :, None]
        )
        score_grad = (weights * weights_grad).astype(jnp.bfloat16)
        query_part = scale * jnp.einsum(
            "hji,ihd->jhd", score_grad, keys_seq, preferred_element_type=jnp.float32
        )
        keys_grad = (
            scale
            * jnp.einsum("hji,jhd->ihd", score_grad, query_low, preferred_element_type=jnp.float32)
        ).astype(jnp.bfloat16)
        query_own = lax.psum_scatter(
            query_part.reshape(latent_count, QK), "fsdp", scatter_dimension=0, tiled=True
        )
        return (carry, (keys_grad, values_grad, query_own))

    _, (keys_grad, values_grad, query_own) = lax.scan(
        backward_step,
        jnp.zeros((), jnp.float32),
        (keys_low, values_low, prefix, sum_grad, total_grad),
    )
    keys_flat = keys_grad.reshape(seq_count * seq_rows, QK)
    values_flat = values_grad.reshape(seq_count * seq_rows, VD)
    key_local = jnp.einsum("rb,rq->bq", byte_low, keys_flat, preferred_element_type=jnp.float32)
    value_local = jnp.einsum("rb,rv->bv", byte_low, values_flat, preferred_element_type=jnp.float32)
    normed_grad = jnp.einsum(
        "rq,bq->rb", keys_flat, key_full, preferred_element_type=jnp.float32
    ) + jnp.einsum("rv,bv->rb", values_flat, value_full, preferred_element_type=jnp.float32)
    byte_part = jnp.sum(normed_grad * byte_hat, axis=0)
    byte_grads = norm_back(normed_grad, byte_hat, byte_inv, byte_gain).reshape(
        seq_count, seq_rows, byte_width
    )
    query_grad_low = query_own.astype(jnp.bfloat16)
    own_low = lax.dynamic_slice_in_dim(latent_low, shard_index * own_latents, own_latents, 0)
    own_hat = lax.dynamic_slice_in_dim(latent_hat, shard_index * own_latents, own_latents, 0)
    own_inv = lax.dynamic_slice_in_dim(latent_inv, shard_index * own_latents, own_latents, 0)
    query_local = jnp.einsum(
        "ld,slq->dq", own_low, query_grad_low, preferred_element_type=jnp.float32
    )
    latent_grad = jnp.einsum(
        "slq,dq->ld", query_grad_low, query_full, preferred_element_type=jnp.float32
    )
    query_part_gain = jnp.sum(latent_grad * own_hat, axis=0)
    init_local = init_rows + norm_back(latent_grad, own_hat, own_inv, query_gain)
    byte_norm, query_norm, mixer_norm = lax.psum(
        (byte_part, query_part_gain, mixer_part), ("rep", "fsdp")
    )
    group_parts = (
        lax.psum_scatter(query_local, "fsdp", scatter_dimension=0, tiled=True),
        lax.psum_scatter(key_local, "fsdp", scatter_dimension=0, tiled=True),
        lax.psum_scatter(value_local, "fsdp", scatter_dimension=0, tiled=True),
        lax.psum_scatter(out_local, "fsdp", scatter_dimension=0, tiled=True),
        lax.psum_scatter(up_local, "fsdp", scatter_dimension=0, tiled=True),
        lax.psum_scatter(down_local, "fsdp", scatter_dimension=0, tiled=True),
    )
    query_grads, key_grads, value_grads, out_grads, up_grads, down_grads, init_grads = lax.psum(
        (
            group_parts[0],
            group_parts[1],
            group_parts[2],
            group_parts[3],
            group_parts[4],
            group_parts[5],
            init_local,
        ),
        "rep",
    )
    return (
        latents,
        byte_grads,
        init_grads,
        byte_norm,
        query_norm,
        mixer_norm,
        query_grads,
        key_grads,
        value_grads,
        out_grads,
        up_grads,
        down_grads,
    )


BF = jnp.bfloat16
F32 = jnp.float32
N = 8
NZ = 4
COST = 100_000_000_000
LOG2E = 1.4426950408889634
ANY = pl.BlockSpec(memory_space=pl.ANY)
VMEM = pl.BlockSpec(memory_space=pltpu.VMEM)
SMEM = pl.BlockSpec(memory_space=pltpu.SMEM)


def dot(a, b, ca, cb):
    return lax.dot_general(a, b, (((ca,), (cb,)), ((), ())), preferred_element_type=F32)


def send(x, k):
    return lax.ppermute(x, "fsdp", [(i, i ^ k) for i in range(N)])


def send_split(x, even, odd):
    return lax.ppermute(x, "fsdp", [(i, i ^ (odd if i & 1 else even)) for i in range(N)])


def send_z(x, k):
    return lax.ppermute(x, "rep", [(i, i ^ k) for i in range(NZ)])


def after(x, *deps):
    return lax.optimization_barrier((x, *deps))[0]


def me_z():
    return lax.axis_index("fsdp"), lax.axis_index("rep")


def owner(me, rel):
    even, odd = rel
    if even == odd:
        return me ^ even
    return me ^ jnp.where((me & 1) == 0, even, odd)


def call(body, out, ins, specs, scratch=(), name=None, grid=(), deps=(), out_specs=None, aliases=None, cost=COST, lead=()):
    n, skip, ahead = len(ins), len(deps), len(lead)

    def run(*refs):
        return body(*refs[ahead : ahead + n], *refs[ahead + n + skip :])

    return pl.pallas_call(
        run,
        grid=grid,
        out_shape=out,
        in_specs=[ANY] * ahead + list(specs) + [ANY] * skip,
        out_specs=jax.tree.map(lambda _: VMEM, out) if out_specs is None else out_specs,
        scratch_shapes=list(scratch),
        input_output_aliases=aliases or {},
        name=name,
        cost_estimate=pl.CostEstimate(flops=cost, bytes_accessed=1024, transcendentals=0),
    )(*lead, *ins, *deps)


def sds(shape, dtype):
    return jax.ShapeDtypeStruct(shape, dtype)


def ln_parts(v):
    centered = v - jnp.mean(v, axis=-1, keepdims=True)
    inverse = lax.rsqrt(jnp.mean(centered * centered, axis=-1, keepdims=True) + EPSILON)
    return centered * inverse, inverse


def ln_back(grad, hat, inverse, gain):
    scaled = grad * gain
    return inverse * (
        scaled
        - jnp.mean(scaled, axis=-1, keepdims=True)
        - hat * jnp.mean(scaled * hat, axis=-1, keepdims=True)
    )


WIDE = ((0, 0), (1, 1), (2, 4), (4, 2), (6, 6), (5, 3), (3, 5), (7, 7))
DIRECT = tuple((k, k) for k in range(N))


def pack_kernel(wk, wq, lat, wv, out):
    rows = wk.shape[0]
    out[0:rows, :] = wk[...]
    at = rows
    out[at : at + wq.shape[0], :] = wq[...]
    at += wq.shape[0]
    for c in range(5):
        out[at : at + lat.shape[0], :] = lat[:, 256 * c : 256 * (c + 1)]
        at += lat.shape[0]
    for c in range(5):
        out[at : at + wv.shape[0], :] = wv[:, 256 * c : 256 * (c + 1)]
        at += wv.shape[0]


def pack_rows_kernel(a, b, c, out):
    rows = a.shape[0]
    for n, ref in enumerate((a, b, c)):
        out[rows * n : rows * (n + 1), :] = ref[...]


def rows_of(j, size):
    return pl.ds(pl.multiple_of(j * size, size & -size), size)


def run_copies(copies, sem):
    handles = [pltpu.make_async_copy(a, b, sem.at[n]) for n, (a, b) in enumerate(copies)]
    for h in handles:
        h.start()
    return handles


def wait_all(handles):
    for h in handles:
        h.wait()


def norm_kernel(x, bg, xn_o):
    hat, _ = ln_parts(x[...].astype(F32))
    xn_o[...] = (hat * bg[...][None, :]).astype(BF)


def query_kernel(xn, qg, *rest):
    pieces, (k_o, wk_o, wq_o, q_o, zn_o, lat, sem) = rest[:N], rest[N:]
    me, _ = me_z()
    copies = []
    for piece, rel in zip(pieces, WIDE):
        j = owner(me, rel)
        copies.append((piece.at[pl.ds(0, 96), :], wk_o.at[rows_of(j, 96), :]))
        copies.append((piece.at[pl.ds(96, 160), :], wq_o.at[rows_of(j, 160), :]))
        for c in range(5):
            copies.append((piece.at[pl.ds(256 + 32 * c, 32), :], lat.at[rows_of(j, 32), pl.ds(256 * c, 256)]))
    wait_all(run_copies(copies, sem))
    zhat, _ = ln_parts(lat[...].astype(F32))
    zn_o[...] = (zhat * qg[...][None, :]).astype(BF)
    q_o[...] = dot(zn_o[...], wq_o[...], 1, 0).astype(BF)
    k_o[...] = dot(xn[...], wk_o[...], 1, 0).astype(BF)


def scores_kernel(prefix, k, q, e_o, ll_o):
    me, _ = me_z()
    lanes = lax.broadcasted_iota(jnp.int32, (256, 256), 1) // 32
    pos = lax.broadcasted_iota(jnp.int32, (256, 512), 1) + me * 512
    own = STRIDE * (lax.broadcasted_iota(jnp.int32, (256, 1), 0) + 1)
    lane = lax.broadcasted_iota(jnp.int32, (256, 128), 1)
    ll_o[...] = jnp.zeros_like(ll_o)
    for s in range(2):
        seen = jnp.maximum(own, prefix[s])

        def head(h, carry, s=s, seen=seen):
            qh = jnp.where(lanes == h, q[...], jnp.zeros((), BF))
            scores = dot(qh, k[512 * s : 512 * (s + 1), :], 1, 1)
            e = jnp.where(pos < seen, jnp.exp2(scores * (LOG2E * 32 ** (-0.5))), 0.0)
            ll_o[s] += jnp.where(lane == h, jnp.sum(e, axis=-1, keepdims=True), 0.0)
            e_o[s, h] = e.astype(BF)
            return carry

        lax.fori_loop(0, H, head, 0, unroll=2)


def values_kernel(xn, *rest):
    pieces, (vt_o, wv_o, sem) = rest[:N], rest[N:]
    me, _ = me_z()
    wait_all(
        run_copies(
            [
                (p.at[pl.ds(416 + 96 * c, 96), :], wv_o.at[rows_of(owner(me, rel), 96), pl.ds(256 * c, 256)])
                for p, rel in zip(pieces, WIDE)
                for c in range(5)
            ],
            sem,
        )
    )
    for c in range(5):
        cols = slice(256 * c, 256 * (c + 1))
        vt_o[cols, :] = dot(wv_o[:, cols], xn[...], 0, 1).astype(BF)


def sums_kernel(vt, e, ll, *rest):
    mine_o, theirs_o, aat, acc = rest[-4:]
    me, _ = me_z()

    def head(h, carry):
        rows = rows_of(h, 160)
        aat[rows, :] = dot(vt[rows, :], e[h], 1, 1).astype(BF)
        return carry

    lax.fori_loop(0, H, head, 0, unroll=2)
    acc[:, 0:1280] = aat[...].T
    acc[:, 1280:1408] = ll[...].astype(BF)
    for kk in range(4):
        for odd, ref in ((0, mine_o), (1, theirs_o)):
            ref[kk] = acc[rows_of(me ^ (2 * kk + odd), 32), :]


def add4_kernel(a, b, *outs):
    for kk in range(4):
        outs[kk][...] = (a[kk].astype(F32) + b[kk].astype(F32)).astype(BF)


def latent_kernel(m0, r1, r2, r3, lat, mg1, cot, *rest):
    pieces, rest = rest[:N], rest[N:]
    latents_o, agb_o, mine_o, theirs_o, dab_o, init_o = rest[:6]
    wout, wup, wdown, sem = rest[6:]
    me, zi = me_z()
    groups = []
    for g, w in enumerate((wout, wup, wdown)):
        copies = [
            (p.at[pl.ds(160 * g, 160), :], w.at[rows_of(owner(me, rel), 160), :]) for p, rel in zip(pieces, WIDE)
        ]
        groups.append(run_copies(copies, sem.at[g]))
    mg = mg1[...][None, :]
    total = (m0[...].astype(F32) + r1[...].astype(F32)) + (r2[...].astype(F32) + r3[...].astype(F32))
    aa = total[:, 0:1280]
    ll = total[:, 1280:1408]
    head = lax.broadcasted_iota(jnp.int32, (64, 1280), 1) // 160
    inv = jnp.zeros((64, 1280), F32)
    for h in range(H):
        inv = jnp.where(head == h, 1.0 / ll[:, h : h + 1], inv)
    oo = aa * inv
    ob = oo.astype(BF)
    for h in groups[0]:
        h.wait()
    start = lat[...].astype(F32)
    hh = jnp.concatenate([start, start], axis=0) + dot(ob, wout[...], 1, 0)
    hat, inverse = ln_parts(hh)
    hn = (hat * mg).astype(BF)
    for h in groups[1]:
        h.wait()
    uu = dot(hn, wup[...], 1, 0)
    cdf = 0.5 * (1.0 + lax.erf(uu * (0.5**0.5)))
    gg = (uu * cdf).astype(BF)
    slope = cdf + uu * (jnp.exp(-0.5 * uu * uu) * 0.3989422804014327)
    for h in groups[2]:
        h.wait()
    latents_o[...] = (hh + dot(gg, wdown[...], 1, 0)).astype(BF)
    du = (dot(cot[...], wdown[...], 1, 1) * slope).astype(BF)
    dhn = dot(du, wup[...], 1, 1)
    dhh = cot[...].astype(F32) + ln_back(dhn, hat, inverse, mg)
    init_o[...] = dhh[0:32] + dhh[32:64]
    dhb = dhh.astype(BF)
    dob = dot(dhb, wout[...], 1, 1).astype(BF).astype(F32)
    dab_o[:, 0:1280] = (dob * inv).astype(BF)
    prod = dob * oo
    lane = lax.broadcasted_iota(jnp.int32, (64, 128), 1)
    dlb = jnp.zeros((64, 128), F32)
    for h in range(H):
        part = jnp.sum(jnp.where(head == h, prod, 0.0), axis=-1, keepdims=True)
        dlb = jnp.where(lane == h, -part / ll[:, h : h + 1], dlb)
    dab_o[:, 1280:1408] = dlb.astype(BF)
    agb_o[0] = dhb
    agb_o[1] = du
    agb_o[2] = cot[...]
    for j in range(N):
        kk = (me >> 1) ^ (j >> 1)
        cols = slice(160 * j, 160 * (j + 1))

        @pl.when((me & 1) == (j & 1))
        def _():
            for n, v in enumerate((ob, hn, gg)):
                mine_o[kk, n] = v[:, cols]

        @pl.when((me & 1) != (j & 1))
        def _():
            for n, v in enumerate((ob, hn, gg)):
                theirs_o[kk, n] = v[:, cols]


def backward_kernel(s, k, vt, q, e, *rest):
    pieces = rest[:N]
    dkvt_o, dq_o, dabx, dabt, qt, sem = rest[-6:] if s else (*rest[N + 2 : N + 4], *rest[-4:])
    me, _ = me_z()
    handles = run_copies(
        [(p.at[pl.ds(32 * s, 32), :], dabx.at[rows_of(owner(me, rel), 32), :]) for p, rel in zip(pieces, DIRECT)], sem
    )
    if s == 0:
        for kk in range(1, 4):
            for n in range(2):
                rest[N + 3 + kk][n] = rest[N + n][kk]
    qt[...] = q[...].T
    dq_o[...] = jnp.zeros_like(dq_o)
    wait_all(handles)
    lanes = lax.broadcasted_iota(jnp.int32, (256, 256), 1) // 32
    lane = lax.broadcasted_iota(jnp.int32, (256, 128), 1)
    scale = 32 ** (-0.5)
    dabt[...] = dabx[:, 0:1280].T

    def head(h, carry):
        rows = rows_of(h, 160)
        dkvt_o[pl.ds(pl.multiple_of(256 + h * 160, 32), 160), :] = dot(dabt[rows, :], e[h], 1, 0).astype(BF)
        dlb = jnp.sum(jnp.where(lane == h, dabx[:, 1280:1408].astype(F32), 0.0), axis=-1, keepdims=True)
        dee = dot(dabt[rows, :], vt[rows, :], 0, 0) + dlb
        dss = (e[h].astype(F32) * dee).astype(BF)
        krows = rows_of(h, 32)
        dkvt_o[krows, :] = (dot(qt[krows, :], dss, 1, 0) * scale).astype(BF)
        dq_o[...] += jnp.where(lanes == h, dot(dss, k[...], 1, 0), 0.0)
        return carry

    lax.fori_loop(0, H, head, 0, unroll=2)
    dq_o[...] = dq_o[...] * scale


def weights_kernel(xn, zn, dkvt, dq0, dq1, mine_o, theirs_o, xnt, dw, dqg, dqs):
    me, _ = me_z()
    xnt[...] = xn[...].T
    dqs[...] = dq0[...] + dq1[...]
    for c in range(6):
        cols = slice(256 * c, 256 * (c + 1))
        dw[:, cols] = dot(xnt[...], dkvt[cols, :], 1, 1).astype(BF)
    dqg[...] = dot(zn[...], dqs[...].astype(BF), 0, 0).astype(BF)
    for kk in range(4):
        for odd, ref in ((0, mine_o), (1, theirs_o)):
            j = me ^ (2 * kk + odd)
            for c in range(6):
                ref[kk, 96 * c : 96 * (c + 1), :] = dw[rows_of(j, 96), 256 * c : 256 * (c + 1)]
            ref[kk, 576:736, :] = dqg[rows_of(j, 160), :]
            ref[kk, 736:768, :] = dqs[rows_of(j, 32), :].astype(BF)


def own_part(gain, me, size):
    out = gain[0:size][None, :]
    for j in range(1, N):
        out = jnp.where(me == j, gain[size * j : size * (j + 1)][None, :], out)
    return out


def sum_slots_kernel(a, b, c, d, wk, wv, wq, bg, qg, mix, *rest):
    near_o, far_o, send_o, acc = rest
    me, zi = me_z()
    total = (a[...].astype(F32) + b[...].astype(F32)) + (c[...].astype(F32) + d[...].astype(F32))
    acc[...] = total.astype(BF)
    near_o[...] = acc[rows_of(zi, 192), :]
    far_o[...] = acc[rows_of(zi ^ 2, 192), :]
    send_o[0:192, :] = acc[rows_of(zi ^ 1, 192), :]
    send_o[192:384, :] = acc[rows_of(zi ^ 3, 192), :]
    prod = total[0:96] * wk[...].astype(F32)
    for n in range(5):
        prod += total[96 * (n + 1) : 96 * (n + 2)] * wv[:, 256 * n : 256 * (n + 1)].astype(F32)
    parts = (
        (row_sums(prod) / own_part(bg[...], me, 96), 96),
        (mix[...], 160),
        (row_sums(total[576:736] * wq[...].astype(F32)) / own_part(qg[...], me, 160), 160),
    )
    padded = [v if size == 160 else jnp.concatenate([v, jnp.zeros((8, 160 - size), F32)], axis=1) for v, size in parts]
    joined = jnp.concatenate(padded + [jnp.zeros((8, 32), F32)], axis=1)
    placed = jnp.where(lax.broadcasted_iota(jnp.int32, (8, 512), 0) == me, joined, 0.0)
    send_o[384:400, :] = jnp.concatenate([placed[:, 0:256], placed[:, 256:512]], axis=0).astype(BF)


def bytes_kernel(x, bg, wk, wv, dkvt, *rest):
    out = rest[-1]
    hat, inverse = ln_parts(x[...].astype(F32))
    dxn = dot(dkvt[0:256, :], wk[...], 0, 1) + dot(dkvt[256:1536, :], wv[...], 0, 1)
    out[...] = ln_back(dxn, hat, inverse, bg[...][None, :])


def latent_grads_kernel(init, wup, mg, *rest):
    (amine, at, b1, b2, b3), rest = rest[N : N + 5], rest[:N] + rest[N + 5 :]
    rows, outs, mix_o, (xs, ys, acc, sem) = rest[:N], rest[N : N + 4], rest[N + 4], rest[N + 5 :]
    me, zi = me_z()
    copies = []
    cols = (amine.at[0], at.at[0], b1.at[0], b1.at[1], b2.at[0], b2.at[1], b3.at[0], b3.at[1])
    for k in range(N):
        copies.append((cols[k], xs.at[:, rows_of(me ^ k, 64), :]))
        copies.append((rows[k], ys.at[:, rows_of(owner(me, WIDE[k]), 64), :]))
    wait_all(run_copies(copies, sem))
    for n in range(3):
        grad = dot(xs[n], ys[n], 0, 0)
        acc[160 * n : 160 * (n + 1), :] = grad.astype(BF)
        if n == 1:
            mix_o[...] = row_sums(grad * wup[...].astype(F32)) / own_part(mg[...], me, 160)
    acc[480:512, :] = init[...].astype(BF)
    for r in range(NZ):
        outs[r][...] = acc[rows_of(zi ^ r, 128), :]


def row_sums(v):
    ones = jnp.ones((8, v.shape[1]), F32)
    return lax.dot_general(
        ones, v, (((1,), (1,)), ((), ())), precision=lax.Precision.HIGHEST, preferred_element_type=F32
    )


def finish_latent_kernel(*rest):
    pieces, (out_o, up_o, down_o, init_o, acc) = rest[:NZ], rest[NZ:]
    _, zi = me_z()
    for r in range(NZ):
        acc[rows_of(zi ^ r, 128), :] = pieces[r][...]
    out_o[...] = acc[0:160, :].astype(F32)
    up_o[...] = acc[160:320, :].astype(F32)
    down_o[...] = acc[320:480, :].astype(F32)
    init_o[...] = acc[480:512, :].astype(F32)


def finish_kernel(wq_full, lat, qg, init, *rest):
    pieces, (key_o, value_o, query_o, init_o, acc) = rest[:NZ], rest[NZ:]
    _, zi = me_z()
    for r in range(NZ):
        acc[rows_of(zi ^ r, 192), :] = pieces[r][...]
    key_o[...] = acc[0:96, :].astype(F32)
    for c in range(5):
        value_o[:, 256 * c : 256 * (c + 1)] = acc[96 * (c + 1) : 96 * (c + 2), :].astype(F32)
    query_o[...] = acc[576:736, :].astype(F32)
    dzn = dot(acc[736:768, :], wq_full[...], 1, 1)
    hat, inverse = ln_parts(lat[...].astype(F32))
    init_o[...] = init[...] + ln_back(dzn, hat, inverse, qg[...][None, :])


def norms_kernel(a, b, c, d, *outs):
    both = (a[...].astype(F32) + b[...].astype(F32)) + (c[...].astype(F32) + d[...].astype(F32))
    total = jnp.concatenate([both[0:8], both[8:16]], axis=1)
    for n, (out, size) in enumerate(zip(outs, (96, 160, 160))):
        width = out.shape[0]
        at = lax.broadcasted_iota(jnp.int32, (160, width), 1)
        pick = (at % size == lax.broadcasted_iota(jnp.int32, (160, width), 0)).astype(F32)
        wide = lax.dot_general(
            total[:, 160 * n : 160 * (n + 1)],
            pick,
            (((1,), (0,)), ((), ())),
            precision=lax.Precision.HIGHEST,
            preferred_element_type=F32,
        )
        mine = lax.broadcasted_iota(jnp.int32, (8, width), 0) == lax.broadcasted_iota(jnp.int32, (8, width), 1) // size
        out[...] = jnp.sum(jnp.where(mine, wide, 0.0), axis=0)


def plus(a, b):
    return (a.astype(F32) + b.astype(F32)).astype(BF)


def sum_of_three_kernel(a, b, c, out):
    out[...] = (a[...].astype(F32) + b[...].astype(F32) + c[...].astype(F32)).astype(BF)


def first_zq_kernel(near, far, mine, got, near_o, far_o):
    near_o[...] = plus(near[...], got[0:192, :])
    far_o[0:192, :] = plus(far[...], got[192:384, :])
    far_o[192:208, :] = plus(mine[384:400, :], got[384:400, :])


def second_zq_kernel(near, mine, got, near_o, norm_o):
    near_o[...] = plus(near[...], got[0:192, :])
    norm_o[...] = plus(mine[192:208, :], got[192:208, :])


def sums_of_pairs_kernel(*refs):
    n = len(refs) // 3
    for k in range(n):
        a, b, out = refs[2 * k], refs[2 * k + 1], refs[2 * n + k]
        out[...] = (a[...].astype(F32) + b[...].astype(F32)).astype(out.dtype)


def sums_of_pairs(pairs, name, deps=(), cost=COST):
    flat = [x for pair in pairs for x in pair]
    out = [sds(a.shape, a.dtype) for a, _ in pairs]
    return call(sums_of_pairs_kernel, out, flat, [VMEM] * len(flat), name=name, deps=deps, cost=cost)


def part(f, *args):
    def body(*refs):
        return f(*args, *refs)

    return body


def tie(*xs):
    return lax.optimization_barrier(xs)


def per_device_fast(
    byte_feats,
    latent_init,
    prefix,
    byte_gain,
    query_gain,
    mixer_gain,
    query_weight,
    key_weight,
    value_weight,
    out_weight,
    up_weight,
    down_weight,
    cotangent,
):
    seqs, rows, width = byte_feats.shape
    own = latent_init.shape[0]
    x = byte_feats.reshape(seqs * rows, width)
    cot = cotangent.reshape(seqs * own, DL)

    def first(w):
        return send_split(w, 2, 4), send_split(w, 4, 2)

    packed = call(
        pack_kernel, sds((896, 256), BF), (key_weight, query_weight, latent_init, value_weight), [VMEM] * 4, name="pack"
    )
    pa, pb = first(packed)
    wcat = call(
        pack_rows_kernel, sds((480, 1280), BF), (out_weight, up_weight, down_weight), [VMEM] * 3, name="pack_rows", deps=(packed,)
    )
    xn = call(norm_kernel, sds((1024, 768), BF), (x, byte_gain), [VMEM] * 2, name="norm", deps=(wcat,))
    pa, pb, xn, near, wcat = tie(pa, pb, xn, packed, wcat)
    wa = send_split(wcat, 2, 4)
    pd = send_split(pa, 4, 2)
    pn, pna, pnb = send(near, 1), send(pa, 1), send(pb, 1)
    pd, pn, wcat = tie(pd, pn, wcat)
    pnd = send(pd, 1)
    wb = send_split(wcat, 4, 2)
    pieces = (packed, pn, pa, pb, pd, pna, pnb, pnd)
    k, wk, wq_full, q, zn = call(
        query_kernel,
        (sds((1024, 256), BF), sds((768, 256), BF), sds((1280, 256), BF), sds((256, 256), BF), sds((256, 1280), BF)),
        (xn, query_gain, *pieces),
        [VMEM] * 2 + [ANY] * N,
        [pltpu.VMEM((256, 1280), BF), pltpu.SemaphoreType.DMA((7 * N,))],
        name="query",
    )
    q, wcat = tie(q, wcat)
    wn = send(wcat, 1)
    e, ll = call(
        scores_kernel,
        (sds((2, 8, 256, 512), BF), sds((2, 256, 128), F32)),
        (prefix, k, q),
        [SMEM, VMEM, VMEM],
        name="scores",
    )
    vt, wv = call(
        values_kernel,
        (sds((1280, 1024), BF), sds((768, 1280), BF)),
        (xn, *pieces),
        [VMEM] + [ANY] * N,
        [pltpu.SemaphoreType.DMA((5 * N,))],
        name="values",
        deps=(e, wn),
    )
    def sums(s, *prev):
        return call(
            sums_kernel,
            (sds((4, 64, 1408), BF), sds((4, 64, 1408), BF)),
            (vt, e, ll, *prev),
            [
                pl.BlockSpec((1280, 512), lambda g: (0, s)),
                pl.BlockSpec((None, 8, 256, 512), lambda g: (s, 0, 0, 0)),
                pl.BlockSpec((None, 256, 128), lambda g: (s, 0, 0)),
            ]
            + [ANY] * len(prev),
            [pltpu.VMEM((1280, 256), BF), pltpu.VMEM((256, 1408), BF)],
            out_specs=[pl.BlockSpec((4, 32, 1408), lambda g: (0, s, 0))] * 2,
            aliases={3: 0, 4: 1} if prev else {},
            name="sums",
            grid=(1,),
        )

    vt, wa, wb = tie(vt, wa, wb)
    mine, theirs = sums(0)
    wd = send_split(wa, 4, 2)
    wna, wnb = send(wa, 1), send(wb, 1)
    mine, theirs = sums(1, mine, theirs)
    got = send(theirs, 1)
    m0, m1, m2, m3 = call(
        add4_kernel, (sds((64, 1408), BF),) * 4, (mine, got), [VMEM] * 2, name="add4", deps=(wna, wnb), cost=1024
    )
    r1, r2, r3 = send(m1, 2), send(m2, 4), send(m3, 6)
    m0, wd = tie(m0, wd)
    wnd = send(wd, 1)
    latents, agb, amine, atheirs, dabx, init = call(
        latent_kernel,
        (
            sds((64, 1280), BF), sds((3, 64, 1280), BF), sds((4, 3, 64, 160), BF), sds((4, 3, 64, 160), BF),
            sds((64, 1408), BF), sds((32, 1280), F32),
        ),
        (m0, r1, r2, r3, latent_init, mixer_gain, cot, wcat, wn, wa, wb, wd, wna, wnb, wnd),
        [VMEM] * 7 + [ANY] * N,
        [pltpu.VMEM((1280, 1280), BF)] * 3 + [pltpu.SemaphoreType.DMA((3, N))],
        name="latent",
    )
    d2, d4, d6, d1 = send(dabx, 2), send(dabx, 4), send(dabx, 6), send(dabx, 1)
    at = send(atheirs, 1)
    d2, d4, d6, agb = tie(d2, d4, d6, agb)
    d3, d5, d7 = send(d2, 1), send(d4, 1), send(d6, 1)
    dab_p = [dabx, d1, d2, d3, d4, d5, d6, d7]
    ga, gb = first(agb)
    gn = send(agb, 1)

    def backward(s, *extra, deps=()):
        both = [sds((2, 3, 64, 160), BF)] * (0 if s else 3)
        return call(
            part(backward_kernel, s),
            (sds((1536, 1024), BF), sds((256, 256), F32), *both),
            (k, vt, q, e, *dab_p, *extra),
            [
                pl.BlockSpec((512, 256), lambda g: (s, 0)),
                pl.BlockSpec((1280, 512), lambda g: (0, s)),
                VMEM,
                pl.BlockSpec((None, 8, 256, 512), lambda g: (s, 0, 0, 0)),
            ]
            + [ANY] * N + [ANY if s else VMEM] * len(extra),
            [
                pltpu.VMEM((256, 1408), BF), pltpu.VMEM((1280, 256), BF), pltpu.VMEM((256, 256), BF),
                pltpu.SemaphoreType.DMA((N,)),
            ],
            out_specs=(pl.BlockSpec((1536, 512), lambda g: (0, s)), VMEM, *[VMEM] * len(both)),
            aliases={4 + N: 0} if s else {},
            name="backward",
            grid=(1,),
            deps=deps,
            cost=1024 if s else COST,
        )

    dkvt, dq0, *both = backward(0, amine, at)
    dq0, ga, gb, gn = tie(dq0, ga, gb, gn)
    gd = send_split(ga, 4, 2)
    gna = send(ga, 1)
    both_s = [send(b, 2 * kk + 2) for kk, b in enumerate(both)]
    dkvt, dq1 = backward(1, dkvt, deps=(dq0,))
    dq1, gd, gna, gb = tie(dq1, gd, gna, gb)
    gnb, gnd = send(gb, 1), send(gd, 1)
    gmine, gtheirs = call(
        weights_kernel,
        (sds((4, 768, 256), BF), sds((4, 768, 256), BF)),
        (xn, zn, dkvt, dq0, dq1),
        [VMEM] * 5,
        [
            pltpu.VMEM((768, 1024), BF), pltpu.VMEM((768, 1536), BF), pltpu.VMEM((1280, 256), BF),
            pltpu.VMEM((256, 256), F32),
        ],
        name="weights",
        deps=(),
    )
    gg = send(gtheirs, 1)

    *oud, mix = call(
        latent_grads_kernel,
        (sds((128, 1280), BF),) * NZ + (sds((8, 160), F32),),
        (init, up_weight, mixer_gain, agb, gn, ga, gb, gd, gna, gnb, gnd, amine, at, *both_s),
        [VMEM] * 3 + [ANY] * (5 + N),
        [
            pltpu.VMEM((3, 512, 160), BF), pltpu.VMEM((3, 512, 1280), BF), pltpu.VMEM((512, 1280), BF),
            pltpu.SemaphoreType.DMA((2 * N,)),
        ],
        name="latent_grads",
        deps=(gtheirs,),
    )
    o3 = send_z(oud[3], 1)
    gm = call(add4_kernel, (sds((768, 256), BF),) * 4, (gmine, gg), [VMEM] * 2, name="add4g", deps=(oud[0],))
    g1, g2, g3 = send(gm[1], 2), send(gm[2], 4), send(gm[3], 6)
    (ofar,) = sums_of_pairs(((oud[2], o3),), "osum", deps=(gm[0],))
    ofar, o1 = tie(ofar, oud[1])
    o22, o1 = send_z(ofar, 2), send_z(o1, 1)
    byte_grads = call(
        bytes_kernel,
        sds((2, 512, 768), F32),
        (x, byte_gain, wk, wv, dkvt),
        [
            pl.BlockSpec((256, 768), lambda b: (b, 0)),
            pl.BlockSpec((768,), lambda b: (0,)),
            pl.BlockSpec((768, 256), lambda b: (0, 0)),
            pl.BlockSpec((768, 1280), lambda b: (0, 0)),
            pl.BlockSpec((1536, 256), lambda b: (0, b)),
        ],
        out_specs=pl.BlockSpec((None, 256, 768), lambda b: (b // 2, b % 2, 0)),
        name="bytes",
        grid=(4,),
        deps=(ofar,),
        cost=1024,
    )
    qnear, qfar, qsend = call(
        sum_slots_kernel,
        (sds((192, 256), BF), sds((192, 256), BF), sds((400, 256), BF)),
        (gm[0], g1, g2, g3, key_weight, value_weight, query_weight, byte_gain, query_gain, mix),
        [VMEM] * 10,
        [pltpu.VMEM((768, 256), BF)],
        name="gsum",
        deps=(byte_grads,),
    )
    qgot = send_z(qsend, 1)
    ototal = call(
        sum_of_three_kernel, sds((128, 1280), BF), (oud[0], o1, o22), [VMEM] * 3, name="ototal", lead=(qnear,)
    )
    o2 = send_z(ototal, 2)
    qnear, qfar = call(
        first_zq_kernel,
        (sds((192, 256), BF), sds((208, 256), BF)),
        (qnear, qfar, qsend, qgot),
        [VMEM] * 4,
        name="qsum",
        deps=(ototal,),
    )
    qfar, oshare = tie(qfar, ototal)
    qgot, o1 = send_z(qfar, 2), send_z(oshare, 1)
    qtotal, norm = call(
        second_zq_kernel,
        (sds((192, 256), BF), sds((16, 256), BF)),
        (qnear, qfar, qgot),
        [VMEM] * 3,
        name="qtotal",
        deps=(o2,),
        cost=1024,
    )
    qtotal, o2 = tie(qtotal, o2)
    q2, n3 = send_z(qtotal, 2), send(norm, 1)
    ofar2 = send_z(o2, 1)
    (norm,) = sums_of_pairs(((norm, n3),), "nsum", cost=1024)
    norm, qshare = tie(norm, qtotal)
    q1 = send_z(qshare, 1)
    n4, n5, n6 = send(norm, 2), send(norm, 4), send(norm, 6)
    q3 = send_z(q2, 1)
    out_g, up_g, down_g, init_sum = call(
        finish_latent_kernel,
        (sds((160, 1280), F32),) * 3 + (sds((32, 1280), F32),),
        (ototal, o1, o2, ofar2),
        [VMEM] * NZ,
        [pltpu.VMEM((512, 1280), BF)],
        name="finish_latent",
    )
    byte_n, mixer_n, query_n = call(
        norms_kernel,
        (sds((768,), F32), sds((1280,), F32), sds((1280,), F32)),
        (norm, n4, n5, n6),
        [VMEM] * 4,
        name="norms",
        deps=(init_sum,),
        cost=1024,
    )
    key_g, value_g, query_g, init_g = call(
        finish_kernel,
        (sds((96, 256), F32), sds((96, 1280), F32), sds((160, 256), F32), sds((32, 1280), F32)),
        (wq_full, latent_init, query_gain, init_sum, qtotal, q1, q2, q3),
        [VMEM] * (4 + NZ),
        [pltpu.VMEM((768, 256), BF)],
        name="finish",
        deps=(byte_n,),
        cost=1024,
    )
    return (
        latents.reshape(seqs, own, DL),
        byte_grads,
        init_g,
        byte_n,
        query_n,
        mixer_n,
        query_g,
        key_g,
        value_g,
        out_g,
        up_g,
        down_g,
    )


def solution(mesh):
    fast = mesh.shape["fsdp"] == 8 and mesh.shape["rep"] == 4
    device_fn = per_device_fast if fast else per_device_plain
    placed = (
        P("rep", "fsdp", None),
        P("fsdp", None),
        P("rep"),
        P(),
        P(),
        P(),
        P("fsdp", None),
        P("fsdp", None),
        P("fsdp", None),
        P("fsdp", None),
        P("fsdp", None),
        P("fsdp", None),
        P("rep", "fsdp", None),
    )
    return jax.shard_map(
        device_fn,
        mesh=mesh,
        in_specs=placed,
        out_specs=(
            P("rep", "fsdp", None),
            P("rep", "fsdp", None),
            P("fsdp", None),
            P(),
            P(),
            P(),
            P("fsdp", None),
            P("fsdp", None),
            P("fsdp", None),
            P("fsdp", None),
            P("fsdp", None),
            P("fsdp", None),
        ),
        check_vma=False,
    )
```

```python
import jax
import jax.numpy as jnp
from jax import lax
from jax.experimental import pallas as pl
from jax.experimental.pallas import tpu as pltpu
from jax.sharding import PartitionSpec as P

DL = 1280
H = 8
QK = 256
VD = 1280
STRIDE = 16


EPSILON = 1e-05


def norm_parts(values, gain):
    centered = values - jnp.mean(values, axis=-1, keepdims=True)
    variance = jnp.mean(centered * centered, axis=-1, keepdims=True)
    inverse = lax.rsqrt(variance + EPSILON)
    normal = centered * inverse
    return (normal * gain, normal, inverse)


def norm_back(grad_out, normal, inverse, gain):
    scaled = grad_out * gain
    mean_one = jnp.mean(scaled, axis=-1, keepdims=True)
    mean_two = jnp.mean(scaled * normal, axis=-1, keepdims=True)
    return inverse * (scaled - mean_one - normal * mean_two)


def per_device_plain(
    byte_feats,
    latent_init,
    prefix,
    byte_gain,
    query_gain,
    mixer_gain,
    query_weight,
    key_weight,
    value_weight,
    out_weight,
    up_weight,
    down_weight,
    cotangent,
):
    shard_count = lax.axis_size("fsdp")
    shard_index = lax.axis_index("fsdp")
    seq_count, seq_rows, byte_width = byte_feats.shape
    own_latents = latent_init.shape[0]
    latent_count = own_latents * shard_count
    head_qk = QK // H
    head_value = VD // H
    scale = head_qk ** (-0.5)
    row_count = seq_count * own_latents
    latent_all, query_full, key_full, value_full = (
        lax.all_gather(latent_init, "fsdp", axis=0, tiled=True),
        lax.all_gather(query_weight, "fsdp", axis=0, tiled=True),
        lax.all_gather(key_weight, "fsdp", axis=0, tiled=True),
        lax.all_gather(value_weight, "fsdp", axis=0, tiled=True),
    )
    out_full, up_full, down_full = (
        lax.all_gather(out_weight, "fsdp", axis=0, tiled=True),
        lax.all_gather(up_weight, "fsdp", axis=0, tiled=True),
        lax.all_gather(down_weight, "fsdp", axis=0, tiled=True),
    )
    byte_flat = byte_feats.astype(jnp.float32).reshape(seq_count * seq_rows, byte_width)
    byte_normed, byte_hat, byte_inv = norm_parts(byte_flat, byte_gain)
    byte_low = byte_normed.astype(jnp.bfloat16)
    keys_low = (
        jnp.dot(byte_low, key_full, preferred_element_type=jnp.float32)
        .astype(jnp.bfloat16)
        .reshape(seq_count, seq_rows, H, head_qk)
    )
    values_low = (
        jnp.dot(byte_low, value_full, preferred_element_type=jnp.float32)
        .astype(jnp.bfloat16)
        .reshape(seq_count, seq_rows, H, head_value)
    )
    latent_normed, latent_hat, latent_inv = norm_parts(latent_all.astype(jnp.float32), query_gain)
    latent_low = latent_normed.astype(jnp.bfloat16)
    query_low = (
        jnp.dot(latent_low, query_full, preferred_element_type=jnp.float32)
        .astype(jnp.bfloat16)
        .reshape(latent_count, H, head_qk)
    )
    byte_pos = shard_index * seq_rows + jnp.arange(seq_rows, dtype=jnp.int32)
    latent_pos = jnp.arange(latent_count, dtype=jnp.int32)

    def exp_scores(keys_seq, limit):
        scores = scale * jnp.einsum(
            "jhd,ihd->hji", query_low, keys_seq, preferred_element_type=jnp.float32
        )
        visible = (byte_pos[None, :] < limit) | (
            byte_pos[None, :] < STRIDE * (latent_pos[:, None] + 1)
        )
        return jnp.where(visible[None], jnp.exp(scores), 0.0)

    def forward_step(carry, inputs):
        keys_seq, values_seq, limit = inputs
        weights = exp_scores(keys_seq, limit)
        totals = jnp.transpose(jnp.sum(weights, axis=-1))
        summed = jnp.einsum(
            "hji,ihv->jhv",
            weights.astype(jnp.bfloat16),
            values_seq,
            preferred_element_type=jnp.float32,
        ).reshape(latent_count, VD)
        own_sum, own_total = (
            lax.psum_scatter(summed, "fsdp", scatter_dimension=0, tiled=True),
            lax.psum_scatter(totals, "fsdp", scatter_dimension=0, tiled=True),
        )
        return (carry, (own_sum, own_total))

    _, (sums_own, totals_own) = lax.scan(
        forward_step, jnp.zeros((), jnp.float32), (keys_low, values_low, prefix)
    )
    attended = sums_own.reshape(seq_count, own_latents, H, head_value) / totals_own[..., None]
    attn_low = attended.reshape(row_count, VD).astype(jnp.bfloat16)
    mixed = jnp.dot(attn_low, out_full, preferred_element_type=jnp.float32).reshape(
        seq_count, own_latents, DL
    )
    hidden = (mixed + latent_init.astype(jnp.float32)[None]).reshape(row_count, DL)
    mixer_normed, mixer_hat, mixer_inv = norm_parts(hidden, mixer_gain)
    mixer_low = mixer_normed.astype(jnp.bfloat16)
    pre_act = jnp.dot(mixer_low, up_full, preferred_element_type=jnp.float32)
    activated, gelu_back = jax.vjp(lambda value: jax.nn.gelu(value, approximate=False), pre_act)
    act_low = activated.astype(jnp.bfloat16)
    output = hidden + jnp.dot(act_low, down_full, preferred_element_type=jnp.float32)
    latents = output.reshape(seq_count, own_latents, DL).astype(jnp.bfloat16)
    cot_low = cotangent.reshape(row_count, DL)
    down_local = jnp.einsum("rf,rd->fd", act_low, cot_low, preferred_element_type=jnp.float32)
    act_grad = jnp.einsum("rd,fd->rf", cot_low, down_full, preferred_element_type=jnp.float32)
    pre_grad = gelu_back(act_grad)[0].astype(jnp.bfloat16)
    up_local = jnp.einsum("rd,rf->df", mixer_low, pre_grad, preferred_element_type=jnp.float32)
    mixer_grad = jnp.einsum("rf,df->rd", pre_grad, up_full, preferred_element_type=jnp.float32)
    mixer_part = jnp.sum(mixer_grad * mixer_hat, axis=0)
    hidden_grad = cot_low.astype(jnp.float32) + norm_back(
        mixer_grad, mixer_hat, mixer_inv, mixer_gain
    )
    hidden_low = hidden_grad.astype(jnp.bfloat16)
    out_local = jnp.einsum("rv,rd->vd", attn_low, hidden_low, preferred_element_type=jnp.float32)
    attn_grad = jnp.einsum(
        "rd,vd->rv", hidden_low, out_full, preferred_element_type=jnp.float32
    ).astype(jnp.bfloat16)
    attn_heads = attn_grad.astype(jnp.float32).reshape(seq_count, own_latents, H, head_value)
    sum_grad = (
        (attn_heads / totals_own[..., None])
        .astype(jnp.bfloat16)
        .reshape(seq_count, own_latents, VD)
    )
    total_grad = (-jnp.sum(attn_heads * attended, axis=-1) / totals_own).astype(jnp.bfloat16)
    init_rows = jnp.sum(hidden_grad.reshape(seq_count, own_latents, DL), axis=0)

    def backward_step(carry, inputs):
        keys_seq, values_seq, limit, sum_own, total_own = inputs
        sum_all, total_all = (
            lax.all_gather(sum_own, "fsdp", axis=0, tiled=True),
            lax.all_gather(total_own, "fsdp", axis=0, tiled=True),
        )
        weights = exp_scores(keys_seq, limit)
        sum_heads = sum_all.reshape(latent_count, H, head_value)
        values_grad = jnp.einsum(
            "hji,jhv->ihv",
            weights.astype(jnp.bfloat16),
            sum_heads,
            preferred_element_type=jnp.float32,
        ).astype(jnp.bfloat16)
        weights_grad = (
            jnp.einsum("jhv,ihv->hji", sum_heads, values_seq, preferred_element_type=jnp.float32)
            + jnp.transpose(total_all.astype(jnp.float32))[:, :, None]
        )
        score_grad = (weights * weights_grad).astype(jnp.bfloat16)
        query_part = scale * jnp.einsum(
            "hji,ihd->jhd", score_grad, keys_seq, preferred_element_type=jnp.float32
        )
        keys_grad = (
            scale
            * jnp.einsum("hji,jhd->ihd", score_grad, query_low, preferred_element_type=jnp.float32)
        ).astype(jnp.bfloat16)
        query_own = lax.psum_scatter(
            query_part.reshape(latent_count, QK), "fsdp", scatter_dimension=0, tiled=True
        )
        return (carry, (keys_grad, values_grad, query_own))

    _, (keys_grad, values_grad, query_own) = lax.scan(
        backward_step,
        jnp.zeros((), jnp.float32),
        (keys_low, values_low, prefix, sum_grad, total_grad),
    )
    keys_flat = keys_grad.reshape(seq_count * seq_rows, QK)
    values_flat = values_grad.reshape(seq_count * seq_rows, VD)
    key_local = jnp.einsum("rb,rq->bq", byte_low, keys_flat, preferred_element_type=jnp.float32)
    value_local = jnp.einsum("rb,rv->bv", byte_low, values_flat, preferred_element_type=jnp.float32)
    normed_grad = jnp.einsum(
        "rq,bq->rb", keys_flat, key_full, preferred_element_type=jnp.float32
    ) + jnp.einsum("rv,bv->rb", values_flat, value_full, preferred_element_type=jnp.float32)
    byte_part = jnp.sum(normed_grad * byte_hat, axis=0)
    byte_grads = norm_back(normed_grad, byte_hat, byte_inv, byte_gain).reshape(
        seq_count, seq_rows, byte_width
    )
    query_grad_low = query_own.astype(jnp.bfloat16)
    own_low = lax.dynamic_slice_in_dim(latent_low, shard_index * own_latents, own_latents, 0)
    own_hat = lax.dynamic_slice_in_dim(latent_hat, shard_index * own_latents, own_latents, 0)
    own_inv = lax.dynamic_slice_in_dim(latent_inv, shard_index * own_latents, own_latents, 0)
    query_local = jnp.einsum(
        "ld,slq->dq", own_low, query_grad_low, preferred_element_type=jnp.float32
    )
    latent_grad = jnp.einsum(
        "slq,dq->ld", query_grad_low, query_full, preferred_element_type=jnp.float32
    )
    query_part_gain = jnp.sum(latent_grad * own_hat, axis=0)
    init_local = init_rows + norm_back(latent_grad, own_hat, own_inv, query_gain)
    byte_norm, query_norm, mixer_norm = lax.psum(
        (byte_part, query_part_gain, mixer_part), ("rep", "fsdp")
    )
    group_parts = (
        lax.psum_scatter(query_local, "fsdp", scatter_dimension=0, tiled=True),
        lax.psum_scatter(key_local, "fsdp", scatter_dimension=0, tiled=True),
        lax.psum_scatter(value_local, "fsdp", scatter_dimension=0, tiled=True),
        lax.psum_scatter(out_local, "fsdp", scatter_dimension=0, tiled=True),
        lax.psum_scatter(up_local, "fsdp", scatter_dimension=0, tiled=True),
        lax.psum_scatter(down_local, "fsdp", scatter_dimension=0, tiled=True),
    )
    query_grads, key_grads, value_grads, out_grads, up_grads, down_grads, init_grads = lax.psum(
        (
            group_parts[0],
            group_parts[1],
            group_parts[2],
            group_parts[3],
            group_parts[4],
            group_parts[5],
            init_local,
        ),
        "rep",
    )
    return (
        latents,
        byte_grads,
        init_grads,
        byte_norm,
        query_norm,
        mixer_norm,
        query_grads,
        key_grads,
        value_grads,
        out_grads,
        up_grads,
        down_grads,
    )


BF = jnp.bfloat16
F32 = jnp.float32
N = 8
NZ = 4
COST = 100_000_000_000
LOG2E = 1.4426950408889634
ANY = pl.BlockSpec(memory_space=pl.ANY)
VMEM = pl.BlockSpec(memory_space=pltpu.VMEM)
SMEM = pl.BlockSpec(memory_space=pltpu.SMEM)


def dot(a, b, ca, cb):
    return lax.dot_general(a, b, (((ca,), (cb,)), ((), ())), preferred_element_type=F32)


def send(x, k):
    return lax.ppermute(x, "fsdp", [(i, i ^ k) for i in range(N)])


def send_split(x, even, odd):
    return lax.ppermute(x, "fsdp", [(i, i ^ (odd if i & 1 else even)) for i in range(N)])


def send_z(x, k):
    return lax.ppermute(x, "rep", [(i, i ^ k) for i in range(NZ)])


def after(x, *deps):
    return lax.optimization_barrier((x, *deps))[0]


def me_z():
    return lax.axis_index("fsdp"), lax.axis_index("rep")


def owner(me, rel):
    even, odd = rel
    if even == odd:
        return me ^ even
    return me ^ jnp.where((me & 1) == 0, even, odd)


def call(body, out, ins, specs, scratch=(), name=None, grid=(), deps=(), out_specs=None, aliases=None, cost=COST, lead=()):
    n, skip, ahead = len(ins), len(deps), len(lead)

    def run(*refs):
        return body(*refs[ahead : ahead + n], *refs[ahead + n + skip :])

    return pl.pallas_call(
        run,
        grid=grid,
        out_shape=out,
        in_specs=[ANY] * ahead + list(specs) + [ANY] * skip,
        out_specs=jax.tree.map(lambda _: VMEM, out) if out_specs is None else out_specs,
        scratch_shapes=list(scratch),
        input_output_aliases=aliases or {},
        name=name,
        cost_estimate=pl.CostEstimate(flops=cost, bytes_accessed=1024, transcendentals=0),
    )(*lead, *ins, *deps)


def sds(shape, dtype):
    return jax.ShapeDtypeStruct(shape, dtype)


def ln_parts(v):
    centered = v - jnp.mean(v, axis=-1, keepdims=True)
    inverse = lax.rsqrt(jnp.mean(centered * centered, axis=-1, keepdims=True) + EPSILON)
    return centered * inverse, inverse


def ln_back(grad, hat, inverse, gain):
    scaled = grad * gain
    return inverse * (
        scaled
        - jnp.mean(scaled, axis=-1, keepdims=True)
        - hat * jnp.mean(scaled * hat, axis=-1, keepdims=True)
    )


WIDE = ((0, 0), (1, 1), (2, 4), (4, 2), (6, 6), (5, 3), (3, 5), (7, 7))
DIRECT = tuple((k, k) for k in range(N))


def pack_kernel(wk, wq, lat, wv, out):
    rows = wk.shape[0]
    out[0:rows, :] = wk[...]
    at = rows
    out[at : at + wq.shape[0], :] = wq[...]
    at += wq.shape[0]
    for c in range(5):
        out[at : at + lat.shape[0], :] = lat[:, 256 * c : 256 * (c + 1)]
        at += lat.shape[0]
    for c in range(5):
        out[at : at + wv.shape[0], :] = wv[:, 256 * c : 256 * (c + 1)]
        at += wv.shape[0]


def pack_rows_kernel(a, b, c, out):
    rows = a.shape[0]
    for n, ref in enumerate((a, b, c)):
        out[rows * n : rows * (n + 1), :] = ref[...]


def rows_of(j, size):
    return pl.ds(pl.multiple_of(j * size, size & -size), size)


def run_copies(copies, sem):
    handles = [pltpu.make_async_copy(a, b, sem.at[n]) for n, (a, b) in enumerate(copies)]
    for h in handles:
        h.start()
    return handles


def wait_all(handles):
    for h in handles:
        h.wait()


def norm_kernel(x, bg, xn_o):
    hat, _ = ln_parts(x[...].astype(F32))
    xn_o[...] = (hat * bg[...][None, :]).astype(BF)


def query_kernel(xn, qg, *rest):
    pieces, (k_o, wk_o, wq_o, q_o, zn_o, lat, sem) = rest[:N], rest[N:]
    me, _ = me_z()
    copies = []
    for piece, rel in zip(pieces, WIDE):
        j = owner(me, rel)
        copies.append((piece.at[pl.ds(0, 96), :], wk_o.at[rows_of(j, 96), :]))
        copies.append((piece.at[pl.ds(96, 160), :], wq_o.at[rows_of(j, 160), :]))
        for c in range(5):
            copies.append((piece.at[pl.ds(256 + 32 * c, 32), :], lat.at[rows_of(j, 32), pl.ds(256 * c, 256)]))
    wait_all(run_copies(copies, sem))
    zhat, _ = ln_parts(lat[...].astype(F32))
    zn_o[...] = (zhat * qg[...][None, :]).astype(BF)
    q_o[...] = dot(zn_o[...], wq_o[...], 1, 0).astype(BF)
    k_o[...] = dot(xn[...], wk_o[...], 1, 0).astype(BF)


def scores_kernel(prefix, k, q, e_o, ll_o):
    me, _ = me_z()
    lanes = lax.broadcasted_iota(jnp.int32, (256, 256), 1) // 32
    pos = lax.broadcasted_iota(jnp.int32, (256, 512), 1) + me * 512
    own = STRIDE * (lax.broadcasted_iota(jnp.int32, (256, 1), 0) + 1)
    lane = lax.broadcasted_iota(jnp.int32, (256, 128), 1)
    ll_o[...] = jnp.zeros_like(ll_o)
    for s in range(2):
        seen = jnp.maximum(own, prefix[s])

        def head(h, carry, s=s, seen=seen):
            qh = jnp.where(lanes == h, q[...], jnp.zeros((), BF))
            scores = dot(qh, k[512 * s : 512 * (s + 1), :], 1, 1)
            e = jnp.where(pos < seen, jnp.exp2(scores * (LOG2E * 32 ** (-0.5))), 0.0)
            ll_o[s] += jnp.where(lane == h, jnp.sum(e, axis=-1, keepdims=True), 0.0)
            e_o[s, h] = e.astype(BF)
            return carry

        lax.fori_loop(0, H, head, 0, unroll=2)


def values_kernel(xn, *rest):
    pieces, (vt_o, wv_o, sem) = rest[:N], rest[N:]
    me, _ = me_z()
    wait_all(
        run_copies(
            [
                (p.at[pl.ds(416 + 96 * c, 96), :], wv_o.at[rows_of(owner(me, rel), 96), pl.ds(256 * c, 256)])
                for p, rel in zip(pieces, WIDE)
                for c in range(5)
            ],
            sem,
        )
    )
    for c in range(5):
        cols = slice(256 * c, 256 * (c + 1))
        vt_o[cols, :] = dot(wv_o[:, cols], xn[...], 0, 1).astype(BF)


def sums_kernel(vt, e, ll, *rest):
    mine_o, theirs_o, aat, acc = rest[-4:]
    me, _ = me_z()

    def head(h, carry):
        rows = rows_of(h, 160)
        aat[rows, :] = dot(vt[rows, :], e[h], 1, 1).astype(BF)
        return carry

    lax.fori_loop(0, H, head, 0, unroll=2)
    acc[:, 0:1280] = aat[...].T
    acc[:, 1280:1408] = ll[...].astype(BF)
    for kk in range(4):
        for odd, ref in ((0, mine_o), (1, theirs_o)):
            ref[kk] = acc[rows_of(me ^ (2 * kk + odd), 32), :]


def add4_kernel(a, b, *outs):
    for kk in range(4):
        outs[kk][...] = (a[kk].astype(F32) + b[kk].astype(F32)).astype(BF)


def latent_kernel(m0, r1, r2, r3, lat, mg1, cot, *rest):
    pieces, rest = rest[:N], rest[N:]
    latents_o, agb_o, mine_o, theirs_o, dab_o, init_o = rest[:6]
    wout, wup, wdown, sem = rest[6:]
    me, zi = me_z()
    groups = []
    for g, w in enumerate((wout, wup, wdown)):
        copies = [
            (p.at[pl.ds(160 * g, 160), :], w.at[rows_of(owner(me, rel), 160), :]) for p, rel in zip(pieces, WIDE)
        ]
        groups.append(run_copies(copies, sem.at[g]))
    mg = mg1[...][None, :]
    total = (m0[...].astype(F32) + r1[...].astype(F32)) + (r2[...].astype(F32) + r3[...].astype(F32))
    aa = total[:, 0:1280]
    ll = total[:, 1280:1408]
    head = lax.broadcasted_iota(jnp.int32, (64, 1280), 1) // 160
    inv = jnp.zeros((64, 1280), F32)
    for h in range(H):
        inv = jnp.where(head == h, 1.0 / ll[:, h : h + 1], inv)
    oo = aa * inv
    ob = oo.astype(BF)
    for h in groups[0]:
        h.wait()
    start = lat[...].astype(F32)
    hh = jnp.concatenate([start, start], axis=0) + dot(ob, wout[...], 1, 0)
    hat, inverse = ln_parts(hh)
    hn = (hat * mg).astype(BF)
    for h in groups[1]:
        h.wait()
    uu = dot(hn, wup[...], 1, 0)
    cdf = 0.5 * (1.0 + lax.erf(uu * (0.5**0.5)))
    gg = (uu * cdf).astype(BF)
    slope = cdf + uu * (jnp.exp(-0.5 * uu * uu) * 0.3989422804014327)
    for h in groups[2]:
        h.wait()
    latents_o[...] = (hh + dot(gg, wdown[...], 1, 0)).astype(BF)
    du = (dot(cot[...], wdown[...], 1, 1) * slope).astype(BF)
    dhn = dot(du, wup[...], 1, 1)
    dhh = cot[...].astype(F32) + ln_back(dhn, hat, inverse, mg)
    init_o[...] = dhh[0:32] + dhh[32:64]
    dhb = dhh.astype(BF)
    dob = dot(dhb, wout[...], 1, 1).astype(BF).astype(F32)
    dab_o[:, 0:1280] = (dob * inv).astype(BF)
    prod = dob * oo
    lane = lax.broadcasted_iota(jnp.int32, (64, 128), 1)
    dlb = jnp.zeros((64, 128), F32)
    for h in range(H):
        part = jnp.sum(jnp.where(head == h, prod, 0.0), axis=-1, keepdims=True)
        dlb = jnp.where(lane == h, -part / ll[:, h : h + 1], dlb)
    dab_o[:, 1280:1408] = dlb.astype(BF)
    agb_o[0] = dhb
    agb_o[1] = du
    agb_o[2] = cot[...]
    for j in range(N):
        kk = (me >> 1) ^ (j >> 1)
        cols = slice(160 * j, 160 * (j + 1))

        @pl.when((me & 1) == (j & 1))
        def _():
            for n, v in enumerate((ob, hn, gg)):
                mine_o[kk, n] = v[:, cols]

        @pl.when((me & 1) != (j & 1))
        def _():
            for n, v in enumerate((ob, hn, gg)):
                theirs_o[kk, n] = v[:, cols]


def backward_kernel(s, k, vt, q, e, *rest):
    pieces = rest[:N]
    dkvt_o, dq_o, dabx, dabt, qt, sem = rest[-6:] if s else (*rest[N + 2 : N + 4], *rest[-4:])
    me, _ = me_z()
    handles = run_copies(
        [(p.at[pl.ds(32 * s, 32), :], dabx.at[rows_of(owner(me, rel), 32), :]) for p, rel in zip(pieces, DIRECT)], sem
    )
    if s == 0:
        for kk in range(1, 4):
            for n in range(2):
                rest[N + 3 + kk][n] = rest[N + n][kk]
    qt[...] = q[...].T
    dq_o[...] = jnp.zeros_like(dq_o)
    wait_all(handles)
    lanes = lax.broadcasted_iota(jnp.int32, (256, 256), 1) // 32
    lane = lax.broadcasted_iota(jnp.int32, (256, 128), 1)
    scale = 32 ** (-0.5)
    dabt[...] = dabx[:, 0:1280].T

    def head(h, carry):
        rows = rows_of(h, 160)
        dkvt_o[pl.ds(pl.multiple_of(256 + h * 160, 32), 160), :] = dot(dabt[rows, :], e[h], 1, 0).astype(BF)
        dlb = jnp.sum(jnp.where(lane == h, dabx[:, 1280:1408].astype(F32), 0.0), axis=-1, keepdims=True)
        dee = dot(dabt[rows, :], vt[rows, :], 0, 0) + dlb
        dss = (e[h].astype(F32) * dee).astype(BF)
        krows = rows_of(h, 32)
        dkvt_o[krows, :] = (dot(qt[krows, :], dss, 1, 0) * scale).astype(BF)
        dq_o[...] += jnp.where(lanes == h, dot(dss, k[...], 1, 0), 0.0)
        return carry

    lax.fori_loop(0, H, head, 0, unroll=2)
    dq_o[...] = dq_o[...] * scale


def weights_kernel(xn, zn, dkvt, dq0, dq1, mine_o, theirs_o, xnt, dw, dqg, dqs):
    me, _ = me_z()
    xnt[...] = xn[...].T
    dqs[...] = dq0[...] + dq1[...]
    for c in range(6):
        cols = slice(256 * c, 256 * (c + 1))
        dw[:, cols] = dot(xnt[...], dkvt[cols, :], 1, 1).astype(BF)
    dqg[...] = dot(zn[...], dqs[...].astype(BF), 0, 0).astype(BF)
    for kk in range(4):
        for odd, ref in ((0, mine_o), (1, theirs_o)):
            j = me ^ (2 * kk + odd)
            for c in range(6):
                ref[kk, 96 * c : 96 * (c + 1), :] = dw[rows_of(j, 96), 256 * c : 256 * (c + 1)]
            ref[kk, 576:736, :] = dqg[rows_of(j, 160), :]
            ref[kk, 736:768, :] = dqs[rows_of(j, 32), :].astype(BF)


def own_part(gain, me, size):
    out = gain[0:size][None, :]
    for j in range(1, N):
        out = jnp.where(me == j, gain[size * j : size * (j + 1)][None, :], out)
    return out


def sum_slots_kernel(a, b, c, d, wk, wv, wq, bg, qg, mix, *rest):
    near_o, far_o, send_o, norm_o, acc = rest
    me, zi = me_z()
    total = (a[...].astype(F32) + b[...].astype(F32)) + (c[...].astype(F32) + d[...].astype(F32))
    acc[...] = total.astype(BF)
    near_o[...] = acc[rows_of(zi, 192), :]
    far_o[...] = acc[rows_of(zi ^ 2, 192), :]
    send_o[0:192, :] = acc[rows_of(zi ^ 1, 192), :]
    send_o[192:384, :] = acc[rows_of(zi ^ 3, 192), :]
    prod = total[0:96] * wk[...].astype(F32)
    for n in range(5):
        prod += total[96 * (n + 1) : 96 * (n + 2)] * wv[:, 256 * n : 256 * (n + 1)].astype(F32)
    parts = (
        (row_sums(prod) / own_part(bg[...], me, 96), 96),
        (mix[...], 160),
        (row_sums(total[576:736] * wq[...].astype(F32)) / own_part(qg[...], me, 160), 160),
    )
    padded = [v if size == 160 else jnp.concatenate([v, jnp.zeros((8, 160 - size), F32)], axis=1) for v, size in parts]
    joined = jnp.concatenate(padded + [jnp.zeros((8, 32), F32)], axis=1)
    placed = jnp.where(lax.broadcasted_iota(jnp.int32, (8, 512), 0) == me, joined, 0.0)
    norm_o[...] = jnp.concatenate([placed[:, 0:256], placed[:, 256:512]], axis=0).astype(BF)


def bytes_kernel(x, bg, wk, wv, dkvt, *rest):
    out = rest[-1]
    hat, inverse = ln_parts(x[...].astype(F32))
    dxn = dot(dkvt[0:256, :], wk[...], 0, 1) + dot(dkvt[256:1536, :], wv[...], 0, 1)
    out[...] = ln_back(dxn, hat, inverse, bg[...][None, :])


def latent_grads_kernel(init, wup, mg, *rest):
    (amine, at, b1, b2, b3), rest = rest[N : N + 5], rest[:N] + rest[N + 5 :]
    rows, outs, mix_o, (xs, ys, acc, sem) = rest[:N], rest[N : N + 4], rest[N + 4], rest[N + 5 :]
    me, zi = me_z()
    copies = []
    cols = (amine.at[0], at.at[0], b1.at[0], b1.at[1], b2.at[0], b2.at[1], b3.at[0], b3.at[1])
    for k in range(N):
        copies.append((cols[k], xs.at[:, rows_of(me ^ k, 64), :]))
        copies.append((rows[k], ys.at[:, rows_of(owner(me, WIDE[k]), 64), :]))
    wait_all(run_copies(copies, sem))
    for n in range(3):
        grad = dot(xs[n], ys[n], 0, 0)
        acc[160 * n : 160 * (n + 1), :] = grad.astype(BF)
        if n == 1:
            mix_o[...] = row_sums(grad * wup[...].astype(F32)) / own_part(mg[...], me, 160)
    acc[480:512, :] = init[...].astype(BF)
    for r in range(NZ):
        outs[r][...] = acc[rows_of(zi ^ r, 128), :]


def row_sums(v):
    ones = jnp.ones((8, v.shape[1]), F32)
    return lax.dot_general(
        ones, v, (((1,), (1,)), ((), ())), precision=lax.Precision.HIGHEST, preferred_element_type=F32
    )


def finish_latent_kernel(*rest):
    pieces, (out_o, up_o, down_o, init_o, acc) = rest[:NZ], rest[NZ:]
    _, zi = me_z()
    for r in range(NZ):
        acc[rows_of(zi ^ r, 128), :] = pieces[r][...]
    out_o[...] = acc[0:160, :].astype(F32)
    up_o[...] = acc[160:320, :].astype(F32)
    down_o[...] = acc[320:480, :].astype(F32)
    init_o[...] = acc[480:512, :].astype(F32)


def finish_norms(both, outs):
    total = jnp.concatenate([both[0:8], both[8:16]], axis=1)
    for n, (out, size) in enumerate(zip(outs, (96, 160, 160))):
        width = out.shape[0]
        at = lax.broadcasted_iota(jnp.int32, (160, width), 1)
        pick = (at % size == lax.broadcasted_iota(jnp.int32, (160, width), 0)).astype(F32)
        wide = lax.dot_general(
            total[:, 160 * n : 160 * (n + 1)],
            pick,
            (((1,), (0,)), ((), ())),
            precision=lax.Precision.HIGHEST,
            preferred_element_type=F32,
        )
        mine = lax.broadcasted_iota(jnp.int32, (8, width), 0) == lax.broadcasted_iota(jnp.int32, (8, width), 1) // size
        out[...] = jnp.sum(jnp.where(mine, wide, 0.0), axis=0)


def plus(a, b):
    return (a.astype(F32) + b.astype(F32)).astype(BF)


def finish_kernel(wq_full, lat, qg, init, *rest):
    pieces, (key_o, value_o, query_o, init_o), outs, acc = rest[:NZ], rest[NZ : NZ + 4], rest[NZ + 4 : NZ + 7], rest[-1]
    _, zi = me_z()
    for r in range(NZ):
        acc[rows_of(zi ^ r, 192), :] = pieces[r][0:192, :]
    a, b, c, d = [p[192:208, :].astype(F32) for p in pieces]
    finish_norms((a + b) + (c + d), outs)
    key_o[...] = acc[0:96, :].astype(F32)
    for c in range(5):
        value_o[:, 256 * c : 256 * (c + 1)] = acc[96 * (c + 1) : 96 * (c + 2), :].astype(F32)
    query_o[...] = acc[576:736, :].astype(F32)
    dzn = dot(acc[736:768, :], wq_full[...], 1, 1)
    hat, inverse = ln_parts(lat[...].astype(F32))
    init_o[...] = init[...] + ln_back(dzn, hat, inverse, qg[...][None, :])


def sum_of_three_kernel(a, b, c, out):
    out[...] = (a[...].astype(F32) + b[...].astype(F32) + c[...].astype(F32)).astype(BF)


def first_zq_kernel(near, far, got, near_o, far_o):
    near_o[...] = plus(near[...], got[0:192, :])
    far_o[...] = plus(far[...], got[192:384, :])


def second_zq_kernel(near, got, a, b, out):
    out[0:192, :] = plus(near[...], got[...])
    out[192:208, :] = plus(a[...], b[...])


def sums_of_pairs_kernel(*refs):
    n = len(refs) // 3
    for k in range(n):
        a, b, out = refs[2 * k], refs[2 * k + 1], refs[2 * n + k]
        out[...] = (a[...].astype(F32) + b[...].astype(F32)).astype(out.dtype)


def sums_of_pairs(pairs, name, deps=(), cost=COST):
    flat = [x for pair in pairs for x in pair]
    out = [sds(a.shape, a.dtype) for a, _ in pairs]
    return call(sums_of_pairs_kernel, out, flat, [VMEM] * len(flat), name=name, deps=deps, cost=cost)


def part(f, *args):
    def body(*refs):
        return f(*args, *refs)

    return body


def tie(*xs):
    return lax.optimization_barrier(xs)


def per_device_fast(
    byte_feats,
    latent_init,
    prefix,
    byte_gain,
    query_gain,
    mixer_gain,
    query_weight,
    key_weight,
    value_weight,
    out_weight,
    up_weight,
    down_weight,
    cotangent,
):
    seqs, rows, width = byte_feats.shape
    own = latent_init.shape[0]
    x = byte_feats.reshape(seqs * rows, width)
    cot = cotangent.reshape(seqs * own, DL)

    def first(w):
        return send_split(w, 2, 4), send_split(w, 4, 2)

    packed = call(
        pack_kernel, sds((896, 256), BF), (key_weight, query_weight, latent_init, value_weight), [VMEM] * 4, name="pack"
    )
    pa, pb = first(packed)
    wcat = call(
        pack_rows_kernel, sds((480, 1280), BF), (out_weight, up_weight, down_weight), [VMEM] * 3, name="pack_rows", deps=(packed,)
    )
    xn = call(norm_kernel, sds((1024, 768), BF), (x, byte_gain), [VMEM] * 2, name="norm", deps=(wcat,))
    pa, pb, xn, near, wcat = tie(pa, pb, xn, packed, wcat)
    wa = send_split(wcat, 2, 4)
    pd = send_split(pa, 4, 2)
    pn, pna, pnb = send(near, 1), send(pa, 1), send(pb, 1)
    pd, pn, wcat = tie(pd, pn, wcat)
    pnd = send(pd, 1)
    wb = send_split(wcat, 4, 2)
    pieces = (packed, pn, pa, pb, pd, pna, pnb, pnd)
    k, wk, wq_full, q, zn = call(
        query_kernel,
        (sds((1024, 256), BF), sds((768, 256), BF), sds((1280, 256), BF), sds((256, 256), BF), sds((256, 1280), BF)),
        (xn, query_gain, *pieces),
        [VMEM] * 2 + [ANY] * N,
        [pltpu.VMEM((256, 1280), BF), pltpu.SemaphoreType.DMA((7 * N,))],
        name="query",
    )
    q, wcat = tie(q, wcat)
    wn = send(wcat, 1)
    e, ll = call(
        scores_kernel,
        (sds((2, 8, 256, 512), BF), sds((2, 256, 128), F32)),
        (prefix, k, q),
        [SMEM, VMEM, VMEM],
        name="scores",
    )
    vt, wv = call(
        values_kernel,
        (sds((1280, 1024), BF), sds((768, 1280), BF)),
        (xn, *pieces),
        [VMEM] + [ANY] * N,
        [pltpu.SemaphoreType.DMA((5 * N,))],
        name="values",
        deps=(e, wn),
    )
    def sums(s, *prev):
        return call(
            sums_kernel,
            (sds((4, 64, 1408), BF), sds((4, 64, 1408), BF)),
            (vt, e, ll, *prev),
            [
                pl.BlockSpec((1280, 512), lambda g: (0, s)),
                pl.BlockSpec((None, 8, 256, 512), lambda g: (s, 0, 0, 0)),
                pl.BlockSpec((None, 256, 128), lambda g: (s, 0, 0)),
            ]
            + [ANY] * len(prev),
            [pltpu.VMEM((1280, 256), BF), pltpu.VMEM((256, 1408), BF)],
            out_specs=[pl.BlockSpec((4, 32, 1408), lambda g: (0, s, 0))] * 2,
            aliases={3: 0, 4: 1} if prev else {},
            name="sums",
            grid=(1,),
        )

    vt, wa, wb = tie(vt, wa, wb)
    mine, theirs = sums(0)
    wd = send_split(wa, 4, 2)
    wna, wnb = send(wa, 1), send(wb, 1)
    mine, theirs = sums(1, mine, theirs)
    got = send(theirs, 1)
    m0, m1, m2, m3 = call(
        add4_kernel, (sds((64, 1408), BF),) * 4, (mine, got), [VMEM] * 2, name="add4", deps=(wna, wnb), cost=1024
    )
    r1, r2, r3 = send(m1, 2), send(m2, 4), send(m3, 6)
    m0, wd = tie(m0, wd)
    wnd = send(wd, 1)
    latents, agb, amine, atheirs, dabx, init = call(
        latent_kernel,
        (
            sds((64, 1280), BF), sds((3, 64, 1280), BF), sds((4, 3, 64, 160), BF), sds((4, 3, 64, 160), BF),
            sds((64, 1408), BF), sds((32, 1280), F32),
        ),
        (m0, r1, r2, r3, latent_init, mixer_gain, cot, wcat, wn, wa, wb, wd, wna, wnb, wnd),
        [VMEM] * 7 + [ANY] * N,
        [pltpu.VMEM((1280, 1280), BF)] * 3 + [pltpu.SemaphoreType.DMA((3, N))],
        name="latent",
    )
    d2, d4, d6, d1 = send(dabx, 2), send(dabx, 4), send(dabx, 6), send(dabx, 1)
    at = send(atheirs, 1)
    d2, d4, d6, agb = tie(d2, d4, d6, agb)
    d3, d5, d7 = send(d2, 1), send(d4, 1), send(d6, 1)
    dab_p = [dabx, d1, d2, d3, d4, d5, d6, d7]
    ga, gb = first(agb)
    gn = send(agb, 1)

    def backward(s, *extra, deps=()):
        both = [sds((2, 3, 64, 160), BF)] * (0 if s else 3)
        return call(
            part(backward_kernel, s),
            (sds((1536, 1024), BF), sds((256, 256), F32), *both),
            (k, vt, q, e, *dab_p, *extra),
            [
                pl.BlockSpec((512, 256), lambda g: (s, 0)),
                pl.BlockSpec((1280, 512), lambda g: (0, s)),
                VMEM,
                pl.BlockSpec((None, 8, 256, 512), lambda g: (s, 0, 0, 0)),
            ]
            + [ANY] * N + [ANY if s else VMEM] * len(extra),
            [
                pltpu.VMEM((256, 1408), BF), pltpu.VMEM((1280, 256), BF), pltpu.VMEM((256, 256), BF),
                pltpu.SemaphoreType.DMA((N,)),
            ],
            out_specs=(pl.BlockSpec((1536, 512), lambda g: (0, s)), VMEM, *[VMEM] * len(both)),
            aliases={4 + N: 0} if s else {},
            name="backward",
            grid=(1,),
            deps=deps,
            cost=1024 if s else COST,
        )

    dkvt, dq0, *both = backward(0, amine, at)
    dq0, ga, gb, gn = tie(dq0, ga, gb, gn)
    gd = send_split(ga, 4, 2)
    gna = send(ga, 1)
    both_s = [send(b, 2 * kk + 2) for kk, b in enumerate(both)]
    dkvt, dq1 = backward(1, dkvt, deps=(dq0,))
    dq1, gd, gna, gb = tie(dq1, gd, gna, gb)
    gnb, gnd = send(gb, 1), send(gd, 1)
    gmine, gtheirs = call(
        weights_kernel,
        (sds((4, 768, 256), BF), sds((4, 768, 256), BF)),
        (xn, zn, dkvt, dq0, dq1),
        [VMEM] * 5,
        [
            pltpu.VMEM((768, 1024), BF), pltpu.VMEM((768, 1536), BF), pltpu.VMEM((1280, 256), BF),
            pltpu.VMEM((256, 256), F32),
        ],
        name="weights",
        deps=(),
    )
    gg = send(gtheirs, 1)

    *oud, mix = call(
        latent_grads_kernel,
        (sds((128, 1280), BF),) * NZ + (sds((8, 160), F32),),
        (init, up_weight, mixer_gain, agb, gn, ga, gb, gd, gna, gnb, gnd, amine, at, *both_s),
        [VMEM] * 3 + [ANY] * (5 + N),
        [
            pltpu.VMEM((3, 512, 160), BF), pltpu.VMEM((3, 512, 1280), BF), pltpu.VMEM((512, 1280), BF),
            pltpu.SemaphoreType.DMA((2 * N,)),
        ],
        name="latent_grads",
        deps=(gtheirs,),
    )
    o3 = send_z(oud[3], 1)
    gm = call(add4_kernel, (sds((768, 256), BF),) * 4, (gmine, gg), [VMEM] * 2, name="add4g", deps=(oud[0],))
    g1, g2, g3 = send(gm[1], 2), send(gm[2], 4), send(gm[3], 6)
    (ofar,) = sums_of_pairs(((oud[2], o3),), "osum", deps=(gm[0],))
    ofar, o1 = tie(ofar, oud[1])
    o22, o1 = send_z(ofar, 2), send_z(o1, 1)
    byte_grads = call(
        bytes_kernel,
        sds((2, 512, 768), F32),
        (x, byte_gain, wk, wv, dkvt),
        [
            pl.BlockSpec((256, 768), lambda b: (b, 0)),
            pl.BlockSpec((768,), lambda b: (0,)),
            pl.BlockSpec((768, 256), lambda b: (0, 0)),
            pl.BlockSpec((768, 1280), lambda b: (0, 0)),
            pl.BlockSpec((1536, 256), lambda b: (0, b)),
        ],
        out_specs=pl.BlockSpec((None, 256, 768), lambda b: (b // 2, b % 2, 0)),
        name="bytes",
        grid=(4,),
        deps=(ofar,),
        cost=1024,
    )
    qnear, qfar, qsend, norm = call(
        sum_slots_kernel,
        (sds((192, 256), BF), sds((192, 256), BF), sds((384, 256), BF), sds((16, 256), BF)),
        (gm[0], g1, g2, g3, key_weight, value_weight, query_weight, byte_gain, query_gain, mix),
        [VMEM] * 10,
        [pltpu.VMEM((768, 256), BF)],
        name="gsum",
        deps=(byte_grads,),
    )
    qgot = send_z(qsend, 1)
    ototal = call(
        sum_of_three_kernel, sds((128, 1280), BF), (oud[0], o1, o22), [VMEM] * 3, name="ototal", lead=(qnear,)
    )
    o2 = send_z(ototal, 2)
    qnear, qfar = call(
        first_zq_kernel,
        (sds((192, 256), BF), sds((192, 256), BF)),
        (qnear, qfar, qgot),
        [VMEM] * 3,
        name="qsum",
        deps=(ototal,),
    )
    qfar, norm, oshare = tie(qfar, norm, ototal)
    qgot, n3, o1 = send_z(qfar, 2), send(norm, 1), send_z(oshare, 1)
    (norm,) = sums_of_pairs(((norm, n3),), "nsum", cost=1024)
    n4 = send(norm, 2)
    (norm,) = sums_of_pairs(((norm, n4),), "nsum", cost=1024)
    norm, o2 = tie(norm, o2)
    n5, ofar2 = send(norm, 4), send_z(o2, 1)
    qtotal = call(
        second_zq_kernel,
        sds((208, 256), BF),
        (qnear, qgot, norm, n5),
        [VMEM] * 4,
        name="qtotal",
        deps=(o2, o1),
    )
    q2, q1 = send_z(qtotal, 2), send_z(qtotal, 1)
    out_g, up_g, down_g, init_sum = call(
        finish_latent_kernel,
        (sds((160, 1280), F32),) * 3 + (sds((32, 1280), F32),),
        (ototal, o1, o2, ofar2),
        [VMEM] * NZ,
        [pltpu.VMEM((512, 1280), BF)],
        name="finish_latent",
        cost=1024,
    )
    q2, init_sum = tie(q2, init_sum)
    q3 = send_z(q2, 1)
    key_g, value_g, query_g, init_g, byte_n, mixer_n, query_n = call(
        finish_kernel,
        (
            sds((96, 256), F32), sds((96, 1280), F32), sds((160, 256), F32), sds((32, 1280), F32),
            sds((768,), F32), sds((1280,), F32), sds((1280,), F32),
        ),
        (wq_full, latent_init, query_gain, init_sum, qtotal, q1, q2, q3),
        [VMEM] * (4 + NZ),
        [pltpu.VMEM((768, 256), BF)],
        name="finish",
        cost=1024,
    )
    return (
        latents.reshape(seqs, own, DL),
        byte_grads,
        init_g,
        byte_n,
        query_n,
        mixer_n,
        query_g,
        key_g,
        value_g,
        out_g,
        up_g,
        down_g,
    )


def solution(mesh):
    fast = mesh.shape["fsdp"] == 8 and mesh.shape["rep"] == 4
    device_fn = per_device_fast if fast else per_device_plain
    placed = (
        P("rep", "fsdp", None),
        P("fsdp", None),
        P("rep"),
        P(),
        P(),
        P(),
        P("fsdp", None),
        P("fsdp", None),
        P("fsdp", None),
        P("fsdp", None),
        P("fsdp", None),
        P("fsdp", None),
        P("rep", "fsdp", None),
    )
    return jax.shard_map(
        device_fn,
        mesh=mesh,
        in_specs=placed,
        out_specs=(
            P("rep", "fsdp", None),
            P("rep", "fsdp", None),
            P("fsdp", None),
            P(),
            P(),
            P(),
            P("fsdp", None),
            P("fsdp", None),
            P("fsdp", None),
            P("fsdp", None),
            P("fsdp", None),
            P("fsdp", None),
        ),
        check_vma=False,
    )
```

```python
import jax
import jax.numpy as jnp
from jax import lax
from jax.experimental import pallas as pl
from jax.experimental.pallas import tpu as pltpu
from jax.sharding import PartitionSpec as P

DL = 1280
H = 8
QK = 256
VD = 1280
STRIDE = 16


EPSILON = 1e-05


def norm_parts(values, gain):
    centered = values - jnp.mean(values, axis=-1, keepdims=True)
    variance = jnp.mean(centered * centered, axis=-1, keepdims=True)
    inverse = lax.rsqrt(variance + EPSILON)
    normal = centered * inverse
    return (normal * gain, normal, inverse)


def norm_back(grad_out, normal, inverse, gain):
    scaled = grad_out * gain
    mean_one = jnp.mean(scaled, axis=-1, keepdims=True)
    mean_two = jnp.mean(scaled * normal, axis=-1, keepdims=True)
    return inverse * (scaled - mean_one - normal * mean_two)


def per_device_plain(
    byte_feats,
    latent_init,
    prefix,
    byte_gain,
    query_gain,
    mixer_gain,
    query_weight,
    key_weight,
    value_weight,
    out_weight,
    up_weight,
    down_weight,
    cotangent,
):
    shard_count = lax.axis_size("fsdp")
    shard_index = lax.axis_index("fsdp")
    seq_count, seq_rows, byte_width = byte_feats.shape
    own_latents = latent_init.shape[0]
    latent_count = own_latents * shard_count
    head_qk = QK // H
    head_value = VD // H
    scale = head_qk ** (-0.5)
    row_count = seq_count * own_latents
    latent_all, query_full, key_full, value_full = (
        lax.all_gather(latent_init, "fsdp", axis=0, tiled=True),
        lax.all_gather(query_weight, "fsdp", axis=0, tiled=True),
        lax.all_gather(key_weight, "fsdp", axis=0, tiled=True),
        lax.all_gather(value_weight, "fsdp", axis=0, tiled=True),
    )
    out_full, up_full, down_full = (
        lax.all_gather(out_weight, "fsdp", axis=0, tiled=True),
        lax.all_gather(up_weight, "fsdp", axis=0, tiled=True),
        lax.all_gather(down_weight, "fsdp", axis=0, tiled=True),
    )
    byte_flat = byte_feats.astype(jnp.float32).reshape(seq_count * seq_rows, byte_width)
    byte_normed, byte_hat, byte_inv = norm_parts(byte_flat, byte_gain)
    byte_low = byte_normed.astype(jnp.bfloat16)
    keys_low = (
        jnp.dot(byte_low, key_full, preferred_element_type=jnp.float32)
        .astype(jnp.bfloat16)
        .reshape(seq_count, seq_rows, H, head_qk)
    )
    values_low = (
        jnp.dot(byte_low, value_full, preferred_element_type=jnp.float32)
        .astype(jnp.bfloat16)
        .reshape(seq_count, seq_rows, H, head_value)
    )
    latent_normed, latent_hat, latent_inv = norm_parts(latent_all.astype(jnp.float32), query_gain)
    latent_low = latent_normed.astype(jnp.bfloat16)
    query_low = (
        jnp.dot(latent_low, query_full, preferred_element_type=jnp.float32)
        .astype(jnp.bfloat16)
        .reshape(latent_count, H, head_qk)
    )
    byte_pos = shard_index * seq_rows + jnp.arange(seq_rows, dtype=jnp.int32)
    latent_pos = jnp.arange(latent_count, dtype=jnp.int32)

    def exp_scores(keys_seq, limit):
        scores = scale * jnp.einsum(
            "jhd,ihd->hji", query_low, keys_seq, preferred_element_type=jnp.float32
        )
        visible = (byte_pos[None, :] < limit) | (
            byte_pos[None, :] < STRIDE * (latent_pos[:, None] + 1)
        )
        return jnp.where(visible[None], jnp.exp(scores), 0.0)

    def forward_step(carry, inputs):
        keys_seq, values_seq, limit = inputs
        weights = exp_scores(keys_seq, limit)
        totals = jnp.transpose(jnp.sum(weights, axis=-1))
        summed = jnp.einsum(
            "hji,ihv->jhv",
            weights.astype(jnp.bfloat16),
            values_seq,
            preferred_element_type=jnp.float32,
        ).reshape(latent_count, VD)
        own_sum, own_total = (
            lax.psum_scatter(summed, "fsdp", scatter_dimension=0, tiled=True),
            lax.psum_scatter(totals, "fsdp", scatter_dimension=0, tiled=True),
        )
        return (carry, (own_sum, own_total))

    _, (sums_own, totals_own) = lax.scan(
        forward_step, jnp.zeros((), jnp.float32), (keys_low, values_low, prefix)
    )
    attended = sums_own.reshape(seq_count, own_latents, H, head_value) / totals_own[..., None]
    attn_low = attended.reshape(row_count, VD).astype(jnp.bfloat16)
    mixed = jnp.dot(attn_low, out_full, preferred_element_type=jnp.float32).reshape(
        seq_count, own_latents, DL
    )
    hidden = (mixed + latent_init.astype(jnp.float32)[None]).reshape(row_count, DL)
    mixer_normed, mixer_hat, mixer_inv = norm_parts(hidden, mixer_gain)
    mixer_low = mixer_normed.astype(jnp.bfloat16)
    pre_act = jnp.dot(mixer_low, up_full, preferred_element_type=jnp.float32)
    activated, gelu_back = jax.vjp(lambda value: jax.nn.gelu(value, approximate=False), pre_act)
    act_low = activated.astype(jnp.bfloat16)
    output = hidden + jnp.dot(act_low, down_full, preferred_element_type=jnp.float32)
    latents = output.reshape(seq_count, own_latents, DL).astype(jnp.bfloat16)
    cot_low = cotangent.reshape(row_count, DL)
    down_local = jnp.einsum("rf,rd->fd", act_low, cot_low, preferred_element_type=jnp.float32)
    act_grad = jnp.einsum("rd,fd->rf", cot_low, down_full, preferred_element_type=jnp.float32)
    pre_grad = gelu_back(act_grad)[0].astype(jnp.bfloat16)
    up_local = jnp.einsum("rd,rf->df", mixer_low, pre_grad, preferred_element_type=jnp.float32)
    mixer_grad = jnp.einsum("rf,df->rd", pre_grad, up_full, preferred_element_type=jnp.float32)
    mixer_part = jnp.sum(mixer_grad * mixer_hat, axis=0)
    hidden_grad = cot_low.astype(jnp.float32) + norm_back(
        mixer_grad, mixer_hat, mixer_inv, mixer_gain
    )
    hidden_low = hidden_grad.astype(jnp.bfloat16)
    out_local = jnp.einsum("rv,rd->vd", attn_low, hidden_low, preferred_element_type=jnp.float32)
    attn_grad = jnp.einsum(
        "rd,vd->rv", hidden_low, out_full, preferred_element_type=jnp.float32
    ).astype(jnp.bfloat16)
    attn_heads = attn_grad.astype(jnp.float32).reshape(seq_count, own_latents, H, head_value)
    sum_grad = (
        (attn_heads / totals_own[..., None])
        .astype(jnp.bfloat16)
        .reshape(seq_count, own_latents, VD)
    )
    total_grad = (-jnp.sum(attn_heads * attended, axis=-1) / totals_own).astype(jnp.bfloat16)
    init_rows = jnp.sum(hidden_grad.reshape(seq_count, own_latents, DL), axis=0)

    def backward_step(carry, inputs):
        keys_seq, values_seq, limit, sum_own, total_own = inputs
        sum_all, total_all = (
            lax.all_gather(sum_own, "fsdp", axis=0, tiled=True),
            lax.all_gather(total_own, "fsdp", axis=0, tiled=True),
        )
        weights = exp_scores(keys_seq, limit)
        sum_heads = sum_all.reshape(latent_count, H, head_value)
        values_grad = jnp.einsum(
            "hji,jhv->ihv",
            weights.astype(jnp.bfloat16),
            sum_heads,
            preferred_element_type=jnp.float32,
        ).astype(jnp.bfloat16)
        weights_grad = (
            jnp.einsum("jhv,ihv->hji", sum_heads, values_seq, preferred_element_type=jnp.float32)
            + jnp.transpose(total_all.astype(jnp.float32))[:, :, None]
        )
        score_grad = (weights * weights_grad).astype(jnp.bfloat16)
        query_part = scale * jnp.einsum(
            "hji,ihd->jhd", score_grad, keys_seq, preferred_element_type=jnp.float32
        )
        keys_grad = (
            scale
            * jnp.einsum("hji,jhd->ihd", score_grad, query_low, preferred_element_type=jnp.float32)
        ).astype(jnp.bfloat16)
        query_own = lax.psum_scatter(
            query_part.reshape(latent_count, QK), "fsdp", scatter_dimension=0, tiled=True
        )
        return (carry, (keys_grad, values_grad, query_own))

    _, (keys_grad, values_grad, query_own) = lax.scan(
        backward_step,
        jnp.zeros((), jnp.float32),
        (keys_low, values_low, prefix, sum_grad, total_grad),
    )
    keys_flat = keys_grad.reshape(seq_count * seq_rows, QK)
    values_flat = values_grad.reshape(seq_count * seq_rows, VD)
    key_local = jnp.einsum("rb,rq->bq", byte_low, keys_flat, preferred_element_type=jnp.float32)
    value_local = jnp.einsum("rb,rv->bv", byte_low, values_flat, preferred_element_type=jnp.float32)
    normed_grad = jnp.einsum(
        "rq,bq->rb", keys_flat, key_full, preferred_element_type=jnp.float32
    ) + jnp.einsum("rv,bv->rb", values_flat, value_full, preferred_element_type=jnp.float32)
    byte_part = jnp.sum(normed_grad * byte_hat, axis=0)
    byte_grads = norm_back(normed_grad, byte_hat, byte_inv, byte_gain).reshape(
        seq_count, seq_rows, byte_width
    )
    query_grad_low = query_own.astype(jnp.bfloat16)
    own_low = lax.dynamic_slice_in_dim(latent_low, shard_index * own_latents, own_latents, 0)
    own_hat = lax.dynamic_slice_in_dim(latent_hat, shard_index * own_latents, own_latents, 0)
    own_inv = lax.dynamic_slice_in_dim(latent_inv, shard_index * own_latents, own_latents, 0)
    query_local = jnp.einsum(
        "ld,slq->dq", own_low, query_grad_low, preferred_element_type=jnp.float32
    )
    latent_grad = jnp.einsum(
        "slq,dq->ld", query_grad_low, query_full, preferred_element_type=jnp.float32
    )
    query_part_gain = jnp.sum(latent_grad * own_hat, axis=0)
    init_local = init_rows + norm_back(latent_grad, own_hat, own_inv, query_gain)
    byte_norm, query_norm, mixer_norm = lax.psum(
        (byte_part, query_part_gain, mixer_part), ("rep", "fsdp")
    )
    group_parts = (
        lax.psum_scatter(query_local, "fsdp", scatter_dimension=0, tiled=True),
        lax.psum_scatter(key_local, "fsdp", scatter_dimension=0, tiled=True),
        lax.psum_scatter(value_local, "fsdp", scatter_dimension=0, tiled=True),
        lax.psum_scatter(out_local, "fsdp", scatter_dimension=0, tiled=True),
        lax.psum_scatter(up_local, "fsdp", scatter_dimension=0, tiled=True),
        lax.psum_scatter(down_local, "fsdp", scatter_dimension=0, tiled=True),
    )
    query_grads, key_grads, value_grads, out_grads, up_grads, down_grads, init_grads = lax.psum(
        (
            group_parts[0],
            group_parts[1],
            group_parts[2],
            group_parts[3],
            group_parts[4],
            group_parts[5],
            init_local,
        ),
        "rep",
    )
    return (
        latents,
        byte_grads,
        init_grads,
        byte_norm,
        query_norm,
        mixer_norm,
        query_grads,
        key_grads,
        value_grads,
        out_grads,
        up_grads,
        down_grads,
    )


BF = jnp.bfloat16
F32 = jnp.float32
N = 8
NZ = 4
COST = 100_000_000_000
LOG2E = 1.4426950408889634
ANY = pl.BlockSpec(memory_space=pl.ANY)
VMEM = pl.BlockSpec(memory_space=pltpu.VMEM)
SMEM = pl.BlockSpec(memory_space=pltpu.SMEM)


def dot(a, b, ca, cb):
    return lax.dot_general(a, b, (((ca,), (cb,)), ((), ())), preferred_element_type=F32)


def send(x, k):
    return lax.ppermute(x, "fsdp", [(i, i ^ k) for i in range(N)])


def send_split(x, even, odd):
    return lax.ppermute(x, "fsdp", [(i, i ^ (odd if i & 1 else even)) for i in range(N)])


def send_z(x, k):
    return lax.ppermute(x, "rep", [(i, i ^ k) for i in range(NZ)])


def after(x, *deps):
    return lax.optimization_barrier((x, *deps))[0]


def me_z():
    return lax.axis_index("fsdp"), lax.axis_index("rep")


def owner(me, rel):
    even, odd = rel
    if even == odd:
        return me ^ even
    return me ^ jnp.where((me & 1) == 0, even, odd)


def call(body, out, ins, specs, scratch=(), name=None, grid=(), deps=(), out_specs=None, aliases=None, cost=COST, lead=()):
    n, skip, ahead = len(ins), len(deps), len(lead)

    def run(*refs):
        return body(*refs[ahead : ahead + n], *refs[ahead + n + skip :])

    return pl.pallas_call(
        run,
        grid=grid,
        out_shape=out,
        in_specs=[ANY] * ahead + list(specs) + [ANY] * skip,
        out_specs=jax.tree.map(lambda _: VMEM, out) if out_specs is None else out_specs,
        scratch_shapes=list(scratch),
        input_output_aliases=aliases or {},
        name=name,
        cost_estimate=pl.CostEstimate(flops=cost, bytes_accessed=1024, transcendentals=0),
    )(*lead, *ins, *deps)


def sds(shape, dtype):
    return jax.ShapeDtypeStruct(shape, dtype)


def ln_parts(v):
    centered = v - jnp.mean(v, axis=-1, keepdims=True)
    inverse = lax.rsqrt(jnp.mean(centered * centered, axis=-1, keepdims=True) + EPSILON)
    return centered * inverse, inverse


def ln_back(grad, hat, inverse, gain):
    scaled = grad * gain
    return inverse * (
        scaled
        - jnp.mean(scaled, axis=-1, keepdims=True)
        - hat * jnp.mean(scaled * hat, axis=-1, keepdims=True)
    )


WIDE = ((0, 0), (1, 1), (2, 4), (4, 2), (6, 6), (5, 3), (3, 5), (7, 7))
DIRECT = tuple((k, k) for k in range(N))


def pack_kernel(wk, wq, lat, wv, out):
    rows = wk.shape[0]
    out[0:rows, :] = wk[...]
    at = rows
    out[at : at + wq.shape[0], :] = wq[...]
    at += wq.shape[0]
    for c in range(5):
        out[at : at + lat.shape[0], :] = lat[:, 256 * c : 256 * (c + 1)]
        at += lat.shape[0]
    for c in range(5):
        out[at : at + wv.shape[0], :] = wv[:, 256 * c : 256 * (c + 1)]
        at += wv.shape[0]


def pack_rows_kernel(a, b, c, out):
    rows = a.shape[0]
    for n, ref in enumerate((a, b, c)):
        out[rows * n : rows * (n + 1), :] = ref[...]


def rows_of(j, size):
    return pl.ds(pl.multiple_of(j * size, size & -size), size)


def run_copies(copies, sem):
    handles = [pltpu.make_async_copy(a, b, sem.at[n]) for n, (a, b) in enumerate(copies)]
    for h in handles:
        h.start()
    return handles


def wait_all(handles):
    for h in handles:
        h.wait()


def norm_kernel(x, bg, xn_o):
    hat, _ = ln_parts(x[...].astype(F32))
    xn_o[...] = (hat * bg[...][None, :]).astype(BF)


def query_kernel(xn, qg, *rest):
    pieces, (k_o, wk_o, wq_o, q_o, zn_o, lat, sem) = rest[:N], rest[N:]
    me, _ = me_z()
    copies = []
    for piece, rel in zip(pieces, WIDE):
        j = owner(me, rel)
        copies.append((piece.at[pl.ds(0, 96), :], wk_o.at[rows_of(j, 96), :]))
        copies.append((piece.at[pl.ds(96, 160), :], wq_o.at[rows_of(j, 160), :]))
        for c in range(5):
            copies.append((piece.at[pl.ds(256 + 32 * c, 32), :], lat.at[rows_of(j, 32), pl.ds(256 * c, 256)]))
    wait_all(run_copies(copies, sem))
    zhat, _ = ln_parts(lat[...].astype(F32))
    zn_o[...] = (zhat * qg[...][None, :]).astype(BF)
    q_o[...] = dot(zn_o[...], wq_o[...], 1, 0).astype(BF)
    k_o[...] = dot(xn[...], wk_o[...], 1, 0).astype(BF)


def scores_kernel(prefix, k, q, e_o, ll_o):
    me, _ = me_z()
    lanes = lax.broadcasted_iota(jnp.int32, (256, 256), 1) // 32
    pos = lax.broadcasted_iota(jnp.int32, (256, 512), 1) + me * 512
    own = STRIDE * (lax.broadcasted_iota(jnp.int32, (256, 1), 0) + 1)
    lane = lax.broadcasted_iota(jnp.int32, (256, 128), 1)
    ll_o[...] = jnp.zeros_like(ll_o)
    for s in range(2):
        seen = jnp.maximum(own, prefix[s])

        def head(h, carry, s=s, seen=seen):
            qh = jnp.where(lanes == h, q[...], jnp.zeros((), BF))
            scores = dot(qh, k[512 * s : 512 * (s + 1), :], 1, 1)
            e = jnp.where(pos < seen, jnp.exp2(scores * (LOG2E * 32 ** (-0.5))), 0.0)
            ll_o[s] += jnp.where(lane == h, jnp.sum(e, axis=-1, keepdims=True), 0.0)
            e_o[s, h] = e.astype(BF)
            return carry

        lax.fori_loop(0, H, head, 0, unroll=2)


def values_kernel(xn, *rest):
    pieces, (vt_o, wv_o, sem) = rest[:N], rest[N:]
    me, _ = me_z()
    wait_all(
        run_copies(
            [
                (p.at[pl.ds(416 + 96 * c, 96), :], wv_o.at[rows_of(owner(me, rel), 96), pl.ds(256 * c, 256)])
                for p, rel in zip(pieces, WIDE)
                for c in range(5)
            ],
            sem,
        )
    )
    for c in range(5):
        cols = slice(256 * c, 256 * (c + 1))
        vt_o[cols, :] = dot(wv_o[:, cols], xn[...], 0, 1).astype(BF)


def sums_kernel(vt, e, ll, *rest):
    mine_o, theirs_o, aat, acc = rest[-4:]
    me, _ = me_z()

    def head(h, carry):
        rows = rows_of(h, 160)
        aat[rows, :] = dot(vt[rows, :], e[h], 1, 1).astype(BF)
        return carry

    lax.fori_loop(0, H, head, 0, unroll=2)
    acc[:, 0:1280] = aat[...].T
    acc[:, 1280:1408] = ll[...].astype(BF)
    for kk in range(4):
        for odd, ref in ((0, mine_o), (1, theirs_o)):
            ref[kk] = acc[rows_of(me ^ (2 * kk + odd), 32), :]


def add4_kernel(a, b, *outs):
    for kk in range(4):
        outs[kk][...] = (a[kk].astype(F32) + b[kk].astype(F32)).astype(BF)


def latent_kernel(m0, r1, r2, r3, lat, mg1, cot, *rest):
    pieces, rest = rest[:N], rest[N:]
    latents_o, agb_o, mine_o, theirs_o, dab_o, init_o = rest[:6]
    wout, wup, wdown, sem = rest[6:]
    me, zi = me_z()
    groups = []
    for g, w in enumerate((wout, wup, wdown)):
        copies = [
            (p.at[pl.ds(160 * g, 160), :], w.at[rows_of(owner(me, rel), 160), :]) for p, rel in zip(pieces, WIDE)
        ]
        groups.append(run_copies(copies, sem.at[g]))
    mg = mg1[...][None, :]
    total = (m0[...].astype(F32) + r1[...].astype(F32)) + (r2[...].astype(F32) + r3[...].astype(F32))
    aa = total[:, 0:1280]
    ll = total[:, 1280:1408]
    head = lax.broadcasted_iota(jnp.int32, (64, 1280), 1) // 160
    inv = jnp.zeros((64, 1280), F32)
    for h in range(H):
        inv = jnp.where(head == h, 1.0 / ll[:, h : h + 1], inv)
    oo = aa * inv
    ob = oo.astype(BF)
    for h in groups[0]:
        h.wait()
    start = lat[...].astype(F32)
    hh = jnp.concatenate([start, start], axis=0) + dot(ob, wout[...], 1, 0)
    hat, inverse = ln_parts(hh)
    hn = (hat * mg).astype(BF)
    for h in groups[1]:
        h.wait()
    uu = dot(hn, wup[...], 1, 0)
    cdf = 0.5 * (1.0 + lax.erf(uu * (0.5**0.5)))
    gg = (uu * cdf).astype(BF)
    slope = cdf + uu * (jnp.exp(-0.5 * uu * uu) * 0.3989422804014327)
    for h in groups[2]:
        h.wait()
    latents_o[...] = (hh + dot(gg, wdown[...], 1, 0)).astype(BF)
    du = (dot(cot[...], wdown[...], 1, 1) * slope).astype(BF)
    dhn = dot(du, wup[...], 1, 1)
    dhh = cot[...].astype(F32) + ln_back(dhn, hat, inverse, mg)
    init_o[...] = dhh[0:32] + dhh[32:64]
    dhb = dhh.astype(BF)
    dob = dot(dhb, wout[...], 1, 1).astype(BF).astype(F32)
    dab_o[:, 0:1280] = (dob * inv).astype(BF)
    prod = dob * oo
    lane = lax.broadcasted_iota(jnp.int32, (64, 128), 1)
    dlb = jnp.zeros((64, 128), F32)
    for h in range(H):
        part = jnp.sum(jnp.where(head == h, prod, 0.0), axis=-1, keepdims=True)
        dlb = jnp.where(lane == h, -part / ll[:, h : h + 1], dlb)
    dab_o[:, 1280:1408] = dlb.astype(BF)
    agb_o[0] = dhb
    agb_o[1] = du
    agb_o[2] = cot[...]
    for j in range(N):
        kk = (me >> 1) ^ (j >> 1)
        cols = slice(160 * j, 160 * (j + 1))

        @pl.when((me & 1) == (j & 1))
        def _():
            for n, v in enumerate((ob, hn, gg)):
                mine_o[kk, n] = v[:, cols]

        @pl.when((me & 1) != (j & 1))
        def _():
            for n, v in enumerate((ob, hn, gg)):
                theirs_o[kk, n] = v[:, cols]


def backward_kernel(s, k, vt, q, e, *rest):
    pieces = rest[:N]
    dkvt_o, dq_o, dabx, dabt, qt, sem = rest[-6:] if s else (*rest[N + 2 : N + 4], *rest[-4:])
    me, _ = me_z()
    handles = run_copies(
        [(p.at[pl.ds(32 * s, 32), :], dabx.at[rows_of(owner(me, rel), 32), :]) for p, rel in zip(pieces, DIRECT)], sem
    )
    if s == 0:
        for kk in range(1, 4):
            for n in range(2):
                rest[N + 3 + kk][n] = rest[N + n][kk]
    qt[...] = q[...].T
    dq_o[...] = jnp.zeros_like(dq_o)
    wait_all(handles)
    lanes = lax.broadcasted_iota(jnp.int32, (256, 256), 1) // 32
    lane = lax.broadcasted_iota(jnp.int32, (256, 128), 1)
    scale = 32 ** (-0.5)
    dabt[...] = dabx[:, 0:1280].T

    def head(h, carry):
        rows = rows_of(h, 160)
        dkvt_o[pl.ds(pl.multiple_of(256 + h * 160, 32), 160), :] = dot(dabt[rows, :], e[h], 1, 0).astype(BF)
        dlb = jnp.sum(jnp.where(lane == h, dabx[:, 1280:1408].astype(F32), 0.0), axis=-1, keepdims=True)
        dee = dot(dabt[rows, :], vt[rows, :], 0, 0) + dlb
        dss = (e[h].astype(F32) * dee).astype(BF)
        krows = rows_of(h, 32)
        dkvt_o[krows, :] = (dot(qt[krows, :], dss, 1, 0) * scale).astype(BF)
        dq_o[...] += jnp.where(lanes == h, dot(dss, k[...], 1, 0), 0.0)
        return carry

    lax.fori_loop(0, H, head, 0, unroll=2)
    dq_o[...] = dq_o[...] * scale


def weights_kernel(xn, zn, dkvt, dq0, dq1, mine_o, theirs_o, xnt, dw, dqg, dqs):
    me, _ = me_z()
    xnt[...] = xn[...].T
    dqs[...] = dq0[...] + dq1[...]
    for c in range(6):
        cols = slice(256 * c, 256 * (c + 1))
        dw[:, cols] = dot(xnt[...], dkvt[cols, :], 1, 1).astype(BF)
    dqg[...] = dot(zn[...], dqs[...].astype(BF), 0, 0).astype(BF)
    for kk in range(4):
        for odd, ref in ((0, mine_o), (1, theirs_o)):
            j = me ^ (2 * kk + odd)
            for c in range(6):
                ref[kk, 96 * c : 96 * (c + 1), :] = dw[rows_of(j, 96), 256 * c : 256 * (c + 1)]
            ref[kk, 576:736, :] = dqg[rows_of(j, 160), :]
            ref[kk, 736:768, :] = dqs[rows_of(j, 32), :].astype(BF)


def own_part(gain, me, size):
    out = gain[0:size][None, :]
    for j in range(1, N):
        out = jnp.where(me == j, gain[size * j : size * (j + 1)][None, :], out)
    return out


def sum_slots_kernel(a, b, c, d, wk, wv, wq, bg, qg, mix, *rest):
    near_o, far_o, send_o, norm_o, acc = rest
    me, zi = me_z()
    total = (a[...].astype(F32) + b[...].astype(F32)) + (c[...].astype(F32) + d[...].astype(F32))
    acc[...] = total.astype(BF)
    near_o[...] = acc[rows_of(zi, 192), :]
    far_o[...] = acc[rows_of(zi ^ 2, 192), :]
    send_o[0:192, :] = acc[rows_of(zi ^ 1, 192), :]
    send_o[192:384, :] = acc[rows_of(zi ^ 3, 192), :]
    prod = total[0:96] * wk[...].astype(F32)
    for n in range(5):
        prod += total[96 * (n + 1) : 96 * (n + 2)] * wv[:, 256 * n : 256 * (n + 1)].astype(F32)
    parts = (
        (row_sums(prod) / own_part(bg[...], me, 96), 96),
        (mix[...], 160),
        (row_sums(total[576:736] * wq[...].astype(F32)) / own_part(qg[...], me, 160), 160),
    )
    padded = [v if size == 160 else jnp.concatenate([v, jnp.zeros((8, 160 - size), F32)], axis=1) for v, size in parts]
    joined = jnp.concatenate(padded + [jnp.zeros((8, 32), F32)], axis=1)
    placed = jnp.where(lax.broadcasted_iota(jnp.int32, (8, 512), 0) == me, joined, 0.0)
    norm_o[...] = jnp.concatenate([placed[:, 0:256], placed[:, 256:512]], axis=0).astype(BF)


def bytes_kernel(x, bg, wk, wv, dkvt, *rest):
    out = rest[-1]
    hat, inverse = ln_parts(x[...].astype(F32))
    dxn = dot(dkvt[0:256, :], wk[...], 0, 1) + dot(dkvt[256:1536, :], wv[...], 0, 1)
    out[...] = ln_back(dxn, hat, inverse, bg[...][None, :])


def latent_grads_kernel(init, wup, mg, *rest):
    (amine, at, b1, b2, b3), rest = rest[N : N + 5], rest[:N] + rest[N + 5 :]
    rows, outs, mix_o, (xs, ys, acc, sem) = rest[:N], rest[N : N + 4], rest[N + 4], rest[N + 5 :]
    me, zi = me_z()
    copies = []
    cols = (amine.at[0], at.at[0], b1.at[0], b1.at[1], b2.at[0], b2.at[1], b3.at[0], b3.at[1])
    for k in range(N):
        copies.append((cols[k], xs.at[:, rows_of(me ^ k, 64), :]))
        copies.append((rows[k], ys.at[:, rows_of(owner(me, WIDE[k]), 64), :]))
    wait_all(run_copies(copies, sem))
    for n in range(3):
        grad = dot(xs[n], ys[n], 0, 0)
        acc[160 * n : 160 * (n + 1), :] = grad.astype(BF)
        if n == 1:
            mix_o[...] = row_sums(grad * wup[...].astype(F32)) / own_part(mg[...], me, 160)
    acc[480:512, :] = init[...].astype(BF)
    for r in range(NZ):
        outs[r][...] = acc[rows_of(zi ^ r, 128), :]


def row_sums(v):
    ones = jnp.ones((8, v.shape[1]), F32)
    return lax.dot_general(
        ones, v, (((1,), (1,)), ((), ())), precision=lax.Precision.HIGHEST, preferred_element_type=F32
    )


def finish_latent_kernel(*rest):
    pieces, (out_o, up_o, down_o, init_o, acc) = rest[:NZ], rest[NZ:]
    _, zi = me_z()
    for r in range(NZ):
        acc[rows_of(zi ^ r, 128), :] = pieces[r][...]
    out_o[...] = acc[0:160, :].astype(F32)
    up_o[...] = acc[160:320, :].astype(F32)
    down_o[...] = acc[320:480, :].astype(F32)
    init_o[...] = acc[480:512, :].astype(F32)


def finish_norms(both, outs):
    total = jnp.concatenate([both[0:8], both[8:16]], axis=1)
    for n, (out, size) in enumerate(zip(outs, (96, 160, 160))):
        width = out.shape[0]
        at = lax.broadcasted_iota(jnp.int32, (160, width), 1)
        pick = (at % size == lax.broadcasted_iota(jnp.int32, (160, width), 0)).astype(F32)
        wide = lax.dot_general(
            total[:, 160 * n : 160 * (n + 1)],
            pick,
            (((1,), (0,)), ((), ())),
            precision=lax.Precision.HIGHEST,
            preferred_element_type=F32,
        )
        mine = lax.broadcasted_iota(jnp.int32, (8, width), 0) == lax.broadcasted_iota(jnp.int32, (8, width), 1) // size
        out[...] = jnp.sum(jnp.where(mine, wide, 0.0), axis=0)


def plus(a, b):
    return (a.astype(F32) + b.astype(F32)).astype(BF)


def finish_kernel(wq_full, lat, qg, init, *rest):
    pieces, (key_o, value_o, query_o, init_o), outs, acc = rest[:NZ], rest[NZ : NZ + 4], rest[NZ + 4 : NZ + 7], rest[-1]
    _, zi = me_z()
    for r in range(NZ):
        acc[rows_of(zi ^ r, 192), :] = pieces[r][0:192, :]
    a, b, c, d = [p[192:208, :].astype(F32) for p in pieces]
    finish_norms((a + b) + (c + d), outs)
    key_o[...] = acc[0:96, :].astype(F32)
    for c in range(5):
        value_o[:, 256 * c : 256 * (c + 1)] = acc[96 * (c + 1) : 96 * (c + 2), :].astype(F32)
    query_o[...] = acc[576:736, :].astype(F32)
    dzn = dot(acc[736:768, :], wq_full[...], 1, 1)
    hat, inverse = ln_parts(lat[...].astype(F32))
    init_o[...] = init[...] + ln_back(dzn, hat, inverse, qg[...][None, :])


def sum_of_three_kernel(a, b, c, out):
    out[...] = (a[...].astype(F32) + b[...].astype(F32) + c[...].astype(F32)).astype(BF)


def first_zq_kernel(near, far, got, near_o, far_o):
    near_o[...] = plus(near[...], got[0:192, :])
    far_o[...] = plus(far[...], got[192:384, :])


def second_zq_kernel(near, got, a, b, out):
    out[0:192, :] = plus(near[...], got[...])
    out[192:208, :] = plus(a[...], b[...])


def sums_of_pairs_kernel(*refs):
    n = len(refs) // 3
    for k in range(n):
        a, b, out = refs[2 * k], refs[2 * k + 1], refs[2 * n + k]
        out[...] = (a[...].astype(F32) + b[...].astype(F32)).astype(out.dtype)


def sums_of_pairs(pairs, name, deps=(), cost=COST):
    flat = [x for pair in pairs for x in pair]
    out = [sds(a.shape, a.dtype) for a, _ in pairs]
    return call(sums_of_pairs_kernel, out, flat, [VMEM] * len(flat), name=name, deps=deps, cost=cost)


def part(f, *args):
    def body(*refs):
        return f(*args, *refs)

    return body


def tie(*xs):
    return lax.optimization_barrier(xs)


def per_device_fast(
    byte_feats,
    latent_init,
    prefix,
    byte_gain,
    query_gain,
    mixer_gain,
    query_weight,
    key_weight,
    value_weight,
    out_weight,
    up_weight,
    down_weight,
    cotangent,
):
    seqs, rows, width = byte_feats.shape
    own = latent_init.shape[0]
    x = byte_feats.reshape(seqs * rows, width)
    cot = cotangent.reshape(seqs * own, DL)

    def first(w):
        return send_split(w, 2, 4), send_split(w, 4, 2)

    packed = call(
        pack_kernel, sds((896, 256), BF), (key_weight, query_weight, latent_init, value_weight), [VMEM] * 4, name="pack"
    )
    pa, pb = first(packed)
    wcat = call(
        pack_rows_kernel, sds((480, 1280), BF), (out_weight, up_weight, down_weight), [VMEM] * 3, name="pack_rows", deps=(packed,)
    )
    xn = call(norm_kernel, sds((1024, 768), BF), (x, byte_gain), [VMEM] * 2, name="norm", deps=(wcat,))
    pa, pb, xn, near, wcat = tie(pa, pb, xn, packed, wcat)
    wa = send_split(wcat, 2, 4)
    pd = send_split(pa, 4, 2)
    pn, pna, pnb = send(near, 1), send(pa, 1), send(pb, 1)
    pd, pn, wcat = tie(pd, pn, wcat)
    pnd = send(pd, 1)
    wb = send_split(wcat, 4, 2)
    pieces = (packed, pn, pa, pb, pd, pna, pnb, pnd)
    k, wk, wq_full, q, zn = call(
        query_kernel,
        (sds((1024, 256), BF), sds((768, 256), BF), sds((1280, 256), BF), sds((256, 256), BF), sds((256, 1280), BF)),
        (xn, query_gain, *pieces),
        [VMEM] * 2 + [ANY] * N,
        [pltpu.VMEM((256, 1280), BF), pltpu.SemaphoreType.DMA((7 * N,))],
        name="query",
    )
    q, wcat = tie(q, wcat)
    wn = send(wcat, 1)
    e, ll = call(
        scores_kernel,
        (sds((2, 8, 256, 512), BF), sds((2, 256, 128), F32)),
        (prefix, k, q),
        [SMEM, VMEM, VMEM],
        name="scores",
    )
    vt, wv = call(
        values_kernel,
        (sds((1280, 1024), BF), sds((768, 1280), BF)),
        (xn, *pieces),
        [VMEM] + [ANY] * N,
        [pltpu.SemaphoreType.DMA((5 * N,))],
        name="values",
        deps=(e, wn),
    )
    def sums(s, *prev):
        return call(
            sums_kernel,
            (sds((4, 64, 1408), BF), sds((4, 64, 1408), BF)),
            (vt, e, ll, *prev),
            [
                pl.BlockSpec((1280, 512), lambda g: (0, s)),
                pl.BlockSpec((None, 8, 256, 512), lambda g: (s, 0, 0, 0)),
                pl.BlockSpec((None, 256, 128), lambda g: (s, 0, 0)),
            ]
            + [ANY] * len(prev),
            [pltpu.VMEM((1280, 256), BF), pltpu.VMEM((256, 1408), BF)],
            out_specs=[pl.BlockSpec((4, 32, 1408), lambda g: (0, s, 0))] * 2,
            aliases={3: 0, 4: 1} if prev else {},
            name="sums",
            grid=(1,),
        )

    vt, wa, wb = tie(vt, wa, wb)
    mine, theirs = sums(0)
    wd = send_split(wa, 4, 2)
    wna, wnb = send(wa, 1), send(wb, 1)
    mine, theirs = sums(1, mine, theirs)
    got = send(theirs, 1)
    m0, m1, m2, m3 = call(
        add4_kernel, (sds((64, 1408), BF),) * 4, (mine, got), [VMEM] * 2, name="add4", deps=(wna, wnb), cost=1024
    )
    r1, r2, r3 = send(m1, 2), send(m2, 4), send(m3, 6)
    m0, wd = tie(m0, wd)
    wnd = send(wd, 1)
    latents, agb, amine, atheirs, dabx, init = call(
        latent_kernel,
        (
            sds((64, 1280), BF), sds((3, 64, 1280), BF), sds((4, 3, 64, 160), BF), sds((4, 3, 64, 160), BF),
            sds((64, 1408), BF), sds((32, 1280), F32),
        ),
        (m0, r1, r2, r3, latent_init, mixer_gain, cot, wcat, wn, wa, wb, wd, wna, wnb, wnd),
        [VMEM] * 7 + [ANY] * N,
        [pltpu.VMEM((1280, 1280), BF)] * 3 + [pltpu.SemaphoreType.DMA((3, N))],
        name="latent",
    )
    d2, d4, d6, d1 = send(dabx, 2), send(dabx, 4), send(dabx, 6), send(dabx, 1)
    at = send(atheirs, 1)
    d2, d4, d6, agb = tie(d2, d4, d6, agb)
    d3, d5, d7 = send(d2, 1), send(d4, 1), send(d6, 1)
    dab_p = [dabx, d1, d2, d3, d4, d5, d6, d7]
    ga, gb = first(agb)
    gn = send(agb, 1)

    def backward(s, *extra, deps=()):
        both = [sds((2, 3, 64, 160), BF)] * (0 if s else 3)
        return call(
            part(backward_kernel, s),
            (sds((1536, 1024), BF), sds((256, 256), F32), *both),
            (k, vt, q, e, *dab_p, *extra),
            [
                pl.BlockSpec((512, 256), lambda g: (s, 0)),
                pl.BlockSpec((1280, 512), lambda g: (0, s)),
                VMEM,
                pl.BlockSpec((None, 8, 256, 512), lambda g: (s, 0, 0, 0)),
            ]
            + [ANY] * N + [ANY if s else VMEM] * len(extra),
            [
                pltpu.VMEM((256, 1408), BF), pltpu.VMEM((1280, 256), BF), pltpu.VMEM((256, 256), BF),
                pltpu.SemaphoreType.DMA((N,)),
            ],
            out_specs=(pl.BlockSpec((1536, 512), lambda g: (0, s)), VMEM, *[VMEM] * len(both)),
            aliases={4 + N: 0} if s else {},
            name="backward",
            grid=(1,),
            deps=deps,
            cost=1024 if s else COST,
        )

    dkvt, dq0, *both = backward(0, amine, at)
    dq0, ga, gb, gn = tie(dq0, ga, gb, gn)
    gd = send_split(ga, 4, 2)
    gna = send(ga, 1)
    both_s = [send(b, 2 * kk + 2) for kk, b in enumerate(both)]
    dkvt, dq1 = backward(1, dkvt, deps=(dq0,))
    dq1, gd, gna, gb = tie(dq1, gd, gna, gb)
    gnb, gnd = send(gb, 1), send(gd, 1)
    gmine, gtheirs = call(
        weights_kernel,
        (sds((4, 768, 256), BF), sds((4, 768, 256), BF)),
        (xn, zn, dkvt, dq0, dq1),
        [VMEM] * 5,
        [
            pltpu.VMEM((768, 1024), BF), pltpu.VMEM((768, 1536), BF), pltpu.VMEM((1280, 256), BF),
            pltpu.VMEM((256, 256), F32),
        ],
        name="weights",
        deps=(),
    )
    gg = send(gtheirs, 1)

    *oud, mix = call(
        latent_grads_kernel,
        (sds((128, 1280), BF),) * NZ + (sds((8, 160), F32),),
        (init, up_weight, mixer_gain, agb, gn, ga, gb, gd, gna, gnb, gnd, amine, at, *both_s),
        [VMEM] * 3 + [ANY] * (5 + N),
        [
            pltpu.VMEM((3, 512, 160), BF), pltpu.VMEM((3, 512, 1280), BF), pltpu.VMEM((512, 1280), BF),
            pltpu.SemaphoreType.DMA((2 * N,)),
        ],
        name="latent_grads",
        deps=(gtheirs,),
    )
    o3 = send_z(oud[3], 1)
    gm = call(add4_kernel, (sds((768, 256), BF),) * 4, (gmine, gg), [VMEM] * 2, name="add4g", deps=(oud[0],))
    g1, g2, g3 = send(gm[1], 2), send(gm[2], 4), send(gm[3], 6)
    (ofar,) = sums_of_pairs(((oud[2], o3),), "osum", deps=(gm[0],))
    ofar, o1 = tie(ofar, oud[1])
    o22, o1 = send_z(ofar, 2), send_z(o1, 1)
    byte_grads = call(
        bytes_kernel,
        sds((2, 512, 768), F32),
        (x, byte_gain, wk, wv, dkvt),
        [
            pl.BlockSpec((256, 768), lambda b: (b, 0)),
            pl.BlockSpec((768,), lambda b: (0,)),
            pl.BlockSpec((768, 256), lambda b: (0, 0)),
            pl.BlockSpec((768, 1280), lambda b: (0, 0)),
            pl.BlockSpec((1536, 256), lambda b: (0, b)),
        ],
        out_specs=pl.BlockSpec((None, 256, 768), lambda b: (b // 2, b % 2, 0)),
        name="bytes",
        grid=(4,),
        deps=(ofar,),
        cost=1024,
    )
    qnear, qfar, qsend, norm = call(
        sum_slots_kernel,
        (sds((192, 256), BF), sds((192, 256), BF), sds((384, 256), BF), sds((16, 256), BF)),
        (gm[0], g1, g2, g3, key_weight, value_weight, query_weight, byte_gain, query_gain, mix),
        [VMEM] * 10,
        [pltpu.VMEM((768, 256), BF)],
        name="gsum",
        deps=(byte_grads,),
    )
    qgot = send_z(qsend, 1)
    ototal = call(
        sum_of_three_kernel, sds((128, 1280), BF), (oud[0], o1, o22), [VMEM] * 3, name="ototal", lead=(qnear,)
    )
    o2 = send_z(ototal, 2)
    qnear, qfar = call(
        first_zq_kernel,
        (sds((192, 256), BF), sds((192, 256), BF)),
        (qnear, qfar, qgot),
        [VMEM] * 3,
        name="qsum",
        deps=(ototal,),
    )
    qfar, norm, oshare = tie(qfar, norm, ototal)
    qgot, n3, o1 = send_z(qfar, 2), send(norm, 1), send_z(oshare, 1)
    (norm,) = sums_of_pairs(((norm, n3),), "nsum", cost=1024)
    n4 = send(norm, 2)
    (norm,) = sums_of_pairs(((norm, n4),), "nsum", cost=1024)
    norm, o2 = tie(norm, o2)
    n5, ofar2 = send(norm, 4), send_z(o2, 1)
    qtotal = call(
        second_zq_kernel,
        sds((208, 256), BF),
        (qnear, qgot, norm, n5),
        [VMEM] * 4,
        name="qtotal",
        deps=(o2, o1),
    )
    q2, q1 = send_z(qtotal, 2), send_z(qtotal, 1)
    out_g, up_g, down_g, init_sum = call(
        finish_latent_kernel,
        (sds((160, 1280), F32),) * 3 + (sds((32, 1280), F32),),
        (ototal, o1, o2, ofar2),
        [VMEM] * NZ,
        [pltpu.VMEM((512, 1280), BF)],
        name="finish_latent",
        cost=1024,
    )
    q3 = send_z(q2, 1)
    key_g, value_g, query_g, init_g, byte_n, mixer_n, query_n = call(
        finish_kernel,
        (
            sds((96, 256), F32), sds((96, 1280), F32), sds((160, 256), F32), sds((32, 1280), F32),
            sds((768,), F32), sds((1280,), F32), sds((1280,), F32),
        ),
        (wq_full, latent_init, query_gain, init_sum, qtotal, q1, q2, q3),
        [VMEM] * (4 + NZ),
        [pltpu.VMEM((768, 256), BF)],
        name="finish",
        cost=1024,
    )
    return (
        latents.reshape(seqs, own, DL),
        byte_grads,
        init_g,
        byte_n,
        query_n,
        mixer_n,
        query_g,
        key_g,
        value_g,
        out_g,
        up_g,
        down_g,
    )


def solution(mesh):
    fast = mesh.shape["fsdp"] == 8 and mesh.shape["rep"] == 4
    device_fn = per_device_fast if fast else per_device_plain
    placed = (
        P("rep", "fsdp", None),
        P("fsdp", None),
        P("rep"),
        P(),
        P(),
        P(),
        P("fsdp", None),
        P("fsdp", None),
        P("fsdp", None),
        P("fsdp", None),
        P("fsdp", None),
        P("fsdp", None),
        P("rep", "fsdp", None),
    )
    return jax.shard_map(
        device_fn,
        mesh=mesh,
        in_specs=placed,
        out_specs=(
            P("rep", "fsdp", None),
            P("rep", "fsdp", None),
            P("fsdp", None),
            P(),
            P(),
            P(),
            P("fsdp", None),
            P("fsdp", None),
            P("fsdp", None),
            P("fsdp", None),
            P("fsdp", None),
            P("fsdp", None),
        ),
        check_vma=False,
    )
```

```python
import jax
import jax.numpy as jnp
from jax import lax
from jax.experimental import pallas as pl
from jax.experimental.pallas import tpu as pltpu
from jax.sharding import PartitionSpec as P

DL = 1280
H = 8
QK = 256
VD = 1280
STRIDE = 16


EPSILON = 1e-05


def norm_parts(values, gain):
    centered = values - jnp.mean(values, axis=-1, keepdims=True)
    variance = jnp.mean(centered * centered, axis=-1, keepdims=True)
    inverse = lax.rsqrt(variance + EPSILON)
    normal = centered * inverse
    return (normal * gain, normal, inverse)


def norm_back(grad_out, normal, inverse, gain):
    scaled = grad_out * gain
    mean_one = jnp.mean(scaled, axis=-1, keepdims=True)
    mean_two = jnp.mean(scaled * normal, axis=-1, keepdims=True)
    return inverse * (scaled - mean_one - normal * mean_two)


def per_device_plain(
    byte_feats,
    latent_init,
    prefix,
    byte_gain,
    query_gain,
    mixer_gain,
    query_weight,
    key_weight,
    value_weight,
    out_weight,
    up_weight,
    down_weight,
    cotangent,
):
    shard_count = lax.axis_size("fsdp")
    shard_index = lax.axis_index("fsdp")
    seq_count, seq_rows, byte_width = byte_feats.shape
    own_latents = latent_init.shape[0]
    latent_count = own_latents * shard_count
    head_qk = QK // H
    head_value = VD // H
    scale = head_qk ** (-0.5)
    row_count = seq_count * own_latents
    latent_all, query_full, key_full, value_full = (
        lax.all_gather(latent_init, "fsdp", axis=0, tiled=True),
        lax.all_gather(query_weight, "fsdp", axis=0, tiled=True),
        lax.all_gather(key_weight, "fsdp", axis=0, tiled=True),
        lax.all_gather(value_weight, "fsdp", axis=0, tiled=True),
    )
    out_full, up_full, down_full = (
        lax.all_gather(out_weight, "fsdp", axis=0, tiled=True),
        lax.all_gather(up_weight, "fsdp", axis=0, tiled=True),
        lax.all_gather(down_weight, "fsdp", axis=0, tiled=True),
    )
    byte_flat = byte_feats.astype(jnp.float32).reshape(seq_count * seq_rows, byte_width)
    byte_normed, byte_hat, byte_inv = norm_parts(byte_flat, byte_gain)
    byte_low = byte_normed.astype(jnp.bfloat16)
    keys_low = (
        jnp.dot(byte_low, key_full, preferred_element_type=jnp.float32)
        .astype(jnp.bfloat16)
        .reshape(seq_count, seq_rows, H, head_qk)
    )
    values_low = (
        jnp.dot(byte_low, value_full, preferred_element_type=jnp.float32)
        .astype(jnp.bfloat16)
        .reshape(seq_count, seq_rows, H, head_value)
    )
    latent_normed, latent_hat, latent_inv = norm_parts(latent_all.astype(jnp.float32), query_gain)
    latent_low = latent_normed.astype(jnp.bfloat16)
    query_low = (
        jnp.dot(latent_low, query_full, preferred_element_type=jnp.float32)
        .astype(jnp.bfloat16)
        .reshape(latent_count, H, head_qk)
    )
    byte_pos = shard_index * seq_rows + jnp.arange(seq_rows, dtype=jnp.int32)
    latent_pos = jnp.arange(latent_count, dtype=jnp.int32)

    def exp_scores(keys_seq, limit):
        scores = scale * jnp.einsum(
            "jhd,ihd->hji", query_low, keys_seq, preferred_element_type=jnp.float32
        )
        visible = (byte_pos[None, :] < limit) | (
            byte_pos[None, :] < STRIDE * (latent_pos[:, None] + 1)
        )
        return jnp.where(visible[None], jnp.exp(scores), 0.0)

    def forward_step(carry, inputs):
        keys_seq, values_seq, limit = inputs
        weights = exp_scores(keys_seq, limit)
        totals = jnp.transpose(jnp.sum(weights, axis=-1))
        summed = jnp.einsum(
            "hji,ihv->jhv",
            weights.astype(jnp.bfloat16),
            values_seq,
            preferred_element_type=jnp.float32,
        ).reshape(latent_count, VD)
        own_sum, own_total = (
            lax.psum_scatter(summed, "fsdp", scatter_dimension=0, tiled=True),
            lax.psum_scatter(totals, "fsdp", scatter_dimension=0, tiled=True),
        )
        return (carry, (own_sum, own_total))

    _, (sums_own, totals_own) = lax.scan(
        forward_step, jnp.zeros((), jnp.float32), (keys_low, values_low, prefix)
    )
    attended = sums_own.reshape(seq_count, own_latents, H, head_value) / totals_own[..., None]
    attn_low = attended.reshape(row_count, VD).astype(jnp.bfloat16)
    mixed = jnp.dot(attn_low, out_full, preferred_element_type=jnp.float32).reshape(
        seq_count, own_latents, DL
    )
    hidden = (mixed + latent_init.astype(jnp.float32)[None]).reshape(row_count, DL)
    mixer_normed, mixer_hat, mixer_inv = norm_parts(hidden, mixer_gain)
    mixer_low = mixer_normed.astype(jnp.bfloat16)
    pre_act = jnp.dot(mixer_low, up_full, preferred_element_type=jnp.float32)
    activated, gelu_back = jax.vjp(lambda value: jax.nn.gelu(value, approximate=False), pre_act)
    act_low = activated.astype(jnp.bfloat16)
    output = hidden + jnp.dot(act_low, down_full, preferred_element_type=jnp.float32)
    latents = output.reshape(seq_count, own_latents, DL).astype(jnp.bfloat16)
    cot_low = cotangent.reshape(row_count, DL)
    down_local = jnp.einsum("rf,rd->fd", act_low, cot_low, preferred_element_type=jnp.float32)
    act_grad = jnp.einsum("rd,fd->rf", cot_low, down_full, preferred_element_type=jnp.float32)
    pre_grad = gelu_back(act_grad)[0].astype(jnp.bfloat16)
    up_local = jnp.einsum("rd,rf->df", mixer_low, pre_grad, preferred_element_type=jnp.float32)
    mixer_grad = jnp.einsum("rf,df->rd", pre_grad, up_full, preferred_element_type=jnp.float32)
    mixer_part = jnp.sum(mixer_grad * mixer_hat, axis=0)
    hidden_grad = cot_low.astype(jnp.float32) + norm_back(
        mixer_grad, mixer_hat, mixer_inv, mixer_gain
    )
    hidden_low = hidden_grad.astype(jnp.bfloat16)
    out_local = jnp.einsum("rv,rd->vd", attn_low, hidden_low, preferred_element_type=jnp.float32)
    attn_grad = jnp.einsum(
        "rd,vd->rv", hidden_low, out_full, preferred_element_type=jnp.float32
    ).astype(jnp.bfloat16)
    attn_heads = attn_grad.astype(jnp.float32).reshape(seq_count, own_latents, H, head_value)
    sum_grad = (
        (attn_heads / totals_own[..., None])
        .astype(jnp.bfloat16)
        .reshape(seq_count, own_latents, VD)
    )
    total_grad = (-jnp.sum(attn_heads * attended, axis=-1) / totals_own).astype(jnp.bfloat16)
    init_rows = jnp.sum(hidden_grad.reshape(seq_count, own_latents, DL), axis=0)

    def backward_step(carry, inputs):
        keys_seq, values_seq, limit, sum_own, total_own = inputs
        sum_all, total_all = (
            lax.all_gather(sum_own, "fsdp", axis=0, tiled=True),
            lax.all_gather(total_own, "fsdp", axis=0, tiled=True),
        )
        weights = exp_scores(keys_seq, limit)
        sum_heads = sum_all.reshape(latent_count, H, head_value)
        values_grad = jnp.einsum(
            "hji,jhv->ihv",
            weights.astype(jnp.bfloat16),
            sum_heads,
            preferred_element_type=jnp.float32,
        ).astype(jnp.bfloat16)
        weights_grad = (
            jnp.einsum("jhv,ihv->hji", sum_heads, values_seq, preferred_element_type=jnp.float32)
            + jnp.transpose(total_all.astype(jnp.float32))[:, :, None]
        )
        score_grad = (weights * weights_grad).astype(jnp.bfloat16)
        query_part = scale * jnp.einsum(
            "hji,ihd->jhd", score_grad, keys_seq, preferred_element_type=jnp.float32
        )
        keys_grad = (
            scale
            * jnp.einsum("hji,jhd->ihd", score_grad, query_low, preferred_element_type=jnp.float32)
        ).astype(jnp.bfloat16)
        query_own = lax.psum_scatter(
            query_part.reshape(latent_count, QK), "fsdp", scatter_dimension=0, tiled=True
        )
        return (carry, (keys_grad, values_grad, query_own))

    _, (keys_grad, values_grad, query_own) = lax.scan(
        backward_step,
        jnp.zeros((), jnp.float32),
        (keys_low, values_low, prefix, sum_grad, total_grad),
    )
    keys_flat = keys_grad.reshape(seq_count * seq_rows, QK)
    values_flat = values_grad.reshape(seq_count * seq_rows, VD)
    key_local = jnp.einsum("rb,rq->bq", byte_low, keys_flat, preferred_element_type=jnp.float32)
    value_local = jnp.einsum("rb,rv->bv", byte_low, values_flat, preferred_element_type=jnp.float32)
    normed_grad = jnp.einsum(
        "rq,bq->rb", keys_flat, key_full, preferred_element_type=jnp.float32
    ) + jnp.einsum("rv,bv->rb", values_flat, value_full, preferred_element_type=jnp.float32)
    byte_part = jnp.sum(normed_grad * byte_hat, axis=0)
    byte_grads = norm_back(normed_grad, byte_hat, byte_inv, byte_gain).reshape(
        seq_count, seq_rows, byte_width
    )
    query_grad_low = query_own.astype(jnp.bfloat16)
    own_low = lax.dynamic_slice_in_dim(latent_low, shard_index * own_latents, own_latents, 0)
    own_hat = lax.dynamic_slice_in_dim(latent_hat, shard_index * own_latents, own_latents, 0)
    own_inv = lax.dynamic_slice_in_dim(latent_inv, shard_index * own_latents, own_latents, 0)
    query_local = jnp.einsum(
        "ld,slq->dq", own_low, query_grad_low, preferred_element_type=jnp.float32
    )
    latent_grad = jnp.einsum(
        "slq,dq->ld", query_grad_low, query_full, preferred_element_type=jnp.float32
    )
    query_part_gain = jnp.sum(latent_grad * own_hat, axis=0)
    init_local = init_rows + norm_back(latent_grad, own_hat, own_inv, query_gain)
    byte_norm, query_norm, mixer_norm = lax.psum(
        (byte_part, query_part_gain, mixer_part), ("rep", "fsdp")
    )
    group_parts = (
        lax.psum_scatter(query_local, "fsdp", scatter_dimension=0, tiled=True),
        lax.psum_scatter(key_local, "fsdp", scatter_dimension=0, tiled=True),
        lax.psum_scatter(value_local, "fsdp", scatter_dimension=0, tiled=True),
        lax.psum_scatter(out_local, "fsdp", scatter_dimension=0, tiled=True),
        lax.psum_scatter(up_local, "fsdp", scatter_dimension=0, tiled=True),
        lax.psum_scatter(down_local, "fsdp", scatter_dimension=0, tiled=True),
    )
    query_grads, key_grads, value_grads, out_grads, up_grads, down_grads, init_grads = lax.psum(
        (
            group_parts[0],
            group_parts[1],
            group_parts[2],
            group_parts[3],
            group_parts[4],
            group_parts[5],
            init_local,
        ),
        "rep",
    )
    return (
        latents,
        byte_grads,
        init_grads,
        byte_norm,
        query_norm,
        mixer_norm,
        query_grads,
        key_grads,
        value_grads,
        out_grads,
        up_grads,
        down_grads,
    )


BF = jnp.bfloat16
F32 = jnp.float32
N = 8
NZ = 4
COST = 100_000_000_000
LOG2E = 1.4426950408889634
ANY = pl.BlockSpec(memory_space=pl.ANY)
VMEM = pl.BlockSpec(memory_space=pltpu.VMEM)
SMEM = pl.BlockSpec(memory_space=pltpu.SMEM)


def dot(a, b, ca, cb):
    return lax.dot_general(a, b, (((ca,), (cb,)), ((), ())), preferred_element_type=F32)


def send(x, k):
    return lax.ppermute(x, "fsdp", [(i, i ^ k) for i in range(N)])


def send_split(x, even, odd):
    return lax.ppermute(x, "fsdp", [(i, i ^ (odd if i & 1 else even)) for i in range(N)])


def send_z(x, k):
    return lax.ppermute(x, "rep", [(i, i ^ k) for i in range(NZ)])


def after(x, *deps):
    return lax.optimization_barrier((x, *deps))[0]


def me_z():
    return lax.axis_index("fsdp"), lax.axis_index("rep")


def owner(me, rel):
    even, odd = rel
    if even == odd:
        return me ^ even
    return me ^ jnp.where((me & 1) == 0, even, odd)


def call(body, out, ins, specs, scratch=(), name=None, grid=(), deps=(), out_specs=None, aliases=None, cost=COST, lead=()):
    n, skip, ahead = len(ins), len(deps), len(lead)

    def run(*refs):
        return body(*refs[ahead : ahead + n], *refs[ahead + n + skip :])

    return pl.pallas_call(
        run,
        grid=grid,
        out_shape=out,
        in_specs=[ANY] * ahead + list(specs) + [ANY] * skip,
        out_specs=jax.tree.map(lambda _: VMEM, out) if out_specs is None else out_specs,
        scratch_shapes=list(scratch),
        input_output_aliases=aliases or {},
        name=name,
        cost_estimate=pl.CostEstimate(flops=cost, bytes_accessed=1024, transcendentals=0),
    )(*lead, *ins, *deps)


def sds(shape, dtype):
    return jax.ShapeDtypeStruct(shape, dtype)


def ln_parts(v):
    centered = v - jnp.mean(v, axis=-1, keepdims=True)
    inverse = lax.rsqrt(jnp.mean(centered * centered, axis=-1, keepdims=True) + EPSILON)
    return centered * inverse, inverse


def ln_back(grad, hat, inverse, gain):
    scaled = grad * gain
    return inverse * (
        scaled
        - jnp.mean(scaled, axis=-1, keepdims=True)
        - hat * jnp.mean(scaled * hat, axis=-1, keepdims=True)
    )


WIDE = ((0, 0), (1, 1), (2, 4), (4, 2), (6, 6), (5, 3), (3, 5), (7, 7))
DIRECT = tuple((k, k) for k in range(N))


def pack_kernel(wk, wq, lat, wv, out):
    rows = wk.shape[0]
    out[0:rows, :] = wk[...]
    at = rows
    out[at : at + wq.shape[0], :] = wq[...]
    at += wq.shape[0]
    for c in range(5):
        out[at : at + lat.shape[0], :] = lat[:, 256 * c : 256 * (c + 1)]
        at += lat.shape[0]
    for c in range(5):
        out[at : at + wv.shape[0], :] = wv[:, 256 * c : 256 * (c + 1)]
        at += wv.shape[0]


def pack_rows_kernel(a, b, c, out):
    rows = a.shape[0]
    for n, ref in enumerate((a, b, c)):
        out[rows * n : rows * (n + 1), :] = ref[...]


def rows_of(j, size):
    return pl.ds(pl.multiple_of(j * size, size & -size), size)


def run_copies(copies, sem):
    handles = [pltpu.make_async_copy(a, b, sem.at[n]) for n, (a, b) in enumerate(copies)]
    for h in handles:
        h.start()
    return handles


def wait_all(handles):
    for h in handles:
        h.wait()


def norm_kernel(x, bg, xn_o):
    hat, _ = ln_parts(x[...].astype(F32))
    xn_o[...] = (hat * bg[...][None, :]).astype(BF)


def query_kernel(xn, qg, *rest):
    pieces, (k_o, wk_o, wq_o, q_o, zn_o, lat, sem) = rest[:N], rest[N:]
    me, _ = me_z()
    copies = []
    for piece, rel in zip(pieces, WIDE):
        j = owner(me, rel)
        copies.append((piece.at[pl.ds(0, 96), :], wk_o.at[rows_of(j, 96), :]))
        copies.append((piece.at[pl.ds(96, 160), :], wq_o.at[rows_of(j, 160), :]))
        for c in range(5):
            copies.append((piece.at[pl.ds(256 + 32 * c, 32), :], lat.at[rows_of(j, 32), pl.ds(256 * c, 256)]))
    wait_all(run_copies(copies, sem))
    zhat, _ = ln_parts(lat[...].astype(F32))
    zn_o[...] = (zhat * qg[...][None, :]).astype(BF)
    q_o[...] = dot(zn_o[...], wq_o[...], 1, 0).astype(BF)
    k_o[...] = dot(xn[...], wk_o[...], 1, 0).astype(BF)


def scores_kernel(prefix, k, q, e_o, ll_o):
    me, _ = me_z()
    lanes = lax.broadcasted_iota(jnp.int32, (256, 256), 1) // 32
    pos = lax.broadcasted_iota(jnp.int32, (256, 512), 1) + me * 512
    own = STRIDE * (lax.broadcasted_iota(jnp.int32, (256, 1), 0) + 1)
    lane = lax.broadcasted_iota(jnp.int32, (256, 128), 1)
    ll_o[...] = jnp.zeros_like(ll_o)
    for s in range(2):
        seen = jnp.maximum(own, prefix[s])

        def head(h, carry, s=s, seen=seen):
            qh = jnp.where(lanes == h, q[...], jnp.zeros((), BF))
            scores = dot(qh, k[512 * s : 512 * (s + 1), :], 1, 1)
            e = jnp.where(pos < seen, jnp.exp2(scores * (LOG2E * 32 ** (-0.5))), 0.0)
            ll_o[s] += jnp.where(lane == h, jnp.sum(e, axis=-1, keepdims=True), 0.0)
            e_o[s, h] = e.astype(BF)
            return carry

        lax.fori_loop(0, H, head, 0, unroll=2)


def values_kernel(xn, *rest):
    pieces, (vt_o, wv_o, sem) = rest[:N], rest[N:]
    me, _ = me_z()
    wait_all(
        run_copies(
            [
                (p.at[pl.ds(416 + 96 * c, 96), :], wv_o.at[rows_of(owner(me, rel), 96), pl.ds(256 * c, 256)])
                for p, rel in zip(pieces, WIDE)
                for c in range(5)
            ],
            sem,
        )
    )
    for c in range(5):
        cols = slice(256 * c, 256 * (c + 1))
        vt_o[cols, :] = dot(wv_o[:, cols], xn[...], 0, 1).astype(BF)


def sums_kernel(vt, e, ll, *rest):
    mine_o, theirs_o, aat, acc = rest[-4:]
    me, _ = me_z()

    def head(h, carry):
        rows = rows_of(h, 160)
        aat[rows, :] = dot(vt[rows, :], e[h], 1, 1).astype(BF)
        return carry

    lax.fori_loop(0, H, head, 0, unroll=2)
    acc[:, 0:1280] = aat[...].T
    acc[:, 1280:1408] = ll[...].astype(BF)
    for kk in range(4):
        for odd, ref in ((0, mine_o), (1, theirs_o)):
            ref[kk] = acc[rows_of(me ^ (2 * kk + odd), 32), :]


def add4_kernel(a, b, *outs):
    for kk in range(4):
        outs[kk][...] = a[kk] + b[kk]


def latent_kernel(m0, r1, r2, r3, lat, mg1, cot, *rest):
    pieces, rest = rest[:N], rest[N:]
    latents_o, agb_o, mine_o, theirs_o, dab_o, init_o = rest[:6]
    wout, wup, wdown, sem = rest[6:]
    me, zi = me_z()
    groups = []
    for g, w in enumerate((wout, wup, wdown)):
        copies = [
            (p.at[pl.ds(160 * g, 160), :], w.at[rows_of(owner(me, rel), 160), :]) for p, rel in zip(pieces, WIDE)
        ]
        groups.append(run_copies(copies, sem.at[g]))
    mg = mg1[...][None, :]
    total = (m0[...].astype(F32) + r1[...].astype(F32)) + (r2[...].astype(F32) + r3[...].astype(F32))
    aa = total[:, 0:1280]
    ll = total[:, 1280:1408]
    head = lax.broadcasted_iota(jnp.int32, (64, 1280), 1) // 160
    inv = jnp.zeros((64, 1280), F32)
    for h in range(H):
        inv = jnp.where(head == h, 1.0 / ll[:, h : h + 1], inv)
    oo = aa * inv
    ob = oo.astype(BF)
    for h in groups[0]:
        h.wait()
    start = lat[...].astype(F32)
    hh = jnp.concatenate([start, start], axis=0) + dot(ob, wout[...], 1, 0)
    hat, inverse = ln_parts(hh)
    hn = (hat * mg).astype(BF)
    for h in groups[1]:
        h.wait()
    uu = dot(hn, wup[...], 1, 0)
    cdf = 0.5 * (1.0 + lax.erf(uu * (0.5**0.5)))
    gg = (uu * cdf).astype(BF)
    slope = cdf + uu * (jnp.exp(-0.5 * uu * uu) * 0.3989422804014327)
    for h in groups[2]:
        h.wait()
    latents_o[...] = (hh + dot(gg, wdown[...], 1, 0)).astype(BF)
    du = (dot(cot[...], wdown[...], 1, 1) * slope).astype(BF)
    dhn = dot(du, wup[...], 1, 1)
    dhh = cot[...].astype(F32) + ln_back(dhn, hat, inverse, mg)
    init_o[...] = dhh[0:32] + dhh[32:64]
    dhb = dhh.astype(BF)
    dob = dot(dhb, wout[...], 1, 1).astype(BF).astype(F32)
    dab_o[:, 0:1280] = (dob * inv).astype(BF)
    prod = dob * oo
    lane = lax.broadcasted_iota(jnp.int32, (64, 128), 1)
    dlb = jnp.zeros((64, 128), F32)
    for h in range(H):
        part = jnp.sum(jnp.where(head == h, prod, 0.0), axis=-1, keepdims=True)
        dlb = jnp.where(lane == h, -part / ll[:, h : h + 1], dlb)
    dab_o[:, 1280:1408] = dlb.astype(BF)
    agb_o[0] = dhb
    agb_o[1] = du
    agb_o[2] = cot[...]
    for j in range(N):
        kk = (me >> 1) ^ (j >> 1)
        cols = slice(160 * j, 160 * (j + 1))

        @pl.when((me & 1) == (j & 1))
        def _():
            for n, v in enumerate((ob, hn, gg)):
                mine_o[kk, n] = v[:, cols]

        @pl.when((me & 1) != (j & 1))
        def _():
            for n, v in enumerate((ob, hn, gg)):
                theirs_o[kk, n] = v[:, cols]


def backward_kernel(s, k, vt, q, e, *rest):
    pieces = rest[:N]
    dkvt_o, dq_o, dabx, dabt, qt, sem = rest[-6:] if s else (*rest[N + 2 : N + 4], *rest[-4:])
    me, _ = me_z()
    handles = run_copies(
        [(p.at[pl.ds(32 * s, 32), :], dabx.at[rows_of(owner(me, rel), 32), :]) for p, rel in zip(pieces, DIRECT)], sem
    )
    if s == 0:
        for kk in range(1, 4):
            for n in range(2):
                rest[N + 3 + kk][n] = rest[N + n][kk]
    qt[...] = q[...].T
    dq_o[...] = jnp.zeros_like(dq_o)
    wait_all(handles)
    lanes = lax.broadcasted_iota(jnp.int32, (256, 256), 1) // 32
    lane = lax.broadcasted_iota(jnp.int32, (256, 128), 1)
    scale = 32 ** (-0.5)
    dabt[...] = dabx[:, 0:1280].T

    def head(h, carry):
        rows = rows_of(h, 160)
        dkvt_o[pl.ds(pl.multiple_of(256 + h * 160, 32), 160), :] = dot(dabt[rows, :], e[h], 1, 0).astype(BF)
        dlb = jnp.sum(jnp.where(lane == h, dabx[:, 1280:1408].astype(F32), 0.0), axis=-1, keepdims=True)
        dee = dot(dabt[rows, :], vt[rows, :], 0, 0) + dlb
        dss = (e[h].astype(F32) * dee).astype(BF)
        krows = rows_of(h, 32)
        dkvt_o[krows, :] = (dot(qt[krows, :], dss, 1, 0) * scale).astype(BF)
        dq_o[...] += jnp.where(lanes == h, dot(dss, k[...], 1, 0), 0.0)
        return carry

    lax.fori_loop(0, H, head, 0, unroll=2)
    dq_o[...] = dq_o[...] * scale


def weights_kernel(xn, zn, dkvt, dq0, dq1, mine_o, theirs_o, xnt, dw, dqg, dqs):
    me, _ = me_z()
    xnt[...] = xn[...].T
    dqs[...] = dq0[...] + dq1[...]
    for c in range(6):
        cols = slice(256 * c, 256 * (c + 1))
        dw[:, cols] = dot(xnt[...], dkvt[cols, :], 1, 1).astype(BF)
    dqg[...] = dot(zn[...], dqs[...].astype(BF), 0, 0).astype(BF)
    for kk in range(4):
        for odd, ref in ((0, mine_o), (1, theirs_o)):
            j = me ^ (2 * kk + odd)
            for c in range(6):
                ref[kk, 96 * c : 96 * (c + 1), :] = dw[rows_of(j, 96), 256 * c : 256 * (c + 1)]
            ref[kk, 576:736, :] = dqg[rows_of(j, 160), :]
            ref[kk, 736:768, :] = dqs[rows_of(j, 32), :].astype(BF)


def own_part(gain, me, size):
    out = gain[0:size][None, :]
    for j in range(1, N):
        out = jnp.where(me == j, gain[size * j : size * (j + 1)][None, :], out)
    return out


def sum_slots_kernel(a, b, c, d, wk, wv, wq, bg, qg, mix, *rest):
    near_o, far_o, send_o, norm_o, acc = rest
    me, zi = me_z()
    total = (a[...].astype(F32) + b[...].astype(F32)) + (c[...].astype(F32) + d[...].astype(F32))
    acc[...] = total.astype(BF)
    near_o[...] = acc[rows_of(zi, 192), :]
    far_o[...] = acc[rows_of(zi ^ 2, 192), :]
    send_o[0:192, :] = acc[rows_of(zi ^ 1, 192), :]
    send_o[192:384, :] = acc[rows_of(zi ^ 3, 192), :]
    prod = total[0:96] * wk[...].astype(F32)
    for n in range(5):
        prod += total[96 * (n + 1) : 96 * (n + 2)] * wv[:, 256 * n : 256 * (n + 1)].astype(F32)
    parts = (
        (row_sums(prod) / own_part(bg[...], me, 96), 96),
        (mix[...], 160),
        (row_sums(total[576:736] * wq[...].astype(F32)) / own_part(qg[...], me, 160), 160),
    )
    padded = [v if size == 160 else jnp.concatenate([v, jnp.zeros((8, 160 - size), F32)], axis=1) for v, size in parts]
    joined = jnp.concatenate(padded + [jnp.zeros((8, 32), F32)], axis=1)
    placed = jnp.where(lax.broadcasted_iota(jnp.int32, (8, 512), 0) == me, joined, 0.0)
    norm_o[...] = jnp.concatenate([placed[:, 0:256], placed[:, 256:512]], axis=0).astype(BF)


def bytes_kernel(x, bg, wk, wv, dkvt, *rest):
    out = rest[-1]
    hat, inverse = ln_parts(x[...].astype(F32))
    dxn = dot(dkvt[0:256, :], wk[...], 0, 1) + dot(dkvt[256:1536, :], wv[...], 0, 1)
    out[...] = ln_back(dxn, hat, inverse, bg[...][None, :])


def latent_grads_kernel(init, wup, mg, *rest):
    (amine, at, b1, b2, b3), rest = rest[N : N + 5], rest[:N] + rest[N + 5 :]
    rows, outs, mix_o, (xs, ys, acc, sem) = rest[:N], rest[N : N + 4], rest[N + 4], rest[N + 5 :]
    me, zi = me_z()
    copies = []
    cols = (amine.at[0], at.at[0], b1.at[0], b1.at[1], b2.at[0], b2.at[1], b3.at[0], b3.at[1])
    for k in range(N):
        copies.append((cols[k], xs.at[:, rows_of(me ^ k, 64), :]))
        copies.append((rows[k], ys.at[:, rows_of(owner(me, WIDE[k]), 64), :]))
    wait_all(run_copies(copies, sem))
    for n in range(3):
        grad = dot(xs[n], ys[n], 0, 0)
        acc[160 * n : 160 * (n + 1), :] = grad.astype(BF)
        if n == 1:
            mix_o[...] = row_sums(grad * wup[...].astype(F32)) / own_part(mg[...], me, 160)
    acc[480:512, :] = init[...].astype(BF)
    for r in range(NZ):
        outs[r][...] = acc[rows_of(zi ^ r, 128), :]


def row_sums(v):
    ones = jnp.ones((8, v.shape[1]), F32)
    return lax.dot_general(
        ones, v, (((1,), (1,)), ((), ())), precision=lax.Precision.HIGHEST, preferred_element_type=F32
    )


def finish_latent_kernel(*rest):
    pieces, (out_o, up_o, down_o, init_o, acc) = rest[:NZ], rest[NZ:]
    _, zi = me_z()
    for r in range(NZ):
        acc[rows_of(zi ^ r, 128), :] = pieces[r][...]
    out_o[...] = acc[0:160, :].astype(F32)
    up_o[...] = acc[160:320, :].astype(F32)
    down_o[...] = acc[320:480, :].astype(F32)
    init_o[...] = acc[480:512, :].astype(F32)


def finish_norms(both, outs):
    total = jnp.concatenate([both[0:8], both[8:16]], axis=1)
    for n, (out, size) in enumerate(zip(outs, (96, 160, 160))):
        width = out.shape[0]
        at = lax.broadcasted_iota(jnp.int32, (1, width), 1) % size
        pick = (at == lax.broadcasted_iota(jnp.int32, (160, width), 0)).astype(F32)
        wide = lax.dot_general(
            total[:, 160 * n : 160 * (n + 1)],
            pick,
            (((1,), (0,)), ((), ())),
            precision=lax.Precision.HIGHEST,
            preferred_element_type=F32,
        )
        mine = lax.broadcasted_iota(jnp.int32, (8, width), 0) == lax.broadcasted_iota(jnp.int32, (1, width), 1) // size
        out[...] = jnp.sum(jnp.where(mine, wide, 0.0), axis=0)


def plus(a, b):
    return a + b


def finish_kernel(wq_full, lat, qg, init, *rest):
    pieces, (key_o, value_o, query_o, init_o), outs, acc = rest[:NZ], rest[NZ : NZ + 4], rest[NZ + 4 : NZ + 7], rest[-1]
    _, zi = me_z()
    for r in range(NZ):
        acc[rows_of(zi ^ r, 192), :] = pieces[r][0:192, :]
    a, b, c, d = [p[192:208, :].astype(F32) for p in pieces]
    finish_norms((a + b) + (c + d), outs)
    key_o[...] = acc[0:96, :].astype(F32)
    for c in range(5):
        value_o[:, 256 * c : 256 * (c + 1)] = acc[96 * (c + 1) : 96 * (c + 2), :].astype(F32)
    query_o[...] = acc[576:736, :].astype(F32)
    dzn = dot(acc[736:768, :], wq_full[...], 1, 1)
    hat, inverse = ln_parts(lat[...].astype(F32))
    init_o[...] = init[...] + ln_back(dzn, hat, inverse, qg[...][None, :])


def sum_of_three_kernel(a, b, c, out):
    out[...] = (a[...].astype(F32) + b[...].astype(F32) + c[...].astype(F32)).astype(BF)


def first_zq_kernel(near, far, got, near_o, far_o):
    near_o[...] = plus(near[...], got[0:192, :])
    far_o[...] = plus(far[...], got[192:384, :])


def second_zq_kernel(near, got, a, b, out):
    out[0:192, :] = plus(near[...], got[...])
    out[192:208, :] = plus(a[...], b[...])


def sums_of_pairs_kernel(*refs):
    n = len(refs) // 3
    for k in range(n):
        a, b, out = refs[2 * k], refs[2 * k + 1], refs[2 * n + k]
        out[...] = plus(a[...], b[...])


def sums_of_pairs(pairs, name, deps=(), cost=COST):
    flat = [x for pair in pairs for x in pair]
    out = [sds(a.shape, a.dtype) for a, _ in pairs]
    return call(sums_of_pairs_kernel, out, flat, [VMEM] * len(flat), name=name, deps=deps, cost=cost)


def part(f, *args):
    def body(*refs):
        return f(*args, *refs)

    return body


def tie(*xs):
    return lax.optimization_barrier(xs)


def per_device_fast(
    byte_feats,
    latent_init,
    prefix,
    byte_gain,
    query_gain,
    mixer_gain,
    query_weight,
    key_weight,
    value_weight,
    out_weight,
    up_weight,
    down_weight,
    cotangent,
):
    seqs, rows, width = byte_feats.shape
    own = latent_init.shape[0]
    x = byte_feats.reshape(seqs * rows, width)
    cot = cotangent.reshape(seqs * own, DL)

    def first(w):
        return send_split(w, 2, 4), send_split(w, 4, 2)

    packed = call(
        pack_kernel, sds((896, 256), BF), (key_weight, query_weight, latent_init, value_weight), [VMEM] * 4, name="pack"
    )
    pa, pb = first(packed)
    wcat = call(
        pack_rows_kernel, sds((480, 1280), BF), (out_weight, up_weight, down_weight), [VMEM] * 3, name="pack_rows", deps=(packed,)
    )
    xn = call(norm_kernel, sds((1024, 768), BF), (x, byte_gain), [VMEM] * 2, name="norm", deps=(wcat,))
    pa, pb, xn, near, wcat = tie(pa, pb, xn, packed, wcat)
    wa = send_split(wcat, 2, 4)
    pd = send_split(pa, 4, 2)
    pn, pna, pnb = send(near, 1), send(pa, 1), send(pb, 1)
    pd, pn, wcat = tie(pd, pn, wcat)
    pnd = send(pd, 1)
    wb = send_split(wcat, 4, 2)
    pieces = (packed, pn, pa, pb, pd, pna, pnb, pnd)
    k, wk, wq_full, q, zn = call(
        query_kernel,
        (sds((1024, 256), BF), sds((768, 256), BF), sds((1280, 256), BF), sds((256, 256), BF), sds((256, 1280), BF)),
        (xn, query_gain, *pieces),
        [VMEM] * 2 + [ANY] * N,
        [pltpu.VMEM((256, 1280), BF), pltpu.SemaphoreType.DMA((7 * N,))],
        name="query",
    )
    q, wcat = tie(q, wcat)
    wn = send(wcat, 1)
    e, ll = call(
        scores_kernel,
        (sds((2, 8, 256, 512), BF), sds((2, 256, 128), F32)),
        (prefix, k, q),
        [SMEM, VMEM, VMEM],
        name="scores",
    )
    vt, wv = call(
        values_kernel,
        (sds((1280, 1024), BF), sds((768, 1280), BF)),
        (xn, *pieces),
        [VMEM] + [ANY] * N,
        [pltpu.SemaphoreType.DMA((5 * N,))],
        name="values",
        deps=(e, wn),
    )
    def sums(s, *prev):
        return call(
            sums_kernel,
            (sds((4, 64, 1408), BF), sds((4, 64, 1408), BF)),
            (vt, e, ll, *prev),
            [
                pl.BlockSpec((1280, 512), lambda g: (0, s)),
                pl.BlockSpec((None, 8, 256, 512), lambda g: (s, 0, 0, 0)),
                pl.BlockSpec((None, 256, 128), lambda g: (s, 0, 0)),
            ]
            + [ANY] * len(prev),
            [pltpu.VMEM((1280, 256), BF), pltpu.VMEM((256, 1408), BF)],
            out_specs=[pl.BlockSpec((4, 32, 1408), lambda g: (0, s, 0))] * 2,
            aliases={3: 0, 4: 1} if prev else {},
            name="sums",
            grid=(1,),
        )

    vt, wa, wb = tie(vt, wa, wb)
    mine, theirs = sums(0)
    wd = send_split(wa, 4, 2)
    wna, wnb = send(wa, 1), send(wb, 1)
    mine, theirs = sums(1, mine, theirs)
    got = send(theirs, 1)
    m0, m1, m2, m3 = call(
        add4_kernel, (sds((64, 1408), BF),) * 4, (mine, got), [VMEM] * 2, name="add4", deps=(wna, wnb), cost=1024
    )
    r1, r2, r3 = send(m1, 2), send(m2, 4), send(m3, 6)
    m0, wd = tie(m0, wd)
    wnd = send(wd, 1)
    latents, agb, amine, atheirs, dabx, init = call(
        latent_kernel,
        (
            sds((64, 1280), BF), sds((3, 64, 1280), BF), sds((4, 3, 64, 160), BF), sds((4, 3, 64, 160), BF),
            sds((64, 1408), BF), sds((32, 1280), F32),
        ),
        (m0, r1, r2, r3, latent_init, mixer_gain, cot, wcat, wn, wa, wb, wd, wna, wnb, wnd),
        [VMEM] * 7 + [ANY] * N,
        [pltpu.VMEM((1280, 1280), BF)] * 3 + [pltpu.SemaphoreType.DMA((3, N))],
        name="latent",
    )
    d2, d4, d6, d1 = send(dabx, 2), send(dabx, 4), send(dabx, 6), send(dabx, 1)
    at = send(atheirs, 1)
    d2, d4, d6, agb = tie(d2, d4, d6, agb)
    d3, d5, d7 = send(d2, 1), send(d4, 1), send(d6, 1)
    dab_p = [dabx, d1, d2, d3, d4, d5, d6, d7]
    ga, gb = first(agb)
    gn = send(agb, 1)

    def backward(s, *extra, deps=()):
        both = [sds((2, 3, 64, 160), BF)] * (0 if s else 3)
        return call(
            part(backward_kernel, s),
            (sds((1536, 1024), BF), sds((256, 256), F32), *both),
            (k, vt, q, e, *dab_p, *extra),
            [
                pl.BlockSpec((512, 256), lambda g: (s, 0)),
                pl.BlockSpec((1280, 512), lambda g: (0, s)),
                VMEM,
                pl.BlockSpec((None, 8, 256, 512), lambda g: (s, 0, 0, 0)),
            ]
            + [ANY] * N + [ANY if s else VMEM] * len(extra),
            [
                pltpu.VMEM((256, 1408), BF), pltpu.VMEM((1280, 256), BF), pltpu.VMEM((256, 256), BF),
                pltpu.SemaphoreType.DMA((N,)),
            ],
            out_specs=(pl.BlockSpec((1536, 512), lambda g: (0, s)), VMEM, *[VMEM] * len(both)),
            aliases={4 + N: 0} if s else {},
            name="backward",
            grid=(1,),
            deps=deps,
            cost=1024 if s else COST,
        )

    dkvt, dq0, *both = backward(0, amine, at)
    dq0, ga, gb, gn = tie(dq0, ga, gb, gn)
    gd = send_split(ga, 4, 2)
    gna = send(ga, 1)
    both_s = [send(b, 2 * kk + 2) for kk, b in enumerate(both)]
    dkvt, dq1 = backward(1, dkvt, deps=(dq0,))
    dq1, gd, gna, gb = tie(dq1, gd, gna, gb)
    gnb, gnd = send(gb, 1), send(gd, 1)
    gmine, gtheirs = call(
        weights_kernel,
        (sds((4, 768, 256), BF), sds((4, 768, 256), BF)),
        (xn, zn, dkvt, dq0, dq1),
        [VMEM] * 5,
        [
            pltpu.VMEM((768, 1024), BF), pltpu.VMEM((768, 1536), BF), pltpu.VMEM((1280, 256), BF),
            pltpu.VMEM((256, 256), F32),
        ],
        name="weights",
        deps=(),
    )
    gg = send(gtheirs, 1)

    *oud, mix = call(
        latent_grads_kernel,
        (sds((128, 1280), BF),) * NZ + (sds((8, 160), F32),),
        (init, up_weight, mixer_gain, agb, gn, ga, gb, gd, gna, gnb, gnd, amine, at, *both_s),
        [VMEM] * 3 + [ANY] * (5 + N),
        [
            pltpu.VMEM((3, 512, 160), BF), pltpu.VMEM((3, 512, 1280), BF), pltpu.VMEM((512, 1280), BF),
            pltpu.SemaphoreType.DMA((2 * N,)),
        ],
        name="latent_grads",
        deps=(gtheirs,),
    )
    o3 = send_z(oud[3], 1)
    gm = call(add4_kernel, (sds((768, 256), BF),) * 4, (gmine, gg), [VMEM] * 2, name="add4g", deps=(oud[0],))
    g1, g2, g3 = send(gm[1], 2), send(gm[2], 4), send(gm[3], 6)
    (ofar,) = sums_of_pairs(((oud[2], o3),), "osum", deps=(gm[0],))
    ofar, o1 = tie(ofar, oud[1])
    o22, o1 = send_z(ofar, 2), send_z(o1, 1)
    byte_grads = call(
        bytes_kernel,
        sds((2, 512, 768), F32),
        (x, byte_gain, wk, wv, dkvt),
        [
            pl.BlockSpec((256, 768), lambda b: (b, 0)),
            pl.BlockSpec((768,), lambda b: (0,)),
            pl.BlockSpec((768, 256), lambda b: (0, 0)),
            pl.BlockSpec((768, 1280), lambda b: (0, 0)),
            pl.BlockSpec((1536, 256), lambda b: (0, b)),
        ],
        out_specs=pl.BlockSpec((None, 256, 768), lambda b: (b // 2, b % 2, 0)),
        name="bytes",
        grid=(4,),
        deps=(ofar,),
        cost=1024,
    )
    qnear, qfar, qsend, norm = call(
        sum_slots_kernel,
        (sds((192, 256), BF), sds((192, 256), BF), sds((384, 256), BF), sds((16, 256), BF)),
        (gm[0], g1, g2, g3, key_weight, value_weight, query_weight, byte_gain, query_gain, mix),
        [VMEM] * 10,
        [pltpu.VMEM((768, 256), BF)],
        name="gsum",
        deps=(byte_grads,),
    )
    qgot = send_z(qsend, 1)
    ototal = call(
        sum_of_three_kernel, sds((128, 1280), BF), (oud[0], o1, o22), [VMEM] * 3, name="ototal", lead=(qnear,)
    )
    o2 = send_z(ototal, 2)
    qnear, qfar = call(
        first_zq_kernel,
        (sds((192, 256), BF), sds((192, 256), BF)),
        (qnear, qfar, qgot),
        [VMEM] * 3,
        name="qsum",
        deps=(ototal,),
    )
    qfar, norm, oshare = tie(qfar, norm, ototal)
    qgot, n3, o1 = send_z(qfar, 2), send(norm, 1), send_z(oshare, 1)
    (norm,) = sums_of_pairs(((norm, n3),), "nsum", cost=1024)
    n4 = send(norm, 2)
    (norm,) = sums_of_pairs(((norm, n4),), "nsum", cost=1024)
    norm, o2 = tie(norm, o2)
    n5, ofar2 = send(norm, 4), send_z(o2, 1)
    qtotal = call(
        second_zq_kernel,
        sds((208, 256), BF),
        (qnear, qgot, norm, n5),
        [VMEM] * 4,
        name="qtotal",
        deps=(o2, o1),
    )
    q2, q1 = send_z(qtotal, 2), send_z(qtotal, 1)
    out_g, up_g, down_g, init_sum = call(
        finish_latent_kernel,
        (sds((160, 1280), F32),) * 3 + (sds((32, 1280), F32),),
        (ototal, o1, o2, ofar2),
        [VMEM] * NZ,
        [pltpu.VMEM((512, 1280), BF)],
        name="finish_latent",
        cost=1024,
    )
    q3 = send_z(q2, 1)
    key_g, value_g, query_g, init_g, byte_n, mixer_n, query_n = call(
        finish_kernel,
        (
            sds((96, 256), F32), sds((96, 1280), F32), sds((160, 256), F32), sds((32, 1280), F32),
            sds((768,), F32), sds((1280,), F32), sds((1280,), F32),
        ),
        (wq_full, latent_init, query_gain, init_sum, qtotal, q1, q2, q3),
        [VMEM] * (4 + NZ),
        [pltpu.VMEM((768, 256), BF)],
        name="finish",
        cost=1024,
    )
    return (
        latents.reshape(seqs, own, DL),
        byte_grads,
        init_g,
        byte_n,
        query_n,
        mixer_n,
        query_g,
        key_g,
        value_g,
        out_g,
        up_g,
        down_g,
    )


def solution(mesh):
    fast = mesh.shape["fsdp"] == 8 and mesh.shape["rep"] == 4
    device_fn = per_device_fast if fast else per_device_plain
    placed = (
        P("rep", "fsdp", None),
        P("fsdp", None),
        P("rep"),
        P(),
        P(),
        P(),
        P("fsdp", None),
        P("fsdp", None),
        P("fsdp", None),
        P("fsdp", None),
        P("fsdp", None),
        P("fsdp", None),
        P("rep", "fsdp", None),
    )
    return jax.shard_map(
        device_fn,
        mesh=mesh,
        in_specs=placed,
        out_specs=(
            P("rep", "fsdp", None),
            P("rep", "fsdp", None),
            P("fsdp", None),
            P(),
            P(),
            P(),
            P("fsdp", None),
            P("fsdp", None),
            P("fsdp", None),
            P("fsdp", None),
            P("fsdp", None),
            P("fsdp", None),
        ),
        check_vma=False,
    )
```
